128 devices in a mesh: slab: 16 (over x, z), cross: 8 (over y, core).
Axes of the slice: x: 4, y: 4, z: 4, core: 2. Of those that a mesh axis runs over, the one named last changes fastest.
Arguments:
- load: float32 [3, 64, 256, 256], P(None, 'slab', 'cross'), may hold values from -6 to 6
- fixed_dofs: int32 [3, 64, 256, 256], P(None, 'slab', 'cross'), may hold values 0 or 1
- features: bfloat16 [16, 64, 256, 256], P(None, 'slab', 'cross'), may hold values from -1 to 1
- conv_weight: bfloat16 [27, 16], replicated, may hold values from -0.3125 to 0.3125
- active_bricks: int32 [16, 8, 256], P('slab', 'cross'), may hold values from -1 to 511, as said below
Outputs:
- displacement: float32 [3, 64, 256, 256], P(None, 'slab', 'cross')
- feature_grad: bfloat16 [16, 64, 256, 256], P(None, 'slab', 'cross')
- weight_grad: float32 [27, 16], replicated
The draws below stay inside these ranges and needn't reach their ends.
Inputs may be any that keep to these rules, and one draw needn't show every extreme that they name: `active_bricks`: row (i, j) lists distinct bricks of the block of device (slab i, cross j); a cell at local coordinates (x, y, z) lies in brick ((x // 4) * 8 + y // 4) * 64 + z // 4. Live entries come first and -1 fills the rest; each device has at least half of 256 live entries and one device has all 256 live.
All inputs are finite; a program needn't handle non-finite values. No bound on the sum of `fixed_dofs` on one device may be relied on, other than what follows from the above.
Results may differ from the reference program's by a relative error of at most 0.0065.
Values may be sent and summed in bfloat16 or wider, within the bound.
No kernel may reach another device: no remote copies, remote signals or barrier semaphores. Data moves between devices by JAX's collectives and lax.ppermute only.
A program may use at most 128 MiB of HBM per device.

```python
import math
import jax
import jax.numpy as jnp
import numpy as np
from jax import lax

C = 16
EX = 4
EY = 32
EZ = 256
ITERS = 3
BRICKS_DEV = 512
CAP = 256
NX = 64
NY = 256
NZ = 256
N_SLAB = 16
N_CROSS = 8


def draw_active_bricks(key, part):
    device_count = N_SLAB * N_CROSS
    count_key = jax.random.fold_in(key, 11)
    pick_key = jax.random.fold_in(key, 23)
    full_key = jax.random.fold_in(key, 37)
    counts = jax.random.randint(count_key, (device_count,), (CAP + 1) // 2, CAP + 1)
    fullest = jax.random.randint(full_key, (), 0, device_count)
    counts = jnp.where(jnp.arange(device_count) == fullest, CAP, counts)
    keys = jax.random.split(pick_key, device_count)
    orders = jax.vmap(lambda single: jax.random.permutation(single, BRICKS_DEV))(keys)[:, :CAP]
    slots = jnp.arange(CAP)[None, :]
    lists = jnp.where(slots < counts[:, None], orders, -1)
    return lists.reshape(N_SLAB, N_CROSS, CAP).astype(jnp.int32)


def touch_ends(array, stream_key, least, top_value):
    shape = array.shape
    place = [jax.random.randint(jax.random.fold_in(stream_key, axis), (), 0, shape[axis]) for axis in range(len(shape))]
    array = array.at[tuple(place)].set(least)
    longest = shape.index(max(shape))
    place[longest] = (place[longest] + 1) % shape[longest]
    return array.at[tuple(place)].set(top_value)


def shard_levels(rng, shape, cuts, smallest, top_value):
    def one(dim, blocks):
        draws = jax.random.uniform(jax.random.fold_in(jax.random.fold_in(rng, 6), dim), (blocks,), jnp.float32, smallest / len(cuts), top_value / len(cuts))
        return jnp.repeat(jnp.exp(draws), shape[dim] // blocks).reshape((-1,) + (1,) * (len(shape) - dim - 1))

    gain = one(*cuts[0])
    for cut in cuts[1:]:
        gain = gain * one(*cut)
    return gain


def noise(key, dims, scale, reach, cuts=(), held_as=jnp.bfloat16):
    level = shard_levels(key, dims, cuts, -0.22, 0.18) if cuts else 1.0
    result = jax.random.normal(key, dims, jnp.float32) * scale * level
    return jnp.minimum(jnp.maximum(result, -reach), reach).astype(held_as)


def setup_inputs(seed: int = 0) -> dict:
    streams_of = jax.random.split(jax.random.key(seed), 6)
    load = noise(streams_of[0], (3, NX, NY, NZ), 1.0, 6.0, ((1, 16), (2, 8)), jnp.float32)
    fixed_dofs = touch_ends((jax.random.randint(streams_of[1], (3, NX, NY, NZ), 0, 8) < 1).astype(jnp.int32), jax.random.fold_in(streams_of[1], 1), 0, 1)
    features = jnp.clip(jax.random.uniform(streams_of[2], (C, NX, NY, NZ), jnp.float32, -1.0, 1.0) * shard_levels(streams_of[2], (C, NX, NY, NZ), ((1, 16), (2, 8)), -0.4, 0.0), -1.0, 1.0).astype(jnp.bfloat16)
    conv_weight = noise(streams_of[3], (27, C), (27 * C) ** -0.5, 0.3125)
    active_bricks = draw_active_bricks(jax.random.fold_in(streams_of[5], 71), 0)
    return dict(load=load, fixed_dofs=fixed_dofs, features=features, conv_weight=conv_weight, active_bricks=active_bricks)


void_modulus = 0.001
spring = 0.1
corners = [(a, b, c) for a in (0, 1) for b in (0, 1) for c in (0, 1)]
offsets = [(a, b, c) for a in (-1, 0, 1) for b in (-1, 0, 1) for c in (-1, 0, 1)]

def brick_stiffness():
    poisson = 0.3
    lame_first = poisson / ((1.0 + poisson) * (1.0 - 2.0 * poisson))
    shear_modulus = 0.5 / (1.0 + poisson)
    elastic = np.zeros((6, 6))
    elastic[:3, :3] = lame_first
    for axis_number in range(3):
        elastic[axis_number, axis_number] += 2.0 * shear_modulus
        elastic[3 + axis_number, 3 + axis_number] = shear_modulus
    points = [0.5 - 0.5 / math.sqrt(3.0), 0.5 + 0.5 / math.sqrt(3.0)]
    matrix = np.zeros((24, 24))
    for gauss_x in points:
        for gauss_y in points:
            for gauss_z in points:
                strain = np.zeros((6, 24))
                for q, (a, b, c) in enumerate(corners):
                    shape_x = gauss_x if a else 1.0 - gauss_x
                    shape_y = gauss_y if b else 1.0 - gauss_y
                    shape_z = gauss_z if c else 1.0 - gauss_z
                    slope_x = (1.0 if a else -1.0) * shape_y * shape_z
                    slope_y = shape_x * (1.0 if b else -1.0) * shape_z
                    slope_z = shape_x * shape_y * (1.0 if c else -1.0)
                    column = 3 * q
                    strain[0, column] = slope_x
                    strain[1, column + 1] = slope_y
                    strain[2, column + 2] = slope_z
                    strain[3, column] = slope_y
                    strain[3, column + 1] = slope_x
                    strain[4, column + 1] = slope_z
                    strain[4, column + 2] = slope_y
                    strain[5, column] = slope_z
                    strain[5, column + 2] = slope_x
                matrix += strain.T @ elastic @ strain / 8.0
    return matrix.astype(np.float32)

def corner_stack(extended, depth, height, width):
    pieces = [extended[:, a:a + depth, b:b + height, c:c + width] for a, b, c in corners]
    return jnp.stack(pieces).reshape(24, depth * height * width)

def spread(product, depth, height, width):
    total = jnp.zeros((3, depth + 1, height + 1, width + 1), jnp.float32)
    for q, (a, b, c) in enumerate(corners):
        total = total + jnp.pad(product[q], ((0, 0), (a, 1 - a), (b, 1 - b), (c, 1 - c)))
    return total

def live_cells(active_bricks):
    count_slab, count_cross, slots = active_bricks.shape
    safe = jnp.where(active_bricks < 0, BRICKS_DEV, active_bricks).astype(jnp.int32)
    slab_index = jnp.broadcast_to(jnp.arange(count_slab, dtype=jnp.int32)[:, None, None], safe.shape)
    cross_index = jnp.broadcast_to(jnp.arange(count_cross, dtype=jnp.int32)[None, :, None], safe.shape)
    table = jnp.zeros((count_slab, count_cross, BRICKS_DEV + 1), jnp.float32)
    table = table.at[slab_index, cross_index, safe].set(1.0)[:, :, :BRICKS_DEV]
    table = table.reshape(count_slab, count_cross, EX // 4, EY // 4, EZ // 4).transpose(0, 2, 1, 3, 4)
    table = table.reshape(NX // 4, NY // 4, NZ // 4)
    cells = jnp.repeat(jnp.repeat(jnp.repeat(table, 4, axis=0), 4, axis=1), 4, axis=2)
    inside_x = (jnp.arange(NX) < NX - 1)[:, None, None]
    inside_y = (jnp.arange(NY) < NY - 1)[None, :, None]
    inside_z = (jnp.arange(NZ) < NZ - 1)[None, None, :]
    return cells * (inside_x & inside_y & inside_z).astype(jnp.float32)

def conv_forward(features, conv_weight):
    padded = jnp.pad(features, ((0, 0), (1, 1), (1, 1), (1, 1)))
    weight = conv_weight.astype(jnp.float32)

    def block(index):
        piece = lax.dynamic_slice_in_dim(padded, index * EX, EX + 2, 1).astype(jnp.float32)
        taps = jnp.einsum('tc,cxyz->txyz', weight, piece)
        total = jnp.zeros((EX, NY, NZ), jnp.float32)
        for t, (ox, oy, oz) in enumerate(offsets):
            total = total + taps[t, 1 + ox:1 + ox + EX, 1 + oy:1 + oy + NY, 1 + oz:1 + oz + NZ]
        return total
    blocks = lax.map(block, jnp.arange(N_SLAB, dtype=jnp.int32))
    return blocks.reshape(NX, NY, NZ)

def conv_backward(logit_grad, features, conv_weight):
    padded = jnp.pad(logit_grad, 1)
    weight = conv_weight.astype(jnp.float32)

    def block(index):
        piece = lax.dynamic_slice_in_dim(padded, index * EX, EX + 2, 0).astype(jnp.float32)
        shifted = jnp.stack([piece[1 - ox:1 - ox + EX, 1 - oy:1 - oy + NY, 1 - oz:1 - oz + NZ] for ox, oy, oz in offsets])
        own = lax.dynamic_slice_in_dim(features, index * EX, EX, 1).astype(jnp.float32)
        grad_block = jnp.einsum('tc,txyz->cxyz', weight, shifted).astype(jnp.bfloat16)
        weight_block = jnp.einsum('txyz,cxyz->tc', shifted, own)
        return (grad_block, weight_block)
    grads, weights = lax.map(block, jnp.arange(N_SLAB, dtype=jnp.int32))
    feature_grad = grads.transpose(1, 0, 2, 3, 4).reshape(C, NX, NY, NZ)
    return (feature_grad, lax.optimization_barrier(jnp.sum(weights, axis=0)))

def block_map(field, fn):
    padded = jnp.pad(field, ((0, 0), (0, 1), (0, 1), (0, 1)))

    def block(index):
        piece = lax.dynamic_slice_in_dim(padded, index * EX, EX + 1, 1)
        return fn(index, corner_stack(piece, EX, NY, NZ))
    return lax.map(block, jnp.arange(N_SLAB, dtype=jnp.int32))

def assemble(masked, stiffness, stiff):

    def forces(index, stacked):
        factor = lax.dynamic_slice_in_dim(stiffness, index * EX, EX, 0).reshape(1, -1)
        product = jnp.dot(stiff, stacked, precision=lax.Precision.HIGHEST, preferred_element_type=jnp.float32) * factor
        return spread(product.reshape(8, 3, EX, NY, NZ), EX, NY, NZ)
    parts = block_map(masked, forces)
    main = parts[:, :, :EX]
    rim = parts[:, :, EX]
    main = main.at[1:, :, 0].add(rim[:-1])
    return main.transpose(1, 0, 2, 3, 4).reshape(3, NX, NY + 1, NZ + 1)[:, :, :NY, :NZ]

def cell_energy(masked, stiff):

    def energy(index, stacked):
        image = jnp.dot(stiff, stacked, precision=lax.Precision.HIGHEST, preferred_element_type=jnp.float32)
        return lax.optimization_barrier(jnp.sum(stacked * image, axis=0)).reshape(EX, NY, NZ)
    return block_map(masked, energy).reshape(NX, NY, NZ)

def reference(load, fixed_dofs, features, conv_weight, active_bricks):
    stiff = jnp.asarray(brick_stiffness())
    free = (1 - fixed_dofs).astype(jnp.float32)
    live = live_cells(active_bricks)
    logit = conv_forward(features, conv_weight)
    density = 1.0 / (1.0 + jnp.exp(-logit))
    stiffness = live * (void_modulus + density ** 3 * (1.0 - void_modulus))

    def apply(field):
        masked = free * field
        return free * assemble(masked, stiffness, stiff) + spring * masked + (1.0 - free) * field
    displacement = jnp.zeros_like(load)
    residual = free * load
    direction = residual
    norm_now = jnp.sum(residual * residual)
    for step in range(ITERS):
        image = apply(direction)
        alpha = norm_now / jnp.sum(direction * image)
        displacement = displacement + alpha * direction
        residual = residual - alpha * image
        norm_next = jnp.sum(residual * residual)
        direction = residual + norm_next / norm_now * direction
        norm_now = norm_next
    energy = cell_energy(free * displacement, stiff)
    logit_grad = (-3.0 * (1.0 - void_modulus) * live * density ** 3 * (1.0 - density) * energy).astype(jnp.bfloat16)
    feature_grad, weight_part = conv_backward(logit_grad, features, conv_weight)
    weight_grad = weight_part / math.sqrt(NX * NY * NZ)
    return (displacement, feature_grad, weight_grad)
```

```python
import math

import jax
import jax.numpy as jnp
from jax import lax
from jax.experimental import pallas as pl
from jax.experimental.pallas import tpu as pltpu
from jax.sharding import PartitionSpec as P

INTERPRET = False

void_modulus = 0.001
spring = 0.1
shift = 0.4
held = 64.0
dead = -1e30
poisson = 0.3
lame = poisson / ((1.0 + poisson) * (1.0 - 2.0 * poisson))
shear = 0.5 / (1.0 + poisson)

D, H, Z, C = 4, 32, 256, 16
R = 40
TILES = R // 8
KT = C * H
NT = 9 * R

f32 = jnp.float32
bf16 = jnp.bfloat16


def iota(shape, dim):
    return lax.broadcasted_iota(jnp.int32, shape, dim)


def call(kernel, out_shape, scratch=(), n_in=0):
    single = not isinstance(out_shape, (list, tuple))
    n_out = 1 if single else len(out_shape)
    vmem = pl.BlockSpec(memory_space=pltpu.VMEM)
    return pl.pallas_call(
        kernel,
        out_shape=out_shape,
        in_specs=[vmem] * n_in,
        out_specs=vmem if single else [vmem] * n_out,
        scratch_shapes=list(scratch),
        compiler_params=pltpu.CompilerParams(vmem_limit_bytes=56 * 1024 * 1024),
        interpret=INTERPRET,
    )


def shape_of(*dims, dtype=f32):
    return jax.ShapeDtypeStruct(dims, dtype)


def toeplitz(w_ref, t_ref):
    spread = (iota((C, KT), 1) // H == iota((C, KT), 0)).astype(bf16)
    wide = jnp.dot(w_ref[...], spread, preferred_element_type=f32)
    away = iota((R, KT), 1) % H - (iota((R, KT), 0) - 4)
    for ox in range(3):
        for oz in range(3):
            block = jnp.zeros((R, KT), f32)
            for oy in range(3):
                t = 9 * ox + 3 * oy + oz
                block = jnp.where(away == oy - 1, wide[t : t + 1, :], block)
            t_ref[(3 * ox + oz) * R : (3 * ox + oz + 1) * R, :] = block


def conv_kernel(ids_ref, where_ref, w_ref, f_ref, l_ref, up_ref, down_ref, tout_ref, t_ref, acc_ref):
    toeplitz(w_ref, t_ref)
    table = t_ref[...].astype(bf16)
    tout_ref[...] = table
    acc_ref[...] = jnp.zeros_like(acc_ref)
    for xin in range(D):
        product = jnp.dot(table, f_ref[:, xin].reshape(KT, Z), preferred_element_type=f32)
        for ox in range(3):
            for oz in range(3):
                q = 3 * ox + oz
                acc_ref[oz, xin - (ox - 1) + 1] += product[q * R : (q + 1) * R, :]
    ids = jnp.broadcast_to(ids_ref[...], (R, 256))
    row = iota((R, 256), 0) - 4
    own = (row >= 0) & (row < H)
    pick_y = ((ids >> 6) == (row >> 2)) & own
    ids = jnp.broadcast_to(ids_ref[...], (Z, 256))
    pick_z = (ids >= 0) & ((ids & 63) == (iota((Z, 256), 0) >> 2))
    live = lax.dot_general(
        pick_y.astype(f32).astype(bf16),
        pick_z.astype(f32).astype(bf16),
        (((1,), (1,)), ((), ())),
        preferred_element_type=f32,
    )
    lane = iota((R, Z), 1)
    row = iota((R, Z), 0) - 4
    last_y = jnp.where(where_ref[0:1, 1:2] == 1, H - 1, H)
    killed = own & ((live < 0.5) | (lane == Z - 1) | (row >= last_y))
    for x in range(D + 2):
        behind = jnp.where(lane > 0, pltpu.roll(acc_ref[0, x], 1, 1), 0.0)
        ahead = jnp.where(lane < Z - 1, pltpu.roll(acc_ref[2, x], Z - 1, 1), 0.0)
        logit = acc_ref[1, x] + behind + ahead
        if 1 <= x <= D:
            gone = killed
            if x == D:
                gone = gone | (own & (where_ref[0:1, 0:1] == 1))
            logit = jnp.where(gone, dead, logit)
        l_ref[x] = logit
        if x >= 2:
            up_ref[x - 2] = logit
        if x < 4:
            down_ref[x] = logit


def pack_kernel(qlo_ref, q_ref, qhi_ref, l_ref, llo_ref, lhi_ref, lx_ref, up_ref, down_ref):
    for k in range(3):
        for x in range(11):
            source = (qlo_ref, q_ref, qhi_ref)[(x + 1) // 4]
            up_ref[11 * k + x] = source[k, (x + 1) % 4, H - 4 : H, :]
            down_ref[11 * k + x] = source[k, (x + 1) % 4, 0:4, :]
    for x in range(10):
        terms = []
        if x <= 3:
            terms.append(llo_ref[x])
        if 2 <= x <= 7:
            terms.append(l_ref[x - 2])
        if x >= 6:
            terms.append(lhi_ref[x - 6])
        total = terms[0]
        for term in terms[1:]:
            total = total + term
        lx_ref[x] = total
        up_ref[33 + x] = total[33:37, :]
        down_ref[33 + x] = total[3:7, :]


def stage_a(v_ref, base, yz_ref, first, last):
    def plane(x, carry):
        for k in range(3):
            v = v_ref[k, x - base]
            z = pltpu.roll(v, Z - 1, 1)
            s = v + z
            d = z - v
            sy = pltpu.roll(s, R - 1, 0)
            dy = pltpu.roll(d, R - 1, 0)
            yz_ref[4 * k, x] = s + sy
            yz_ref[4 * k + 1, x] = sy - s
            yz_ref[4 * k + 2, x] = d + dy
            yz_ref[4 * k + 3, x] = dy - d
        return carry

    lax.fori_loop(first, last + 1, plane, 0)


def along_x(low, high):
    a = {}
    for k in range(3):
        for f in range(4):
            v0, v1 = low[4 * k + f], high[4 * k + f]
            if f:
                a[0, f, k] = v0 + v1
            a[1, f, k] = v1 - v0
    return a


def hooke(a, s):
    def scaled(value):
        return value if s is None else s * value

    lam, two_mu, mu = scaled(lame / 16), scaled(shear / 8), scaled(shear / 16)
    lam3, mu3, last = scaled(lame / 48), scaled(shear / 48), scaled((lame + 4 * shear) / 144)
    x, y, z = 0, 1, 2
    out = {}
    n = ((1, 0, x), (0, 1, y), (0, 2, z))
    trace = lam * (a[n[0]] + a[n[1]] + a[n[2]])
    for m in n:
        out[m] = trace + two_mu * a[m]
    for m, o in (((0, 1, x), (1, 0, y)), ((0, 2, x), (1, 0, z)), ((0, 2, y), (0, 1, z))):
        out[m] = out[o] = mu * (a[m] + a[o])
    for m, o in (((1, 1, x), (0, 3, z)), ((1, 1, y), (1, 2, z)), ((1, 2, x), (0, 3, y))):
        both = lam3 * (a[m] + a[o])
        out[m] = both + mu * a[m]
        out[o] = both + mu * a[o]
    m = ((0, 3, x), (1, 2, y), (1, 1, z))
    three = a[m[0]] + a[m[1]] + a[m[2]]
    for o in m:
        out[o] = mu3 * (three + a[o])
    for k in range(3):
        out[1, 3, k] = last * a[1, 3, k]
    return out


def tiles(body):
    def step(j, carry):
        rows = pl.ds(pl.multiple_of(8 * j, 8), 8)
        for half in range(2):
            body(rows, pl.ds(128 * half, 128))
        return carry

    lax.fori_loop(0, TILES, step, 0)


def stage_b(yz_ref, s_ref, g_ref, first, last):
    def tile(rows, lanes):
        low = [yz_ref[i, first, rows, lanes] for i in range(12)]
        carried = None
        for x in range(first, last + 1):
            high = [yz_ref[i, x + 1, rows, lanes] for i in range(12)]
            force = hooke(along_x(low, high), s_ref[x, rows, lanes])
            kept = []
            for k in range(3):
                for f in range(4):
                    diff = force[1, f, k]
                    if f:
                        near, far = force[0, f, k] - diff, force[0, f, k] + diff
                    else:
                        near, far = -diff, diff
                    if carried is not None:
                        g_ref[4 * k + f, x, rows, lanes] = near + carried[4 * k + f]
                    kept.append(far)
            carried = kept
            low = high

    tiles(tile)


def stage_c(g_ref, v_ref, m_ref, out_ref, base, first, last):
    def plane(x, carry):
        for k in range(3):
            g = [g_ref[4 * k + f, x] for f in range(4)]
            s = (g[0] - g[1]) + pltpu.roll(g[0] + g[1], 1, 0)
            d = (g[2] - g[3]) + pltpu.roll(g[2] + g[3], 1, 0)
            out = (s - d) + pltpu.roll(s + d, 1, 1)
            out_ref[k, x - base] = m_ref[k, x] * out + (spring - shift) * v_ref[k, x]
        return carry

    lax.fori_loop(first, last + 1, plane, 0)


def energy_of(a):
    force = hooke(a, None)
    total = None
    for key in a:
        term = a[key] * force[key]
        total = term if total is None else total + term
    return total


def krylov_kernel(
    qlo_ref, q_ref, qhi_ref, lx_ref, ylo_ref, yhi_ref, where_ref,
    p0_ref, p1_ref, p2_ref, gain_ref, dots_ref,
    v0_ref, v1_ref, v2_ref, m_ref, s_ref, yz_ref, g_ref, acc_ref,
):
    for k in range(3):
        for x in range(11):
            source = (qlo_ref, q_ref, qhi_ref)[(x + 1) // 4]
            v1_ref[k, x, 0:4, :] = ylo_ref[11 * k + x]
            v1_ref[k, x, 4 : 4 + H, :] = source[k, (x + 1) % 4]
            v1_ref[k, x, 4 + H :, :] = yhi_ref[11 * k + x]

    def split(x, carry):
        for k in range(3):
            v = v1_ref[k, x]
            fixed = v > 0.5 * held
            v0_ref[k, x] = jnp.where(fixed, 0.0, v)
            m_ref[k, x] = jnp.where(fixed, 0.0, 1.0)
        return carry

    lax.fori_loop(0, 11, split, 0)

    v2_ref[0, 0] = jnp.zeros((R, Z), f32)
    row = iota((R, Z), 0) - 4
    low_x, high_x = where_ref[0:1, 2:3] == 1, where_ref[0:1, 0:1] == 1
    low_y, high_y = where_ref[0:1, 3:4] == 1, where_ref[0:1, 1:2] == 1
    outside_y = (low_y & (row < 0)) | (high_y & (row >= H))
    for x in range(10):
        v2_ref[0, 0, 1:5, :] = ylo_ref[33 + x]
        v2_ref[0, 0, 35:39, :] = yhi_ref[33 + x]
        logit = lx_ref[x] + v2_ref[0, 0]
        gone = (logit < 0.1 * dead) | outside_y
        if x < 3:
            gone = gone | low_x
        if x > 6:
            gone = gone | high_x
        density = 1.0 / (1.0 + jnp.exp(-logit))
        cube = density * density * density
        s_ref[x] = jnp.where(gone, 0.0, void_modulus + cube * (1.0 - void_modulus))
        if 2 <= x <= 7:
            factor = (-3.0 * (1.0 - void_modulus)) * cube * (1.0 - density)
            gain_ref[x - 2] = jnp.where(gone, 0.0, factor)

    stage_a(v0_ref, 0, yz_ref, 0, 10)
    stage_b(yz_ref, s_ref, g_ref, 0, 9)
    stage_c(g_ref, v0_ref, m_ref, v1_ref, 0, 1, 9)
    stage_a(v1_ref, 0, yz_ref, 1, 9)
    stage_b(yz_ref, s_ref, g_ref, 1, 8)
    stage_c(g_ref, v1_ref, m_ref, v2_ref, 0, 2, 8)
    stage_a(v2_ref, 0, yz_ref, 3, 7)

    acc_ref[...] = jnp.zeros_like(acc_ref)

    def sums(rows, lanes):
        row = iota((8, 128), 0) + rows.start
        own = (row >= 4) & (row < 4 + H)
        total = [jnp.zeros((8, 128), f32) for _ in range(6)]
        for x in range(3, 7):
            for k in range(3):
                v0 = v0_ref[k, x, rows, lanes]
                v1 = v1_ref[k, x, rows, lanes]
                v2 = v2_ref[k, x, rows, lanes]
                pairs = ((v0, v0), (v0, v1), (v1, v1), (v1, v2), (v2, v2))
                for i, (left, right) in enumerate(pairs):
                    total[i] = total[i] + left * right
        low = [yz_ref[i, 3, rows, lanes] for i in range(12)]
        for x in range(3, 7):
            high = [yz_ref[i, x + 1, rows, lanes] for i in range(12)]
            total[5] = total[5] + s_ref[x, rows, lanes] * energy_of(along_x(low, high))
            low = high
        total[5] = total[5] + spring * total[4]
        for i in range(6):
            acc_ref[i] += jnp.where(own, total[i], 0.0)

    tiles(sums)
    for i in range(6):
        dots_ref[i : i + 1, :] = jnp.sum(acc_ref[i], axis=0, keepdims=True)
    dots_ref[6:8, :] = jnp.zeros((2, 128), f32)
    for k in range(3):
        for x in range(7):
            p0_ref[k, x] = v0_ref[k, x + 2]
            p1_ref[k, x] = v1_ref[k, x + 2]
            p2_ref[k, x] = v2_ref[k, x + 2]


def coefficients(dots_ref):
    total = [jnp.sum(dots_ref[i : i + 1, :], axis=1, keepdims=True) for i in range(6)]
    d00, d01, d11, d12, d22, g22 = total
    d02 = d11
    g00 = d01 + shift * d00
    g01 = d02 + shift * d01
    g02 = d12 + shift * d02
    g11 = d12 + shift * d11
    g12 = d22 + shift * d12
    tiny = 4e-6

    def inverse(pivot, scale):
        fine = pivot > tiny * scale
        return jnp.where(fine, 1.0 / jnp.where(fine, pivot, 1.0), 0.0)

    i0 = 1.0 / g00
    l1, l2 = g01 * i0, g02 * i0
    i1 = inverse(g11 - l1 * g01, g11)
    m = g12 - l2 * g01
    l3 = m * i1
    i2 = inverse(g22 - l2 * g02 - l3 * m, g22)
    b0 = d00
    b1 = d01 - l1 * b0
    b2 = d02 - l2 * b0 - l3 * b1
    c2 = b2 * i2
    c1 = b1 * i1 - l3 * c2
    c0 = b0 * i0 - l1 * c1 - l2 * c2
    return c0, c1, c2


def adjoint_kernel(
    p0_ref, p1_ref, p2_ref, gain_ref, dots_ref, f_ref,
    disp_ref, shifted_ref, wpart_ref,
    u_ref, yz_ref, lg_ref, s32_ref,
):
    c0, c1, c2 = coefficients(dots_ref)

    def combine(x, carry):
        for k in range(3):
            u_ref[k, x] = c0 * p0_ref[k, x] + c1 * p1_ref[k, x] + c2 * p2_ref[k, x]
        return carry

    lax.fori_loop(0, 7, combine, 0)
    for k in range(3):
        for x in range(D):
            disp_ref[k, x] = u_ref[k, x + 1, 4 : 4 + H, :]
    stage_a(u_ref, 0, yz_ref, 0, 6)

    def tile(rows, lanes):
        low = [yz_ref[i, 0, rows, lanes] for i in range(12)]
        for x in range(6):
            high = [yz_ref[i, x + 1, rows, lanes] for i in range(12)]
            grad = gain_ref[x, rows, lanes] * energy_of(along_x(low, high))
            lg_ref[1, x, rows, lanes] = grad.astype(bf16).astype(f32)
            low = high

    tiles(tile)
    lane = iota((R, Z), 1)
    row = iota((R, Z), 0) - 4
    reach = (row >= -1) & (row <= H)
    for x in range(6):
        grad = jnp.where(reach, lg_ref[1, x], 0.0)
        lg_ref[1, x] = grad
        lg_ref[0, x] = jnp.where(lane < Z - 1, pltpu.roll(grad, Z - 1, 1), 0.0)
        lg_ref[2, x] = jnp.where(lane > 0, pltpu.roll(grad, 1, 1), 0.0)
    cross = jnp.zeros((NT, KT), f32)
    for x in range(D):
        for ox in range(3):
            for oz in range(3):
                q = 3 * ox + oz
                s32_ref[q * R : (q + 1) * R, :] = lg_ref[oz, x - (ox - 1) + 1]
        rows = s32_ref[...].astype(bf16)
        shifted_ref[x] = rows
        cross = cross + lax.dot_general(
            rows,
            f_ref[:, x].reshape(KT, Z),
            (((1,), (1,)), ((), ())),
            preferred_element_type=f32,
        )
    away = iota((R, KT), 1) % H - (iota((R, KT), 0) - 4)
    wide = [None] * 27
    for ox in range(3):
        for oz in range(3):
            q = 3 * ox + oz
            block = cross[q * R : (q + 1) * R, :]
            for oy in range(3):
                picked = jnp.where(away == oy - 1, block, 0.0)
                wide[9 * ox + 3 * oy + oz] = jnp.sum(picked, axis=0, keepdims=True)
    for t in range(27):
        s32_ref[t : t + 1, :] = wide[t][:, :Z]
        s32_ref[32 + t : 33 + t, :] = wide[t][:, Z:]
    s32_ref[27:32, :] = jnp.zeros((5, Z), f32)
    gather = (iota((Z, 128), 0) // H == iota((Z, 128), 1)).astype(f32)
    other = (iota((Z, 128), 0) // H + 8 == iota((Z, 128), 1)).astype(f32)
    wpart_ref[...] = jnp.dot(
        s32_ref[0:32, :], gather, precision=lax.Precision.HIGHEST, preferred_element_type=f32
    ) + jnp.dot(
        s32_ref[32:64, :], other, precision=lax.Precision.HIGHEST, preferred_element_type=f32
    )


def feature_kernel(table_ref, shifted_ref, out_ref):
    turned = table_ref[...].astype(f32).T.astype(bf16)
    for x in range(D):
        product = jnp.dot(turned, shifted_ref[x], preferred_element_type=f32)
        out_ref[:, x] = product.astype(bf16).reshape(C, H, Z)


def total_over(x, axis):
    size = lax.axis_size(axis)
    sent = jnp.broadcast_to(x[None], (size,) + x.shape)
    return jnp.sum(lax.all_to_all(sent, axis, 0, 0), axis=0)


def total_everywhere(x):
    return total_over(total_over(x, "cross"), "slab")


def on_device(load, fixed_dofs, features, conv_weight, active_bricks):
    slabs, crosses = lax.axis_size("slab"), lax.axis_size("cross")
    slab, cross = lax.axis_index("slab"), lax.axis_index("cross")

    def to_next(x, axis):
        return lax.ppermute(x, axis, [(i, i + 1) for i in range(lax.axis_size(axis) - 1)])

    def to_last(x, axis):
        return lax.ppermute(x, axis, [(i + 1, i) for i in range(lax.axis_size(axis) - 1)])

    lane = lax.broadcasted_iota(jnp.int32, (1, 128), 1)
    edges = (
        ((lane == 0) & (slab == slabs - 1))
        | ((lane == 1) & (cross == crosses - 1))
        | ((lane == 2) & (slab == 0))
        | ((lane == 3) & (cross == 0))
    ).astype(jnp.int32)

    q = jnp.where(fixed_dofs != 0, held, load)
    qlo = to_next(q, "slab")
    qhi = to_last(q, "slab")
    ids = active_bricks.reshape(1, 256)
    logit, lup, ldown, table = call(
        conv_kernel,
        [
            shape_of(D + 2, R, Z),
            shape_of(4, R, Z),
            shape_of(4, R, Z),
            shape_of(NT, KT, dtype=bf16),
        ],
        [pltpu.VMEM((NT, KT), f32), pltpu.VMEM((3, D + 2, R, Z), f32)],
        n_in=4,
    )(ids, edges, conv_weight, features)
    llo = to_next(lup, "slab")
    lhi = to_last(ldown, "slab")
    lx, yup, ydown = call(
        pack_kernel,
        [shape_of(10, R, Z), shape_of(43, 4, Z), shape_of(43, 4, Z)],
        n_in=6,
    )(qlo, q, qhi, logit, llo, lhi)
    ylo = to_next(yup, "cross")
    yhi = to_last(ydown, "cross")
    field = shape_of(3, 7, R, Z)
    whole = pltpu.VMEM((3, 11, R, Z), f32)
    p0, p1, p2, gain, dots = call(
        krylov_kernel,
        [field, field, field, shape_of(6, R, Z), shape_of(8, 128)],
        [
            whole,
            whole,
            whole,
            whole,
            pltpu.VMEM((10, R, Z), f32),
            pltpu.VMEM((12, 11, R, Z), f32),
            pltpu.VMEM((12, 11, R, Z), f32),
            pltpu.VMEM((6, 8, 128), f32),
        ],
        n_in=7,
    )(qlo, q, qhi, lx, ylo, yhi, edges)
    dots = total_everywhere(dots)
    displacement, shifted, wpart = call(
        adjoint_kernel,
        [shape_of(3, D, H, Z), shape_of(D, NT, Z, dtype=bf16), shape_of(32, 128)],
        [
            pltpu.VMEM((3, 7, R, Z), f32),
            pltpu.VMEM((12, 7, R, Z), f32),
            pltpu.VMEM((3, 6, R, Z), f32),
            pltpu.VMEM((NT, Z), f32),
        ],
        n_in=6,
    )(p0, p1, p2, gain, dots, features)
    packed = jnp.pad(wpart[:27, :C].reshape(432), (0, 80)).reshape(4, 128)
    weight_total = total_everywhere(packed).reshape(512)[:432].reshape(27, C)
    feature_grad = call(feature_kernel, shape_of(C, D, H, Z, dtype=bf16), n_in=2)(table, shifted)
    scale = math.sqrt(D * slabs * H * crosses * Z)
    return displacement, feature_grad, weight_total / scale


def solution(mesh):
    in_specs = (
        P(None, "slab", "cross", None),
        P(None, "slab", "cross", None),
        P(None, "slab", "cross", None),
        P(),
        P("slab", "cross", None),
    )
    out_specs = (P(None, "slab", "cross", None), P(None, "slab", "cross", None), P())
    return jax.shard_map(
        on_device, mesh=mesh, in_specs=in_specs, out_specs=out_specs, check_vma=False
    )
```

```python
import math

import jax
import jax.numpy as jnp
from jax import lax
from jax.experimental import pallas as pl
from jax.experimental.pallas import tpu as pltpu
from jax.sharding import PartitionSpec as P

INTERPRET = False

void_modulus = 0.001
spring = 0.1
shift = 0.4
held = 64.0
dead = -1e30
poisson = 0.3
lame = poisson / ((1.0 + poisson) * (1.0 - 2.0 * poisson))
shear = 0.5 / (1.0 + poisson)

D, H, Z, C = 4, 32, 256, 16
R = 40
TILES = R // 8
KT = C * H
NT = 9 * R

f32 = jnp.float32
bf16 = jnp.bfloat16


def iota(shape, dim):
    return lax.broadcasted_iota(jnp.int32, shape, dim)


def call(kernel, out_shape, scratch=(), n_in=0):
    single = not isinstance(out_shape, (list, tuple))
    n_out = 1 if single else len(out_shape)
    vmem = pl.BlockSpec(memory_space=pltpu.VMEM)
    return pl.pallas_call(
        kernel,
        out_shape=out_shape,
        in_specs=[vmem] * n_in,
        out_specs=vmem if single else [vmem] * n_out,
        scratch_shapes=list(scratch),
        compiler_params=pltpu.CompilerParams(vmem_limit_bytes=56 * 1024 * 1024),
        interpret=INTERPRET,
    )


def shape_of(*dims, dtype=f32):
    return jax.ShapeDtypeStruct(dims, dtype)


def toeplitz(w_ref, t_ref):
    spread = (iota((C, KT), 1) // H == iota((C, KT), 0)).astype(bf16)
    wide = lax.dot_general(
        w_ref[...], spread, (((0,), (0,)), ((), ())), preferred_element_type=f32
    )
    away = iota((R, KT), 1) % H - (iota((R, KT), 0) - 4)
    for ox in range(3):
        for oz in range(3):
            block = jnp.zeros((R, KT), f32)
            for oy in range(3):
                t = 9 * ox + 3 * oy + oz
                block = jnp.where(away == oy - 1, wide[t : t + 1, :], block)
            t_ref[(3 * ox + oz) * R : (3 * ox + oz + 1) * R, :] = block


def is_edge(axis, last):
    return lax.axis_index(axis) == (lax.axis_size(axis) - 1 if last else 0)


def conv_kernel(ids_ref, w_ref, f_ref, q_ref, l_ref, up_ref, down_ref, tout_ref, t_ref, acc_ref):
    for k in range(3):
        for x in range(D):
            up_ref[4 * k + x] = q_ref[k, x, H - 4 : H, :]
            down_ref[4 * k + x] = q_ref[k, x, 0:4, :]
    toeplitz(w_ref, t_ref)
    table = t_ref[...].astype(bf16)
    tout_ref[...] = table
    acc_ref[...] = jnp.zeros_like(acc_ref)
    for xin in range(D):
        product = jnp.dot(table, f_ref[:, xin].reshape(KT, Z), preferred_element_type=f32)
        for ox in range(3):
            for oz in range(3):
                q = 3 * ox + oz
                acc_ref[oz, xin - (ox - 1) + 1] += product[q * R : (q + 1) * R, :]
    ids = jnp.broadcast_to(ids_ref[...], (R, 256))
    row = iota((R, 256), 0) - 4
    own = (row >= 0) & (row < H)
    pick_y = ((ids >> 6) == (row >> 2)) & own
    ids = jnp.broadcast_to(ids_ref[...], (Z, 256))
    pick_z = (ids >= 0) & ((ids & 63) == (iota((Z, 256), 0) >> 2))
    live = lax.dot_general(
        pick_y.astype(f32).astype(bf16),
        pick_z.astype(f32).astype(bf16),
        (((1,), (1,)), ((), ())),
        preferred_element_type=f32,
    )
    lane = iota((R, Z), 1)
    row = iota((R, Z), 0) - 4
    last_y = jnp.where(is_edge("cross", True), H - 1, H)
    killed = own & ((live < 0.5) | (lane == Z - 1) | (row >= last_y))
    for x in range(D + 2):
        behind = jnp.where(lane > 0, pltpu.roll(acc_ref[0, x], 1, 1), 0.0)
        ahead = jnp.where(lane < Z - 1, pltpu.roll(acc_ref[2, x], Z - 1, 1), 0.0)
        logit = acc_ref[1, x] + behind + ahead
        if 1 <= x <= D:
            gone = killed
            if x == D:
                gone = gone | (own & is_edge("slab", True))
            logit = jnp.where(gone, dead, logit)
        l_ref[x] = logit
        up_ref[12 + x] = logit[33:37, :]
        down_ref[12 + x] = logit[3:7, :]


def pack_kernel(l_ref, ylo_ref, yhi_ref, l2_ref, up_ref, down_ref):
    l2_ref[...] = l_ref[...]
    for x in range(D + 2):
        l2_ref[x, 1:5, :] += ylo_ref[12 + x]
        l2_ref[x, 35:39, :] += yhi_ref[12 + x]
    for x in range(4):
        up_ref[R * x : R * x + R, :] = l2_ref[x + 2]
        down_ref[R * x : R * x + R, :] = l2_ref[x]
    for i in range(12):
        for ref in (up_ref, down_ref):
            ref[4 * R + 8 * i : 4 * R + 8 * i + 4, :] = ylo_ref[i]
            ref[4 * R + 8 * i + 4 : 4 * R + 8 * i + 8, :] = yhi_ref[i]


def stage_a(v_ref, base, yz_ref, first, last):
    def plane(x, carry):
        for k in range(3):
            v = v_ref[k, x - base]
            z = pltpu.roll(v, Z - 1, 1)
            s = v + z
            d = z - v
            sy = pltpu.roll(s, R - 1, 0)
            dy = pltpu.roll(d, R - 1, 0)
            yz_ref[4 * k, x] = s + sy
            yz_ref[4 * k + 1, x] = sy - s
            yz_ref[4 * k + 2, x] = d + dy
            yz_ref[4 * k + 3, x] = dy - d
        return carry

    lax.fori_loop(first, last + 1, plane, 0)


def along_x(low, high):
    a = {}
    for k in range(3):
        for f in range(4):
            v0, v1 = low[4 * k + f], high[4 * k + f]
            if f:
                a[0, f, k] = v0 + v1
            a[1, f, k] = v1 - v0
    return a


def hooke(a, s):
    def scaled(value):
        return value if s is None else s * value

    lam, two_mu, mu = scaled(lame / 16), scaled(shear / 8), scaled(shear / 16)
    lam3, mu3, last = scaled(lame / 48), scaled(shear / 48), scaled((lame + 4 * shear) / 144)
    x, y, z = 0, 1, 2
    out = {}
    n = ((1, 0, x), (0, 1, y), (0, 2, z))
    trace = lam * (a[n[0]] + a[n[1]] + a[n[2]])
    for m in n:
        out[m] = trace + two_mu * a[m]
    for m, o in (((0, 1, x), (1, 0, y)), ((0, 2, x), (1, 0, z)), ((0, 2, y), (0, 1, z))):
        out[m] = out[o] = mu * (a[m] + a[o])
    for m, o in (((1, 1, x), (0, 3, z)), ((1, 1, y), (1, 2, z)), ((1, 2, x), (0, 3, y))):
        both = lam3 * (a[m] + a[o])
        out[m] = both + mu * a[m]
        out[o] = both + mu * a[o]
    m = ((0, 3, x), (1, 2, y), (1, 1, z))
    three = a[m[0]] + a[m[1]] + a[m[2]]
    for o in m:
        out[o] = mu3 * (three + a[o])
    for k in range(3):
        out[1, 3, k] = last * a[1, 3, k]
    return out


def tiles(body):
    def step(j, carry):
        rows = pl.ds(pl.multiple_of(8 * j, 8), 8)
        for half in range(2):
            body(rows, pl.ds(128 * half, 128))
        return carry

    lax.fori_loop(0, TILES, step, 0)


def stage_b(yz_ref, s_ref, g_ref, first, last):
    def tile(rows, lanes):
        low = [yz_ref[i, first, rows, lanes] for i in range(12)]
        carried = None
        for x in range(first, last + 1):
            high = [yz_ref[i, x + 1, rows, lanes] for i in range(12)]
            force = hooke(along_x(low, high), s_ref[x, rows, lanes])
            kept = []
            for k in range(3):
                for f in range(4):
                    diff = force[1, f, k]
                    if f:
                        near, far = force[0, f, k] - diff, force[0, f, k] + diff
                    else:
                        near, far = -diff, diff
                    if carried is not None:
                        g_ref[4 * k + f, x, rows, lanes] = near + carried[4 * k + f]
                    kept.append(far)
            carried = kept
            low = high

    tiles(tile)


def stage_c(g_ref, v_ref, m_ref, out_ref, base, first, last):
    def plane(x, carry):
        for k in range(3):
            g = [g_ref[4 * k + f, x] for f in range(4)]
            s = (g[0] - g[1]) + pltpu.roll(g[0] + g[1], 1, 0)
            d = (g[2] - g[3]) + pltpu.roll(g[2] + g[3], 1, 0)
            out = (s - d) + pltpu.roll(s + d, 1, 1)
            out_ref[k, x - base] = m_ref[k, x] * out + (spring - shift) * v_ref[k, x]
        return carry

    lax.fori_loop(first, last + 1, plane, 0)


def energy_of(a):
    force = hooke(a, None)
    total = None
    for key in a:
        term = a[key] * force[key]
        total = term if total is None else total + term
    return total


def krylov_kernel(
    qlo_ref, q_ref, qhi_ref, l_ref, xlo_ref, xhi_ref, ylo_ref, yhi_ref,
    p0_ref, p1_ref, p2_ref, gain_ref, dots_ref,
    v0_ref, v1_ref, v2_ref, m_ref, s_ref, yz_ref, g_ref, acc_ref,
):
    for k in range(3):
        for x in range(11):
            part, at = (x + 1) // 4, (x + 1) % 4
            v1_ref[k, x, 4 : 4 + H, :] = (qlo_ref, q_ref, qhi_ref)[part][k, at]
            i = 4 * k + at
            if part == 1:
                v1_ref[k, x, 0:4, :] = ylo_ref[i]
                v1_ref[k, x, 4 + H :, :] = yhi_ref[i]
            else:
                ref = xhi_ref if part else xlo_ref
                v1_ref[k, x, 0:4, :] = ref[4 * R + 8 * i : 4 * R + 8 * i + 4, :]
                v1_ref[k, x, 4 + H :, :] = ref[4 * R + 8 * i + 4 : 4 * R + 8 * i + 8, :]

    def split(x, carry):
        for k in range(3):
            v = v1_ref[k, x]
            fixed = v > 0.5 * held
            v0_ref[k, x] = jnp.where(fixed, 0.0, v)
            m_ref[k, x] = jnp.where(fixed, 0.0, 1.0)
        return carry

    lax.fori_loop(0, 11, split, 0)

    row = iota((R, Z), 0) - 4
    first_y = jnp.where(is_edge("cross", False), 0, -4)
    last_y = jnp.where(is_edge("cross", True), H - 1, R)
    outside_y = (row < first_y) | (row > last_y)
    for x in range(10):
        logit = None
        if x <= 3:
            logit = xlo_ref[R * x : R * x + R, :]
        if 2 <= x <= 7:
            term = l_ref[x - 2]
            logit = term if logit is None else logit + term
        if x >= 6:
            term = xhi_ref[R * (x - 6) : R * (x - 6) + R, :]
            logit = term if logit is None else logit + term
        gone = (logit < 0.1 * dead) | outside_y
        if x < 3:
            gone = gone | is_edge("slab", False)
        if x > 6:
            gone = gone | is_edge("slab", True)
        density = 1.0 / (1.0 + jnp.exp(-logit))
        cube = density * density * density
        s_ref[x] = jnp.where(gone, 0.0, void_modulus + cube * (1.0 - void_modulus))
        if 2 <= x <= 7:
            factor = (-3.0 * (1.0 - void_modulus)) * cube * (1.0 - density)
            gain_ref[x - 2] = jnp.where(gone, 0.0, factor)

    stage_a(v0_ref, 0, yz_ref, 0, 10)
    stage_b(yz_ref, s_ref, g_ref, 0, 9)
    stage_c(g_ref, v0_ref, m_ref, v1_ref, 0, 1, 9)
    stage_a(v1_ref, 0, yz_ref, 1, 9)
    stage_b(yz_ref, s_ref, g_ref, 1, 8)
    stage_c(g_ref, v1_ref, m_ref, v2_ref, 0, 2, 8)
    stage_a(v2_ref, 0, yz_ref, 3, 7)

    acc_ref[...] = jnp.zeros_like(acc_ref)

    def sums(rows, lanes):
        row = iota((8, 128), 0) + rows.start
        own = (row >= 4) & (row < 4 + H)
        total = [jnp.zeros((8, 128), f32) for _ in range(6)]
        for x in range(3, 7):
            for k in range(3):
                v0 = v0_ref[k, x, rows, lanes]
                v1 = v1_ref[k, x, rows, lanes]
                v2 = v2_ref[k, x, rows, lanes]
                pairs = ((v0, v0), (v0, v1), (v1, v1), (v1, v2), (v2, v2))
                for i, (left, right) in enumerate(pairs):
                    total[i] = total[i] + left * right
        low = [yz_ref[i, 3, rows, lanes] for i in range(12)]
        for x in range(3, 7):
            high = [yz_ref[i, x + 1, rows, lanes] for i in range(12)]
            total[5] = total[5] + s_ref[x, rows, lanes] * energy_of(along_x(low, high))
            low = high
        total[5] = total[5] + spring * total[4]
        for i in range(6):
            acc_ref[i] += jnp.where(own, total[i], 0.0)

    tiles(sums)
    lane = iota((1, 128), 1)
    dots = jnp.zeros((1, 128), f32)
    for i in range(6):
        total = jnp.sum(jnp.sum(acc_ref[i], axis=0, keepdims=True), axis=1, keepdims=True)
        dots = jnp.where(lane == i, total, dots)
    dots_ref[...] = jnp.broadcast_to(dots[None], dots_ref.shape)
    for k in range(3):
        for x in range(7):
            p0_ref[k, x] = v0_ref[k, x + 2]
            p1_ref[k, x] = v1_ref[k, x + 2]
            p2_ref[k, x] = v2_ref[k, x + 2]


def coefficients(dots_ref):
    dots = jnp.sum(dots_ref[...], axis=0)
    total = [dots[:, i : i + 1] for i in range(6)]
    d00, d01, d11, d12, d22, g22 = total
    d02 = d11
    g00 = d01 + shift * d00
    g01 = d02 + shift * d01
    g02 = d12 + shift * d02
    g11 = d12 + shift * d11
    g12 = d22 + shift * d12
    tiny = 4e-6

    def inverse(pivot, scale):
        fine = pivot > tiny * scale
        return jnp.where(fine, 1.0 / jnp.where(fine, pivot, 1.0), 0.0)

    i0 = 1.0 / g00
    l1, l2 = g01 * i0, g02 * i0
    i1 = inverse(g11 - l1 * g01, g11)
    m = g12 - l2 * g01
    l3 = m * i1
    i2 = inverse(g22 - l2 * g02 - l3 * m, g22)
    b0 = d00
    b1 = d01 - l1 * b0
    b2 = d02 - l2 * b0 - l3 * b1
    c2 = b2 * i2
    c1 = b1 * i1 - l3 * c2
    c0 = b0 * i0 - l1 * c1 - l2 * c2
    return c0, c1, c2


def adjoint_kernel(
    p0_ref, p1_ref, p2_ref, gain_ref, dots_ref, f_ref,
    disp_ref, shifted_ref, wpart_ref,
    u_ref, yz_ref, lg_ref, s32_ref,
):
    c0, c1, c2 = coefficients(dots_ref)

    def combine(x, carry):
        for k in range(3):
            u_ref[k, x] = c0 * p0_ref[k, x] + c1 * p1_ref[k, x] + c2 * p2_ref[k, x]
        return carry

    lax.fori_loop(0, 7, combine, 0)
    for k in range(3):
        for x in range(D):
            disp_ref[k, x] = u_ref[k, x + 1, 4 : 4 + H, :]
    stage_a(u_ref, 0, yz_ref, 0, 6)

    def tile(rows, lanes):
        low = [yz_ref[i, 0, rows, lanes] for i in range(12)]
        for x in range(6):
            high = [yz_ref[i, x + 1, rows, lanes] for i in range(12)]
            grad = gain_ref[x, rows, lanes] * energy_of(along_x(low, high))
            lg_ref[1, x, rows, lanes] = grad.astype(bf16).astype(f32)
            low = high

    tiles(tile)
    lane = iota((R, Z), 1)
    row = iota((R, Z), 0) - 4
    reach = (row >= -1) & (row <= H)
    for x in range(6):
        grad = jnp.where(reach, lg_ref[1, x], 0.0)
        lg_ref[1, x] = grad
        lg_ref[0, x] = jnp.where(lane < Z - 1, pltpu.roll(grad, Z - 1, 1), 0.0)
        lg_ref[2, x] = jnp.where(lane > 0, pltpu.roll(grad, 1, 1), 0.0)
    cross = jnp.zeros((NT, KT), f32)
    for x in range(D):
        for ox in range(3):
            for oz in range(3):
                q = 3 * ox + oz
                s32_ref[q * R : (q + 1) * R, :] = lg_ref[oz, x - (ox - 1) + 1]
        rows = s32_ref[...].astype(bf16)
        shifted_ref[x] = rows
        cross = cross + lax.dot_general(
            rows,
            f_ref[:, x].reshape(KT, Z),
            (((1,), (1,)), ((), ())),
            preferred_element_type=f32,
        )
    away = iota((R, KT), 1) % H - (iota((R, KT), 0) - 4)
    wide = [None] * 27
    for ox in range(3):
        for oz in range(3):
            q = 3 * ox + oz
            block = cross[q * R : (q + 1) * R, :]
            for oy in range(3):
                picked = jnp.where(away == oy - 1, block, 0.0)
                wide[9 * ox + 3 * oy + oz] = jnp.sum(picked, axis=0, keepdims=True)
    for t in range(27):
        s32_ref[t : t + 1, :] = wide[t][:, :Z]
        s32_ref[32 + t : 33 + t, :] = wide[t][:, Z:]
    s32_ref[27:32, :] = jnp.zeros((5, Z), f32)
    gather = (iota((Z, 128), 0) // H == iota((Z, 128), 1)).astype(f32)
    other = (iota((Z, 128), 0) // H + 8 == iota((Z, 128), 1)).astype(f32)
    narrow = jnp.dot(
        s32_ref[0:32, :], gather, precision=lax.Precision.HIGHEST, preferred_element_type=f32
    ) + jnp.dot(
        s32_ref[32:64, :], other, precision=lax.Precision.HIGHEST, preferred_element_type=f32
    )
    packed = narrow[0:4, :]
    for g in range(1, 8):
        packed = packed + pltpu.roll(narrow[4 * g : 4 * g + 4, :], C * g, 1)
    wpart_ref[...] = jnp.broadcast_to(packed[None], wpart_ref.shape)


def finish_kernel(parts_ref, out_ref):
    total = jnp.sum(parts_ref[...], axis=0)
    count = lax.axis_size("slab") * D * lax.axis_size("cross") * H * Z
    taps = [total[:, 0:C]]
    for g in range(1, 8):
        taps.append(pltpu.roll(total, 128 - C * g, 1)[:, 0:C])
    turned = jnp.concatenate(taps, axis=0).T
    out_ref[...] = turned[:, 0:27] * (1.0 / math.sqrt(count))


def feature_kernel(table_ref, shifted_ref, out_ref):
    turned = table_ref[...].astype(f32).T.astype(bf16)
    for x in range(D):
        product = jnp.dot(turned, shifted_ref[x], preferred_element_type=f32)
        out_ref[:, x] = product.astype(bf16).reshape(C, H, Z)


def share(x):
    return lax.all_to_all(x, ("slab", "cross"), 0, 0)


def on_device(load, fixed_dofs, features, conv_weight, active_bricks):
    def to_next(x, axis):
        return lax.ppermute(x, axis, [(i, i + 1) for i in range(lax.axis_size(axis) - 1)])

    def to_last(x, axis):
        return lax.ppermute(x, axis, [(i + 1, i) for i in range(lax.axis_size(axis) - 1)])

    devices = lax.axis_size(("slab", "cross"))
    q = jnp.where(fixed_dofs != 0, held, load)
    qlo = to_next(q, "slab")
    qhi = to_last(q, "slab")
    ids = active_bricks.reshape(1, 256)
    rows = shape_of(12 + D + 2, 4, Z)
    logit, yup, ydown, table = call(
        conv_kernel,
        [shape_of(D + 2, R, Z), rows, rows, shape_of(NT, KT, dtype=bf16)],
        [pltpu.VMEM((NT, KT), f32), pltpu.VMEM((3, D + 2, R, Z), f32)],
        n_in=4,
    )(ids, conv_weight.T, features, q)
    ylo = to_next(yup, "cross")
    yhi = to_last(ydown, "cross")
    wide = shape_of(4 * R + 96, Z)
    logit, xup, xdown = call(pack_kernel, [shape_of(D + 2, R, Z), wide, wide], n_in=3)(
        logit, ylo, yhi
    )
    xlo = to_next(xup, "slab")
    xhi = to_last(xdown, "slab")
    field = shape_of(3, 7, R, Z)
    whole = pltpu.VMEM((3, 11, R, Z), f32)
    p0, p1, p2, gain, dots = call(
        krylov_kernel,
        [field, field, field, shape_of(6, R, Z), shape_of(devices, 1, 128)],
        [
            whole,
            whole,
            whole,
            whole,
            pltpu.VMEM((10, R, Z), f32),
            pltpu.VMEM((12, 11, R, Z), f32),
            pltpu.VMEM((12, 11, R, Z), f32),
            pltpu.VMEM((6, 8, 128), f32),
        ],
        n_in=8,
    )(qlo, q, qhi, logit, xlo, xhi, ylo, yhi)
    displacement, shifted, wpart = call(
        adjoint_kernel,
        [shape_of(3, D, H, Z), shape_of(D, NT, Z, dtype=bf16), shape_of(devices, 4, 128)],
        [
            pltpu.VMEM((3, 7, R, Z), f32),
            pltpu.VMEM((12, 7, R, Z), f32),
            pltpu.VMEM((3, 6, R, Z), f32),
            pltpu.VMEM((NT, Z), f32),
        ],
        n_in=6,
    )(p0, p1, p2, gain, share(dots), features)
    parts = share(wpart)
    feature_grad = call(feature_kernel, shape_of(C, D, H, Z, dtype=bf16), n_in=2)(table, shifted)
    weight_grad = call(finish_kernel, shape_of(C, 27), n_in=1)(parts).T
    return displacement, feature_grad, weight_grad


def solution(mesh):
    in_specs = (
        P(None, "slab", "cross", None),
        P(None, "slab", "cross", None),
        P(None, "slab", "cross", None),
        P(),
        P("slab", "cross", None),
    )
    out_specs = (P(None, "slab", "cross", None), P(None, "slab", "cross", None), P())
    return jax.shard_map(
        on_device, mesh=mesh, in_specs=in_specs, out_specs=out_specs, check_vma=False
    )
```

```python
import math

import jax
import jax.numpy as jnp
from jax import lax
from jax.experimental import pallas as pl
from jax.experimental.pallas import tpu as pltpu
from jax.sharding import PartitionSpec as P


INTERPRET = False

void_modulus = 0.001
spring = 0.1
shift = 0.4
held = 64.0
dead = -1e30
poisson = 0.3
lame = poisson / ((1.0 + poisson) * (1.0 - 2.0 * poisson))
shear = 0.5 / (1.0 + poisson)

D, H, Z, C = 4, 32, 256, 16
R = 40
TILES = R // 8
KT = C * H
NT = 9 * R

f32 = jnp.float32
bf16 = jnp.bfloat16


def iota(shape, dim):
    return lax.broadcasted_iota(jnp.int32, shape, dim)


def call(kernel, out_shape, scratch, *args, resident=True):
    vmem = pl.BlockSpec(memory_space=pltpu.VMEM)
    if not INTERPRET:
        space = pltpu.VMEM if resident else pltpu.HBM
        args = [pltpu.with_memory_space_constraint(x, space) for x in args]
    return pl.pallas_call(
        kernel,
        out_shape=out_shape,
        in_specs=[vmem] * len(args),
        out_specs=[vmem] * len(out_shape),
        scratch_shapes=scratch,
        compiler_params=pltpu.CompilerParams(vmem_limit_bytes=24 * 1024 * 1024),
        interpret=INTERPRET,
    )(*args)


def shape_of(*dims, dtype=f32):
    if INTERPRET:
        return jax.ShapeDtypeStruct(dims, dtype)
    return pltpu.VMEM(dims, dtype)


def toeplitz(w_ref, t_ref):
    spread = (iota((C, KT), 1) // H == iota((C, KT), 0)).astype(bf16)
    wide = lax.dot_general(
        w_ref[...], spread, (((0,), (0,)), ((), ())), preferred_element_type=f32
    )
    away = iota((R, KT), 1) % H - (iota((R, KT), 0) - 4)
    for ox in range(3):
        for oz in range(3):
            block = jnp.zeros((R, KT), f32)
            for oy in range(3):
                t = 9 * ox + 3 * oy + oz
                block = jnp.where(away == oy - 1, wide[t : t + 1, :], block)
            t_ref[(3 * ox + oz) * R : (3 * ox + oz + 1) * R, :] = block


def is_edge(axis, last):
    return lax.axis_index(axis) == (lax.axis_size(axis) - 1 if last else 0)


def conv_kernel(
    ids_ref, w_ref, f_ref, load_ref, fixed_ref,
    q_ref, l_ref, up_ref, down_ref, tout_ref, t_ref, acc_ref,
):
    q_ref[...] = jnp.where(fixed_ref[...] != 0, held, load_ref[...])
    for k in range(3):
        for x in range(D):
            up_ref[4 * k + x] = q_ref[k, x, H - 4 : H, :]
            down_ref[4 * k + x] = q_ref[k, x, 0:4, :]
    toeplitz(w_ref, t_ref)
    table = t_ref[...].astype(bf16)
    tout_ref[...] = table
    acc_ref[...] = jnp.zeros_like(acc_ref)
    for xin in range(D):
        product = jnp.dot(table, f_ref[:, xin].reshape(KT, Z), preferred_element_type=f32)
        for ox in range(3):
            for oz in range(3):
                q = 3 * ox + oz
                acc_ref[oz, xin - (ox - 1) + 1] += product[q * R : (q + 1) * R, :]
    ids = jnp.broadcast_to(ids_ref[...], (R, 256))
    row = iota((R, 256), 0) - 4
    own = (row >= 0) & (row < H)
    pick_y = ((ids >> 6) == (row >> 2)) & own
    ids = jnp.broadcast_to(ids_ref[...], (Z, 256))
    pick_z = (ids >= 0) & ((ids & 63) == (iota((Z, 256), 0) >> 2))
    live = lax.dot_general(
        pick_y.astype(f32).astype(bf16),
        pick_z.astype(f32).astype(bf16),
        (((1,), (1,)), ((), ())),
        preferred_element_type=f32,
    )
    lane = iota((R, Z), 1)
    row = iota((R, Z), 0) - 4
    last_y = jnp.where(is_edge("cross", True), H - 1, H)
    killed = own & ((live < 0.5) | (lane == Z - 1) | (row >= last_y))
    for x in range(D + 2):
        behind = jnp.where(lane > 0, pltpu.roll(acc_ref[0, x], 1, 1), 0.0)
        ahead = jnp.where(lane < Z - 1, pltpu.roll(acc_ref[2, x], Z - 1, 1), 0.0)
        logit = acc_ref[1, x] + behind + ahead
        if 1 <= x <= D:
            gone = killed
            if x == D:
                gone = gone | (own & is_edge("slab", True))
            logit = jnp.where(gone, dead, logit)
        l_ref[x] = logit
        up_ref[12 + x] = logit[33:37, :]
        down_ref[12 + x] = logit[3:7, :]


def pack_kernel(l_ref, ylo_ref, yhi_ref, l2_ref, up_ref, down_ref):
    l2_ref[...] = l_ref[...]
    for x in range(D + 2):
        l2_ref[x, 1:5, :] += ylo_ref[12 + x]
        l2_ref[x, 35:39, :] += yhi_ref[12 + x]
    for x in range(4):
        up_ref[R * x : R * x + R, :] = l2_ref[x + 2]
        down_ref[R * x : R * x + R, :] = l2_ref[x]
    for i in range(12):
        for ref in (up_ref, down_ref):
            ref[4 * R + 8 * i : 4 * R + 8 * i + 4, :] = ylo_ref[i]
            ref[4 * R + 8 * i + 4 : 4 * R + 8 * i + 8, :] = yhi_ref[i]


def stage_a(v_ref, base, yz_ref, first, last):
    def plane(x, carry):
        for k in range(3):
            v = v_ref[k, x - base]
            z = pltpu.roll(v, Z - 1, 1)
            s = v + z
            d = z - v
            sy = pltpu.roll(s, R - 1, 0)
            dy = pltpu.roll(d, R - 1, 0)
            yz_ref[4 * k, x] = s + sy
            yz_ref[4 * k + 1, x] = sy - s
            yz_ref[4 * k + 2, x] = d + dy
            yz_ref[4 * k + 3, x] = dy - d
        return carry

    lax.fori_loop(first, last + 1, plane, 0)


def along_x(low, high):
    a = {}
    for k in range(3):
        for f in range(4):
            v0, v1 = low[4 * k + f], high[4 * k + f]
            if f:
                a[0, f, k] = v0 + v1
            a[1, f, k] = v1 - v0
    return a


def hooke(a, s):
    def scaled(value):
        return value if s is None else s * value

    lam, two_mu, mu = scaled(lame / 16), scaled(shear / 8), scaled(shear / 16)
    lam3, mu3, last = scaled(lame / 48), scaled(shear / 48), scaled((lame + 4 * shear) / 144)
    x, y, z = 0, 1, 2
    out = {}
    n = ((1, 0, x), (0, 1, y), (0, 2, z))
    trace = lam * (a[n[0]] + a[n[1]] + a[n[2]])
    for m in n:
        out[m] = trace + two_mu * a[m]
    for m, o in (((0, 1, x), (1, 0, y)), ((0, 2, x), (1, 0, z)), ((0, 2, y), (0, 1, z))):
        out[m] = out[o] = mu * (a[m] + a[o])
    for m, o in (((1, 1, x), (0, 3, z)), ((1, 1, y), (1, 2, z)), ((1, 2, x), (0, 3, y))):
        both = lam3 * (a[m] + a[o])
        out[m] = both + mu * a[m]
        out[o] = both + mu * a[o]
    m = ((0, 3, x), (1, 2, y), (1, 1, z))
    three = a[m[0]] + a[m[1]] + a[m[2]]
    for o in m:
        out[o] = mu3 * (three + a[o])
    for k in range(3):
        out[1, 3, k] = last * a[1, 3, k]
    return out


def tiles(body):
    def step(j, carry):
        rows = pl.ds(pl.multiple_of(8 * j, 8), 8)
        for half in range(2):
            body(rows, pl.ds(128 * half, 128))
        return carry

    lax.fori_loop(0, TILES, step, 0)


def stage_b(yz_ref, s_ref, g_ref, first, last):
    def tile(rows, lanes):
        low = [yz_ref[i, first, rows, lanes] for i in range(12)]
        carried = None
        for x in range(first, last + 1):
            high = [yz_ref[i, x + 1, rows, lanes] for i in range(12)]
            force = hooke(along_x(low, high), s_ref[x, rows, lanes])
            kept = []
            for k in range(3):
                for f in range(4):
                    diff = force[1, f, k]
                    if f:
                        near, far = force[0, f, k] - diff, force[0, f, k] + diff
                    else:
                        near, far = -diff, diff
                    if carried is not None:
                        g_ref[4 * k + f, x, rows, lanes] = near + carried[4 * k + f]
                    kept.append(far)
            carried = kept
            low = high

    tiles(tile)


def stage_c(g_ref, v_ref, m_ref, out_ref, base, first, last):
    def plane(x, carry):
        for k in range(3):
            g = [g_ref[4 * k + f, x] for f in range(4)]
            s = (g[0] - g[1]) + pltpu.roll(g[0] + g[1], 1, 0)
            d = (g[2] - g[3]) + pltpu.roll(g[2] + g[3], 1, 0)
            out = (s - d) + pltpu.roll(s + d, 1, 1)
            out_ref[k, x - base] = m_ref[k, x] * out + (spring - shift) * v_ref[k, x]
        return carry

    lax.fori_loop(first, last + 1, plane, 0)


def energy_of(a):
    force = hooke(a, None)
    total = None
    for key in a:
        term = a[key] * force[key]
        total = term if total is None else total + term
    return total


def krylov_kernel(
    qlo_ref, q_ref, qhi_ref, l_ref, xlo_ref, xhi_ref, ylo_ref, yhi_ref,
    p0_ref, p1_ref, p2_ref, gain_ref, dots_ref,
    v0_ref, v1_ref, v2_ref, m_ref, s_ref, yz_ref, g_ref, acc_ref,
):
    for k in range(3):
        for x in range(11):
            part, at = (x + 1) // 4, (x + 1) % 4
            v1_ref[k, x, 4 : 4 + H, :] = (qlo_ref, q_ref, qhi_ref)[part][k, at]
            i = 4 * k + at
            if part == 1:
                v1_ref[k, x, 0:4, :] = ylo_ref[i]
                v1_ref[k, x, 4 + H :, :] = yhi_ref[i]
            else:
                ref = xhi_ref if part else xlo_ref
                v1_ref[k, x, 0:4, :] = ref[4 * R + 8 * i : 4 * R + 8 * i + 4, :]
                v1_ref[k, x, 4 + H :, :] = ref[4 * R + 8 * i + 4 : 4 * R + 8 * i + 8, :]

    def split(x, carry):
        for k in range(3):
            v = v1_ref[k, x]
            fixed = v > 0.5 * held
            v0_ref[k, x] = jnp.where(fixed, 0.0, v)
            m_ref[k, x] = jnp.where(fixed, 0.0, 1.0)
        return carry

    lax.fori_loop(0, 11, split, 0)

    row = iota((R, Z), 0) - 4
    first_y = jnp.where(is_edge("cross", False), 0, -4)
    last_y = jnp.where(is_edge("cross", True), H - 1, R)
    outside_y = (row < first_y) | (row > last_y)
    for x in range(10):
        logit = None
        if x <= 3:
            logit = xlo_ref[R * x : R * x + R, :]
        if 2 <= x <= 7:
            term = l_ref[x - 2]
            logit = term if logit is None else logit + term
        if x >= 6:
            term = xhi_ref[R * (x - 6) : R * (x - 6) + R, :]
            logit = term if logit is None else logit + term
        gone = (logit < 0.1 * dead) | outside_y
        if x < 3:
            gone = gone | is_edge("slab", False)
        if x > 6:
            gone = gone | is_edge("slab", True)
        density = 1.0 / (1.0 + jnp.exp(-logit))
        cube = density * density * density
        s_ref[x] = jnp.where(gone, 0.0, void_modulus + cube * (1.0 - void_modulus))
        if 2 <= x <= 7:
            factor = (-3.0 * (1.0 - void_modulus)) * cube * (1.0 - density)
            gain_ref[x - 2] = jnp.where(gone, 0.0, factor)

    stage_a(v0_ref, 0, yz_ref, 0, 10)
    stage_b(yz_ref, s_ref, g_ref, 0, 9)
    stage_c(g_ref, v0_ref, m_ref, v1_ref, 0, 1, 9)
    stage_a(v1_ref, 0, yz_ref, 1, 9)
    stage_b(yz_ref, s_ref, g_ref, 1, 8)
    stage_c(g_ref, v1_ref, m_ref, v2_ref, 0, 2, 8)
    stage_a(v2_ref, 0, yz_ref, 3, 7)

    acc_ref[...] = jnp.zeros_like(acc_ref)

    def sums(rows, lanes):
        row = iota((8, 128), 0) + rows.start
        own = (row >= 4) & (row < 4 + H)
        total = [jnp.zeros((8, 128), f32) for _ in range(6)]
        for x in range(3, 7):
            for k in range(3):
                v0 = v0_ref[k, x, rows, lanes]
                v1 = v1_ref[k, x, rows, lanes]
                v2 = v2_ref[k, x, rows, lanes]
                pairs = ((v0, v0), (v0, v1), (v1, v1), (v1, v2), (v2, v2))
                for i, (left, right) in enumerate(pairs):
                    total[i] = total[i] + left * right
        low = [yz_ref[i, 3, rows, lanes] for i in range(12)]
        for x in range(3, 7):
            high = [yz_ref[i, x + 1, rows, lanes] for i in range(12)]
            total[5] = total[5] + s_ref[x, rows, lanes] * energy_of(along_x(low, high))
            low = high
        total[5] = total[5] + spring * total[4]
        for i in range(6):
            acc_ref[i] += jnp.where(own, total[i], 0.0)

    tiles(sums)
    lane = iota((1, 128), 1)
    dots = jnp.zeros((1, 128), f32)
    for i in range(6):
        total = jnp.sum(jnp.sum(acc_ref[i], axis=0, keepdims=True), axis=1, keepdims=True)
        dots = jnp.where(lane == i, total, dots)
    dots_ref[...] = jnp.broadcast_to(dots[None], dots_ref.shape)
    for k in range(3):
        for x in range(7):
            p0_ref[k, x] = v0_ref[k, x + 2]
            p1_ref[k, x] = v1_ref[k, x + 2]
            p2_ref[k, x] = v2_ref[k, x + 2]


def coefficients(dots_ref):
    dots = jnp.sum(dots_ref[...], axis=0)
    total = [dots[:, i : i + 1] for i in range(6)]
    d00, d01, d11, d12, d22, g22 = total
    d02 = d11
    g00 = d01 + shift * d00
    g01 = d02 + shift * d01
    g02 = d12 + shift * d02
    g11 = d12 + shift * d11
    g12 = d22 + shift * d12
    tiny = 4e-6

    def inverse(pivot, scale):
        fine = pivot > tiny * scale
        return jnp.where(fine, 1.0 / jnp.where(fine, pivot, 1.0), 0.0)

    i0 = 1.0 / g00
    l1, l2 = g01 * i0, g02 * i0
    i1 = inverse(g11 - l1 * g01, g11)
    m = g12 - l2 * g01
    l3 = m * i1
    i2 = inverse(g22 - l2 * g02 - l3 * m, g22)
    b0 = d00
    b1 = d01 - l1 * b0
    b2 = d02 - l2 * b0 - l3 * b1
    c2 = b2 * i2
    c1 = b1 * i1 - l3 * c2
    c0 = b0 * i0 - l1 * c1 - l2 * c2
    return c0, c1, c2


def adjoint_kernel(
    p0_ref, p1_ref, p2_ref, gain_ref, dots_ref, f_ref,
    disp_ref, shifted_ref, wpart_ref,
    u_ref, yz_ref, lg_ref, s32_ref,
):
    c0, c1, c2 = coefficients(dots_ref)

    def combine(x, carry):
        for k in range(3):
            u_ref[k, x] = c0 * p0_ref[k, x] + c1 * p1_ref[k, x] + c2 * p2_ref[k, x]
        return carry

    lax.fori_loop(0, 7, combine, 0)
    for k in range(3):
        for x in range(D):
            disp_ref[k, x] = u_ref[k, x + 1, 4 : 4 + H, :]
    stage_a(u_ref, 0, yz_ref, 0, 6)

    def tile(rows, lanes):
        low = [yz_ref[i, 0, rows, lanes] for i in range(12)]
        for x in range(6):
            high = [yz_ref[i, x + 1, rows, lanes] for i in range(12)]
            grad = gain_ref[x, rows, lanes] * energy_of(along_x(low, high))
            lg_ref[1, x, rows, lanes] = grad.astype(bf16).astype(f32)
            low = high

    tiles(tile)
    lane = iota((R, Z), 1)
    row = iota((R, Z), 0) - 4
    reach = (row >= -1) & (row <= H)
    for x in range(6):
        grad = jnp.where(reach, lg_ref[1, x], 0.0)
        lg_ref[1, x] = grad
        lg_ref[0, x] = jnp.where(lane < Z - 1, pltpu.roll(grad, Z - 1, 1), 0.0)
        lg_ref[2, x] = jnp.where(lane > 0, pltpu.roll(grad, 1, 1), 0.0)
    cross = jnp.zeros((NT, KT), f32)
    for x in range(D):
        for ox in range(3):
            for oz in range(3):
                q = 3 * ox + oz
                s32_ref[q * R : (q + 1) * R, :] = lg_ref[oz, x - (ox - 1) + 1]
        rows = s32_ref[...].astype(bf16)
        shifted_ref[x] = rows
        cross = cross + lax.dot_general(
            rows,
            f_ref[:, x].reshape(KT, Z),
            (((1,), (1,)), ((), ())),
            preferred_element_type=f32,
        )
    away = iota((R, KT), 1) % H - (iota((R, KT), 0) - 4)
    wide = [None] * 27
    for ox in range(3):
        for oz in range(3):
            q = 3 * ox + oz
            block = cross[q * R : (q + 1) * R, :]
            for oy in range(3):
                picked = jnp.where(away == oy - 1, block, 0.0)
                wide[9 * ox + 3 * oy + oz] = jnp.sum(picked, axis=0, keepdims=True)
    for t in range(27):
        s32_ref[t : t + 1, :] = wide[t][:, :Z]
        s32_ref[32 + t : 33 + t, :] = wide[t][:, Z:]
    s32_ref[27:32, :] = jnp.zeros((5, Z), f32)
    gather = (iota((Z, 128), 0) // H == iota((Z, 128), 1)).astype(f32)
    other = (iota((Z, 128), 0) // H + 8 == iota((Z, 128), 1)).astype(f32)
    narrow = jnp.dot(
        s32_ref[0:32, :], gather, precision=lax.Precision.HIGHEST, preferred_element_type=f32
    ) + jnp.dot(
        s32_ref[32:64, :], other, precision=lax.Precision.HIGHEST, preferred_element_type=f32
    )
    packed = narrow[0:4, :]
    for g in range(1, 8):
        packed = packed + pltpu.roll(narrow[4 * g : 4 * g + 4, :], C * g, 1)
    wpart_ref[...] = jnp.broadcast_to(packed[None], wpart_ref.shape)


def finish_kernel(parts_ref, out_ref):
    total = jnp.sum(parts_ref[...], axis=0)
    count = lax.axis_size("slab") * D * lax.axis_size("cross") * H * Z
    taps = [total[:, 0:C]]
    for g in range(1, 8):
        taps.append(pltpu.roll(total, 128 - C * g, 1)[:, 0:C])
    turned = jnp.concatenate(taps, axis=0).T
    out_ref[...] = turned[:, 0:27] * (1.0 / math.sqrt(count))


def feature_kernel(table_ref, shifted_ref, out_ref):
    turned = table_ref[...].astype(f32).T.astype(bf16)
    for x in range(D):
        product = jnp.dot(turned, shifted_ref[x], preferred_element_type=f32)
        out_ref[:, x] = product.astype(bf16).reshape(C, H, Z)


def share(x):
    return lax.all_to_all(x, ("slab", "cross"), 0, 0)


def on_device(load, fixed_dofs, features, conv_weight, active_bricks):
    def to_next(x, axis):
        return lax.ppermute(x, axis, [(i, i + 1) for i in range(lax.axis_size(axis) - 1)])

    def to_last(x, axis):
        return lax.ppermute(x, axis, [(i + 1, i) for i in range(lax.axis_size(axis) - 1)])

    devices = lax.axis_size(("slab", "cross"))
    ids = active_bricks.reshape(1, 256)
    rows = shape_of(12 + D + 2, 4, Z)
    logits = shape_of(D + 2, R, Z)
    q, logit, yup, ydown, table = call(
        conv_kernel,
        [shape_of(3, D, H, Z), logits, rows, rows, shape_of(NT, KT, dtype=bf16)],
        [pltpu.VMEM((NT, KT), f32), pltpu.VMEM((3, D + 2, R, Z), f32)],
        ids, conv_weight.T, features, load, fixed_dofs,
        resident=False,
    )
    ylo = to_next(yup, "cross")
    yhi = to_last(ydown, "cross")
    qlo = to_next(q, "slab")
    qhi = to_last(q, "slab")
    wide = shape_of(4 * R + 96, Z)
    logit, xup, xdown = call(pack_kernel, [logits, wide, wide], [], logit, ylo, yhi)
    xlo = to_next(xup, "slab")
    xhi = to_last(xdown, "slab")
    field = shape_of(3, 7, R, Z)
    whole = pltpu.VMEM((3, 11, R, Z), f32)
    p0, p1, p2, gain, dots = call(
        krylov_kernel,
        [field, field, field, logits, shape_of(devices, 1, 128)],
        [
            whole,
            whole,
            whole,
            whole,
            pltpu.VMEM((10, R, Z), f32),
            pltpu.VMEM((12, 11, R, Z), f32),
            pltpu.VMEM((12, 11, R, Z), f32),
            pltpu.VMEM((6, 8, 128), f32),
        ],
        qlo, q, qhi, logit, xlo, xhi, ylo, yhi,
    )
    displacement, shifted, wpart = call(
        adjoint_kernel,
        [shape_of(3, D, H, Z), shape_of(D, NT, Z, dtype=bf16), shape_of(devices, 4, 128)],
        [
            pltpu.VMEM((3, 7, R, Z), f32),
            pltpu.VMEM((12, 7, R, Z), f32),
            pltpu.VMEM((3, 6, R, Z), f32),
            pltpu.VMEM((NT, Z), f32),
        ],
        p0, p1, p2, gain, share(dots), features,
    )
    parts = share(wpart)
    (feature_grad,) = call(
        feature_kernel, [jax.ShapeDtypeStruct((C, D, H, Z), bf16)], [], table, shifted
    )
    (weight_grad,) = call(finish_kernel, [jax.ShapeDtypeStruct((C, 27), f32)], [], parts)
    return displacement, feature_grad, weight_grad.T


def sharded(mesh):
    in_specs = (
        P(None, "slab", "cross", None),
        P(None, "slab", "cross", None),
        P(None, "slab", "cross", None),
        P(),
        P("slab", "cross", None),
    )
    out_specs = (P(None, "slab", "cross", None), P(None, "slab", "cross", None), P())

    return jax.shard_map(
        on_device, mesh=mesh, in_specs=in_specs, out_specs=out_specs, check_vma=False
    )


def solution(mesh):
    return sharded(mesh)
```

```python
import math

import jax
import jax.numpy as jnp
from jax import lax
from jax.experimental import pallas as pl
from jax.experimental.pallas import tpu as pltpu
from jax.sharding import PartitionSpec as P


INTERPRET = False

void_modulus = 0.001
spring = 0.1
shift = 0.4
held = 64.0
dead = -1e30
poisson = 0.3
lame = poisson / ((1.0 + poisson) * (1.0 - 2.0 * poisson))
shear = 0.5 / (1.0 + poisson)

D, H, Z, C = 4, 32, 256, 16
R = 40
TILES = R // 8
KT = C * H
NT = 9 * R

f32 = jnp.float32
bf16 = jnp.bfloat16


def iota(shape, dim):
    return lax.broadcasted_iota(jnp.int32, shape, dim)


def call(kernel, out_shape, scratch, *args, resident=True):
    vmem = pl.BlockSpec(memory_space=pltpu.VMEM)
    if not INTERPRET:
        space = pltpu.VMEM if resident else pltpu.HBM
        args = [pltpu.with_memory_space_constraint(x, space) for x in args]
    return pl.pallas_call(
        kernel,
        out_shape=out_shape,
        in_specs=[vmem] * len(args),
        out_specs=[vmem] * len(out_shape),
        scratch_shapes=scratch,
        compiler_params=pltpu.CompilerParams(vmem_limit_bytes=24 * 1024 * 1024),
        interpret=INTERPRET,
    )(*args)


def shape_of(*dims, dtype=f32):
    if INTERPRET:
        return jax.ShapeDtypeStruct(dims, dtype)
    return pltpu.VMEM(dims, dtype)


def toeplitz(w_ref, t_ref):
    spread = (iota((C, KT), 1) // H == iota((C, KT), 0)).astype(bf16)
    wide = lax.dot_general(
        w_ref[...], spread, (((0,), (0,)), ((), ())), preferred_element_type=f32
    )
    away = iota((R, KT), 1) % H - (iota((R, KT), 0) - 4)
    for ox in range(3):
        for oz in range(3):
            block = jnp.zeros((R, KT), f32)
            for oy in range(3):
                t = 9 * ox + 3 * oy + oz
                block = jnp.where(away == oy - 1, wide[t : t + 1, :], block)
            t_ref[(3 * ox + oz) * R : (3 * ox + oz + 1) * R, :] = block


def is_edge(axis, last):
    return lax.axis_index(axis) == (lax.axis_size(axis) - 1 if last else 0)


def conv_kernel(
    ids_ref, w_ref, f_ref, load_ref, fixed_ref,
    q_ref, qup_ref, qdown_ref, l_ref, up_ref, down_ref, tout_ref, t_ref, acc_ref,
):
    q_ref[...] = jnp.where(fixed_ref[...] != 0, held, load_ref[...])
    qup_ref[...] = q_ref[:, D - 2 : D]
    qdown_ref[...] = q_ref[:, 0:3]
    for k in range(3):
        for x in range(D):
            up_ref[4 * k + x] = q_ref[k, x, H - 4 : H, :]
            down_ref[4 * k + x] = q_ref[k, x, 0:4, :]
    toeplitz(w_ref, t_ref)
    table = t_ref[...].astype(bf16)
    tout_ref[...] = table
    acc_ref[...] = jnp.zeros_like(acc_ref)
    for xin in range(D):
        product = jnp.dot(table, f_ref[:, xin].reshape(KT, Z), preferred_element_type=f32)
        for ox in range(3):
            for oz in range(3):
                q = 3 * ox + oz
                acc_ref[oz, xin - (ox - 1) + 1] += product[q * R : (q + 1) * R, :]
    ids = jnp.broadcast_to(ids_ref[...], (R, 256))
    row = iota((R, 256), 0) - 4
    own = (row >= 0) & (row < H)
    pick_y = ((ids >> 6) == (row >> 2)) & own
    ids = jnp.broadcast_to(ids_ref[...], (Z, 256))
    pick_z = (ids >= 0) & ((ids & 63) == (iota((Z, 256), 0) >> 2))
    live = lax.dot_general(
        pick_y.astype(f32).astype(bf16),
        pick_z.astype(f32).astype(bf16),
        (((1,), (1,)), ((), ())),
        preferred_element_type=f32,
    )
    lane = iota((R, Z), 1)
    row = iota((R, Z), 0) - 4
    last_y = jnp.where(is_edge("cross", True), H - 1, H)
    killed = own & ((live < 0.5) | (lane == Z - 1) | (row >= last_y))
    for x in range(D + 2):
        behind = jnp.where(lane > 0, pltpu.roll(acc_ref[0, x], 1, 1), 0.0)
        ahead = jnp.where(lane < Z - 1, pltpu.roll(acc_ref[2, x], Z - 1, 1), 0.0)
        logit = acc_ref[1, x] + behind + ahead
        if 1 <= x <= D:
            gone = killed
            if x == D:
                gone = gone | (own & is_edge("slab", True))
            logit = jnp.where(gone, dead, logit)
        l_ref[x] = logit
        up_ref[12 + x] = logit[33:37, :]
        down_ref[12 + x] = logit[3:7, :]


def pack_kernel(l_ref, ylo_ref, yhi_ref, l2_ref, up_ref, down_ref):
    l2_ref[...] = l_ref[...]
    for x in range(D + 2):
        l2_ref[x, 1:5, :] += ylo_ref[12 + x]
        l2_ref[x, 35:39, :] += yhi_ref[12 + x]
    for x in range(3):
        up_ref[R * x : R * x + R, :] = l2_ref[x + 3]
        down_ref[R * x : R * x + R, :] = l2_ref[x]
    for k in range(3):
        for ref, first, count in ((up_ref, D - 2, 2), (down_ref, 0, 3)):
            for x in range(count):
                at = 3 * R + 8 * (count * k + x)
                ref[at : at + 4, :] = ylo_ref[4 * k + first + x]
                ref[at + 4 : at + 8, :] = yhi_ref[4 * k + first + x]


def stage_a(v_ref, base, yz_ref, first, last):
    def plane(x, carry):
        for k in range(3):
            v = v_ref[k, x - base]
            z = pltpu.roll(v, Z - 1, 1)
            s = v + z
            d = z - v
            sy = pltpu.roll(s, R - 1, 0)
            dy = pltpu.roll(d, R - 1, 0)
            yz_ref[4 * k, x] = s + sy
            yz_ref[4 * k + 1, x] = sy - s
            yz_ref[4 * k + 2, x] = d + dy
            yz_ref[4 * k + 3, x] = dy - d
        return carry

    lax.fori_loop(first, last + 1, plane, 0)


def along_x(low, high):
    a = {}
    for k in range(3):
        for f in range(4):
            v0, v1 = low[4 * k + f], high[4 * k + f]
            if f:
                a[0, f, k] = v0 + v1
            a[1, f, k] = v1 - v0
    return a


def hooke(a, s):
    def scaled(value):
        return value if s is None else s * value

    lam, two_mu, mu = scaled(lame / 16), scaled(shear / 8), scaled(shear / 16)
    lam3, mu3, last = scaled(lame / 48), scaled(shear / 48), scaled((lame + 4 * shear) / 144)
    x, y, z = 0, 1, 2
    out = {}
    n = ((1, 0, x), (0, 1, y), (0, 2, z))
    trace = lam * (a[n[0]] + a[n[1]] + a[n[2]])
    for m in n:
        out[m] = trace + two_mu * a[m]
    for m, o in (((0, 1, x), (1, 0, y)), ((0, 2, x), (1, 0, z)), ((0, 2, y), (0, 1, z))):
        out[m] = out[o] = mu * (a[m] + a[o])
    for m, o in (((1, 1, x), (0, 3, z)), ((1, 1, y), (1, 2, z)), ((1, 2, x), (0, 3, y))):
        both = lam3 * (a[m] + a[o])
        out[m] = both + mu * a[m]
        out[o] = both + mu * a[o]
    m = ((0, 3, x), (1, 2, y), (1, 1, z))
    three = a[m[0]] + a[m[1]] + a[m[2]]
    for o in m:
        out[o] = mu3 * (three + a[o])
    for k in range(3):
        out[1, 3, k] = last * a[1, 3, k]
    return out


def tiles(body):
    def step(j, carry):
        rows = pl.ds(pl.multiple_of(8 * j, 8), 8)
        for half in range(2):
            body(rows, pl.ds(128 * half, 128))
        return carry

    lax.fori_loop(0, TILES, step, 0)


def stage_b(yz_ref, s_ref, g_ref, first, last):
    def tile(rows, lanes):
        low = [yz_ref[i, first, rows, lanes] for i in range(12)]
        carried = None
        for x in range(first, last + 1):
            high = [yz_ref[i, x + 1, rows, lanes] for i in range(12)]
            force = hooke(along_x(low, high), s_ref[x, rows, lanes])
            kept = []
            for k in range(3):
                for f in range(4):
                    diff = force[1, f, k]
                    if f:
                        near, far = force[0, f, k] - diff, force[0, f, k] + diff
                    else:
                        near, far = -diff, diff
                    if carried is not None:
                        g_ref[4 * k + f, x, rows, lanes] = near + carried[4 * k + f]
                    kept.append(far)
            carried = kept
            low = high

    tiles(tile)


def stage_c(g_ref, v_ref, m_ref, out_ref, base, first, last):
    def plane(x, carry):
        for k in range(3):
            g = [g_ref[4 * k + f, x] for f in range(4)]
            s = (g[0] - g[1]) + pltpu.roll(g[0] + g[1], 1, 0)
            d = (g[2] - g[3]) + pltpu.roll(g[2] + g[3], 1, 0)
            out = (s - d) + pltpu.roll(s + d, 1, 1)
            out_ref[k, x - base] = m_ref[k, x] * out + (spring - shift) * v_ref[k, x]
        return carry

    lax.fori_loop(first, last + 1, plane, 0)


def energy_of(a):
    force = hooke(a, None)
    total = None
    for key in a:
        term = a[key] * force[key]
        total = term if total is None else total + term
    return total


def krylov_kernel(
    qlo_ref, q_ref, qhi_ref, l_ref, xlo_ref, xhi_ref, ylo_ref, yhi_ref,
    v0_ref, v1_ref, v2_ref, pup_ref, pdown_ref, gain_ref, dots_ref,
    m_ref, s_ref, yz_ref, g_ref, acc_ref,
):
    for k in range(3):
        for x in range(9):
            if x < 2:
                ref, main, at = xlo_ref, qlo_ref[k, x], 3 * R + 8 * (2 * k + x)
            elif x < 6:
                ref, main, at = None, q_ref[k, x - 2], 4 * k + x - 2
            else:
                ref, main, at = xhi_ref, qhi_ref[k, x - 6], 3 * R + 8 * (3 * k + x - 6)
            v1_ref[k, x, 4 : 4 + H, :] = main
            if ref is None:
                v1_ref[k, x, 0:4, :] = ylo_ref[at]
                v1_ref[k, x, 4 + H :, :] = yhi_ref[at]
            else:
                v1_ref[k, x, 0:4, :] = ref[at : at + 4, :]
                v1_ref[k, x, 4 + H :, :] = ref[at + 4 : at + 8, :]

    def split(x, carry):
        for k in range(3):
            v = v1_ref[k, x]
            fixed = v > 0.5 * held
            v0_ref[k, x] = jnp.where(fixed, 0.0, v)
            m_ref[k, x] = jnp.where(fixed, 0.0, 1.0)
        return carry

    lax.fori_loop(0, 9, split, 0)

    row = iota((R, Z), 0) - 4
    first_y = jnp.where(is_edge("cross", False), 0, -4)
    last_y = jnp.where(is_edge("cross", True), H - 1, R)
    outside_y = (row < first_y) | (row > last_y)
    for x in range(8):
        logit = None
        if x <= 2:
            logit = xlo_ref[R * x : R * x + R, :]
        if 1 <= x <= 6:
            term = l_ref[x - 1]
            logit = term if logit is None else logit + term
        if x >= 5:
            term = xhi_ref[R * (x - 5) : R * (x - 5) + R, :]
            logit = term if logit is None else logit + term
        gone = (logit < 0.1 * dead) | outside_y
        if x < 2:
            gone = gone | is_edge("slab", False)
        if x > 5:
            gone = gone | is_edge("slab", True)
        density = 1.0 / (1.0 + jnp.exp(-logit))
        cube = density * density * density
        s_ref[x] = jnp.where(gone, 0.0, void_modulus + cube * (1.0 - void_modulus))
        if 1 <= x <= 6:
            factor = (-3.0 * (1.0 - void_modulus)) * cube * (1.0 - density)
            gain_ref[x - 1] = jnp.where(gone, 0.0, factor)

    stage_a(v0_ref, 0, yz_ref, 0, 8)
    stage_b(yz_ref, s_ref, g_ref, 0, 7)
    stage_c(g_ref, v0_ref, m_ref, v1_ref, 0, 1, 7)
    stage_a(v1_ref, 0, yz_ref, 1, 7)
    stage_b(yz_ref, s_ref, g_ref, 1, 6)
    stage_c(g_ref, v1_ref, m_ref, v2_ref, 0, 2, 6)
    for k in range(3):
        pup_ref[k] = v2_ref[k, 5]
        pdown_ref[k] = v2_ref[k, 3]
    stage_a(v2_ref, 0, yz_ref, 2, 6)

    acc_ref[...] = jnp.zeros_like(acc_ref)

    def sums(rows, lanes):
        row = iota((8, 128), 0) + rows.start
        own = (row >= 4) & (row < 4 + H)
        total = [jnp.zeros((8, 128), f32) for _ in range(6)]
        for x in range(2, 6):
            for k in range(3):
                v0 = v0_ref[k, x, rows, lanes]
                v1 = v1_ref[k, x, rows, lanes]
                v2 = v2_ref[k, x, rows, lanes]
                pairs = ((v0, v0), (v0, v1), (v1, v1), (v1, v2), (v2, v2))
                for i, (left, right) in enumerate(pairs):
                    total[i] = total[i] + left * right
        low = [yz_ref[i, 2, rows, lanes] for i in range(12)]
        for x in range(2, 6):
            high = [yz_ref[i, x + 1, rows, lanes] for i in range(12)]
            total[5] = total[5] + s_ref[x, rows, lanes] * energy_of(along_x(low, high))
            low = high
        total[5] = total[5] + spring * total[4]
        for i in range(6):
            acc_ref[i] += jnp.where(own, total[i], 0.0)

    tiles(sums)
    lane = iota((1, 128), 1)
    dots = jnp.zeros((1, 128), f32)
    for i in range(6):
        total = jnp.sum(jnp.sum(acc_ref[i], axis=0, keepdims=True), axis=1, keepdims=True)
        dots = jnp.where(lane == i, total, dots)
    dots_ref[...] = jnp.broadcast_to(dots[None], dots_ref.shape)


def coefficients(dots_ref):
    dots = jnp.sum(dots_ref[...], axis=0)
    total = [dots[:, i : i + 1] for i in range(6)]
    d00, d01, d11, d12, d22, g22 = total
    d02 = d11
    g00 = d01 + shift * d00
    g01 = d02 + shift * d01
    g02 = d12 + shift * d02
    g11 = d12 + shift * d11
    g12 = d22 + shift * d12
    tiny = 4e-6

    def inverse(pivot, scale):
        fine = pivot > tiny * scale
        return jnp.where(fine, 1.0 / jnp.where(fine, pivot, 1.0), 0.0)

    i0 = 1.0 / g00
    l1, l2 = g01 * i0, g02 * i0
    i1 = inverse(g11 - l1 * g01, g11)
    m = g12 - l2 * g01
    l3 = m * i1
    i2 = inverse(g22 - l2 * g02 - l3 * m, g22)
    b0 = d00
    b1 = d01 - l1 * b0
    b2 = d02 - l2 * b0 - l3 * b1
    c2 = b2 * i2
    c1 = b1 * i1 - l3 * c2
    c0 = b0 * i0 - l1 * c1 - l2 * c2
    return c0, c1, c2


def adjoint_kernel(
    p0_ref, p1_ref, p2_ref, plo_ref, phi_ref, gain_ref, dots_ref, f_ref,
    disp_ref, shifted_ref, wpart_ref,
    u_ref, yz_ref, lg_ref, s32_ref,
):
    c0, c1, c2 = coefficients(dots_ref)

    def combine(x, carry):
        for k in range(3):
            u_ref[k, x] += c0 * p0_ref[k, x + 1] + c1 * p1_ref[k, x + 1]
        return carry

    for k in range(3):
        u_ref[k, 0] = c2 * plo_ref[k]
        for x in range(1, 6):
            u_ref[k, x] = c2 * p2_ref[k, x + 1]
        u_ref[k, 6] = c2 * phi_ref[k]
    lax.fori_loop(0, 7, combine, 0)
    for k in range(3):
        for x in range(D):
            disp_ref[k, x] = u_ref[k, x + 1, 4 : 4 + H, :]
    stage_a(u_ref, 0, yz_ref, 0, 6)

    def tile(rows, lanes):
        low = [yz_ref[i, 0, rows, lanes] for i in range(12)]
        for x in range(6):
            high = [yz_ref[i, x + 1, rows, lanes] for i in range(12)]
            grad = gain_ref[x, rows, lanes] * energy_of(along_x(low, high))
            lg_ref[1, x, rows, lanes] = grad.astype(bf16).astype(f32)
            low = high

    tiles(tile)
    lane = iota((R, Z), 1)
    row = iota((R, Z), 0) - 4
    reach = (row >= -1) & (row <= H)
    for x in range(6):
        grad = jnp.where(reach, lg_ref[1, x], 0.0)
        lg_ref[1, x] = grad
        lg_ref[0, x] = jnp.where(lane < Z - 1, pltpu.roll(grad, Z - 1, 1), 0.0)
        lg_ref[2, x] = jnp.where(lane > 0, pltpu.roll(grad, 1, 1), 0.0)
    cross = jnp.zeros((NT, KT), f32)
    for x in range(D):
        for ox in range(3):
            for oz in range(3):
                q = 3 * ox + oz
                s32_ref[q * R : (q + 1) * R, :] = lg_ref[oz, x - (ox - 1) + 1]
        rows = s32_ref[...].astype(bf16)
        shifted_ref[x] = rows
        cross = cross + lax.dot_general(
            rows,
            f_ref[:, x].reshape(KT, Z),
            (((1,), (1,)), ((), ())),
            preferred_element_type=f32,
        )
    away = iota((R, KT), 1) % H - (iota((R, KT), 0) - 4)
    wide = [None] * 27
    for ox in range(3):
        for oz in range(3):
            q = 3 * ox + oz
            block = cross[q * R : (q + 1) * R, :]
            for oy in range(3):
                picked = jnp.where(away == oy - 1, block, 0.0)
                wide[9 * ox + 3 * oy + oz] = jnp.sum(picked, axis=0, keepdims=True)
    for t in range(27):
        s32_ref[t : t + 1, :] = wide[t][:, :Z]
        s32_ref[32 + t : 33 + t, :] = wide[t][:, Z:]
    s32_ref[27:32, :] = jnp.zeros((5, Z), f32)
    gather = (iota((Z, 128), 0) // H == iota((Z, 128), 1)).astype(f32)
    other = (iota((Z, 128), 0) // H + 8 == iota((Z, 128), 1)).astype(f32)
    narrow = jnp.dot(
        s32_ref[0:32, :], gather, precision=lax.Precision.HIGHEST, preferred_element_type=f32
    ) + jnp.dot(
        s32_ref[32:64, :], other, precision=lax.Precision.HIGHEST, preferred_element_type=f32
    )
    packed = narrow[0:4, :]
    for g in range(1, 8):
        packed = packed + pltpu.roll(narrow[4 * g : 4 * g + 4, :], C * g, 1)
    wpart_ref[...] = jnp.broadcast_to(packed[None], wpart_ref.shape)


def finish_kernel(parts_ref, out_ref):
    total = jnp.sum(parts_ref[...], axis=0)
    count = lax.axis_size("slab") * D * lax.axis_size("cross") * H * Z
    taps = [total[:, 0:C]]
    for g in range(1, 8):
        taps.append(pltpu.roll(total, 128 - C * g, 1)[:, 0:C])
    turned = jnp.concatenate(taps, axis=0).T
    out_ref[...] = turned[:, 0:27] * (1.0 / math.sqrt(count))


def feature_kernel(table_ref, shifted_ref, out_ref):
    turned = table_ref[...].astype(f32).T.astype(bf16)
    for x in range(D):
        product = jnp.dot(turned, shifted_ref[x], preferred_element_type=f32)
        out_ref[:, x] = product.astype(bf16).reshape(C, H, Z)


def share(x):
    return lax.all_to_all(x, ("slab", "cross"), 0, 0)


def on_device(load, fixed_dofs, features, conv_weight, active_bricks):
    def to_next(x, axis):
        return lax.ppermute(x, axis, [(i, i + 1) for i in range(lax.axis_size(axis) - 1)])

    def to_last(x, axis):
        return lax.ppermute(x, axis, [(i + 1, i) for i in range(lax.axis_size(axis) - 1)])

    devices = lax.axis_size(("slab", "cross"))
    ids = active_bricks.reshape(1, 256)
    rows = shape_of(12 + D + 2, 4, Z)
    logits = shape_of(D + 2, R, Z)
    q, qup, qdown, logit, yup, ydown, table = call(
        conv_kernel,
        [
            shape_of(3, D, H, Z),
            shape_of(3, 2, H, Z),
            shape_of(3, 3, H, Z),
            logits,
            rows,
            rows,
            shape_of(NT, KT, dtype=bf16),
        ],
        [pltpu.VMEM((NT, KT), f32), pltpu.VMEM((3, D + 2, R, Z), f32)],
        ids, conv_weight.T, features, load, fixed_dofs,
        resident=False,
    )
    ylo = to_next(yup, "cross")
    yhi = to_last(ydown, "cross")
    qlo = to_next(qup, "slab")
    qhi = to_last(qdown, "slab")
    logit, xup, xdown = call(
        pack_kernel,
        [logits, shape_of(3 * R + 48, Z), shape_of(3 * R + 72, Z)],
        [],
        logit, ylo, yhi,
    )
    xlo = to_next(xup, "slab")
    xhi = to_last(xdown, "slab")
    field = shape_of(3, 9, R, Z)
    plane = shape_of(3, R, Z)
    p0, p1, p2, pup, pdown, gain, dots = call(
        krylov_kernel,
        [field, field, field, plane, plane, logits, shape_of(devices, 1, 128)],
        [
            pltpu.VMEM((3, 9, R, Z), f32),
            pltpu.VMEM((8, R, Z), f32),
            pltpu.VMEM((12, 9, R, Z), f32),
            pltpu.VMEM((12, 9, R, Z), f32),
            pltpu.VMEM((6, 8, 128), f32),
        ],
        qlo, q, qhi, logit, xlo, xhi, ylo, yhi,
    )
    dots = share(dots)
    plo = to_next(pup, "slab")
    phi = to_last(pdown, "slab")
    displacement, shifted, wpart = call(
        adjoint_kernel,
        [shape_of(3, D, H, Z), shape_of(D, NT, Z, dtype=bf16), shape_of(devices, 4, 128)],
        [
            pltpu.VMEM((3, 7, R, Z), f32),
            pltpu.VMEM((12, 7, R, Z), f32),
            pltpu.VMEM((3, 6, R, Z), f32),
            pltpu.VMEM((NT, Z), f32),
        ],
        p0, p1, p2, plo, phi, gain, dots, features,
    )
    parts = share(wpart)
    (feature_grad,) = call(
        feature_kernel, [jax.ShapeDtypeStruct((C, D, H, Z), bf16)], [], table, shifted
    )
    (weight_grad,) = call(finish_kernel, [jax.ShapeDtypeStruct((C, 27), f32)], [], parts)
    return displacement, feature_grad, weight_grad.T


def sharded(mesh):
    in_specs = (
        P(None, "slab", "cross", None),
        P(None, "slab", "cross", None),
        P(None, "slab", "cross", None),
        P(),
        P("slab", "cross", None),
    )
    out_specs = (P(None, "slab", "cross", None), P(None, "slab", "cross", None), P())

    return jax.shard_map(
        on_device, mesh=mesh, in_specs=in_specs, out_specs=out_specs, check_vma=False
    )


def solution(mesh):
    return sharded(mesh)
```

```python
import math

import jax
import jax.numpy as jnp
from jax import lax
from jax.experimental import pallas as pl
from jax.experimental.pallas import tpu as pltpu
from jax.sharding import PartitionSpec as P


INTERPRET = False

void_modulus = 0.001
spring = 0.1
shift = 0.4
held = 64.0
dead = -1e30
poisson = 0.3
lame = poisson / ((1.0 + poisson) * (1.0 - 2.0 * poisson))
shear = 0.5 / (1.0 + poisson)

D, H, Z, C = 4, 32, 256, 16
R = 40
TILES = R // 8
KT = C * H
NT = 9 * R

f32 = jnp.float32
bf16 = jnp.bfloat16


def iota(shape, dim):
    return lax.broadcasted_iota(jnp.int32, shape, dim)


def call(kernel, out_shape, scratch, *args, resident=True):
    vmem = pl.BlockSpec(memory_space=pltpu.VMEM)
    if not INTERPRET:
        space = pltpu.VMEM if resident else pltpu.HBM
        args = [pltpu.with_memory_space_constraint(x, space) for x in args]
    return pl.pallas_call(
        kernel,
        out_shape=out_shape,
        in_specs=[vmem] * len(args),
        out_specs=[vmem] * len(out_shape),
        scratch_shapes=scratch,
        compiler_params=pltpu.CompilerParams(vmem_limit_bytes=24 * 1024 * 1024),
        interpret=INTERPRET,
    )(*args)


def shape_of(*dims, dtype=f32):
    if INTERPRET:
        return jax.ShapeDtypeStruct(dims, dtype)
    return pltpu.VMEM(dims, dtype)


def toeplitz(w_ref, t_ref):
    spread = (iota((C, KT), 1) // H == iota((C, KT), 0)).astype(bf16)
    wide = lax.dot_general(
        w_ref[...], spread, (((0,), (0,)), ((), ())), preferred_element_type=f32
    )
    away = iota((R, KT), 1) % H - (iota((R, KT), 0) - 4)
    for ox in range(3):
        for oz in range(3):
            block = jnp.zeros((R, KT), f32)
            for oy in range(3):
                t = 9 * ox + 3 * oy + oz
                block = jnp.where(away == oy - 1, wide[t : t + 1, :], block)
            t_ref[(3 * ox + oz) * R : (3 * ox + oz + 1) * R, :] = block


def is_edge(axis, last):
    return lax.axis_index(axis) == (lax.axis_size(axis) - 1 if last else 0)


def by_parity(axis, body):
    even = lax.axis_index(axis) % 2 == 0
    pl.when(even)(lambda: body(True))
    pl.when(jnp.logical_not(even))(lambda: body(False))


def conv_kernel(
    ids_ref, w_ref, f_ref, load_ref, fixed_ref,
    q_ref, qone_ref, qtwo_ref, l_ref, yone_ref, ytwo_ref, tout_ref, t_ref, acc_ref,
):
    q_ref[...] = jnp.where(fixed_ref[...] != 0, held, load_ref[...])

    def send_length(even):
        up_ref, down_ref = (qone_ref, qtwo_ref) if even else (qtwo_ref, qone_ref)
        up_ref[...] = q_ref[:, D - 3 : D]
        down_ref[...] = q_ref[:, 0:3]

    by_parity("slab", send_length)
    toeplitz(w_ref, t_ref)
    table = t_ref[...].astype(bf16)
    tout_ref[...] = table
    acc_ref[...] = jnp.zeros_like(acc_ref)
    for xin in range(D):
        product = jnp.dot(table, f_ref[:, xin].reshape(KT, Z), preferred_element_type=f32)
        for ox in range(3):
            for oz in range(3):
                q = 3 * ox + oz
                acc_ref[oz, xin - (ox - 1) + 1] += product[q * R : (q + 1) * R, :]
    ids = jnp.broadcast_to(ids_ref[...], (R, 256))
    row = iota((R, 256), 0) - 4
    own = (row >= 0) & (row < H)
    pick_y = ((ids >> 6) == (row >> 2)) & own
    ids = jnp.broadcast_to(ids_ref[...], (Z, 256))
    pick_z = (ids >= 0) & ((ids & 63) == (iota((Z, 256), 0) >> 2))
    live = lax.dot_general(
        pick_y.astype(f32).astype(bf16),
        pick_z.astype(f32).astype(bf16),
        (((1,), (1,)), ((), ())),
        preferred_element_type=f32,
    )
    lane = iota((R, Z), 1)
    row = iota((R, Z), 0) - 4
    last_y = jnp.where(is_edge("cross", True), H - 1, H)
    killed = own & ((live < 0.5) | (lane == Z - 1) | (row >= last_y))
    for x in range(D + 2):
        behind = jnp.where(lane > 0, pltpu.roll(acc_ref[0, x], 1, 1), 0.0)
        ahead = jnp.where(lane < Z - 1, pltpu.roll(acc_ref[2, x], Z - 1, 1), 0.0)
        logit = acc_ref[1, x] + behind + ahead
        if 1 <= x <= D:
            gone = killed
            if x == D:
                gone = gone | (own & is_edge("slab", True))
            logit = jnp.where(gone, dead, logit)
        l_ref[x] = logit

    def send_section(even):
        up_ref, down_ref = (yone_ref, ytwo_ref) if even else (ytwo_ref, yone_ref)
        for k in range(3):
            for x in range(D):
                up_ref[4 * k + x] = q_ref[k, x, H - 4 : H, :]
                down_ref[4 * k + x] = q_ref[k, x, 0:4, :]
        for x in range(D + 2):
            up_ref[12 + x] = l_ref[x, 33:37, :]
            down_ref[12 + x] = l_ref[x, 3:7, :]

    by_parity("cross", send_section)


def pack_kernel(l_ref, yone_ref, ytwo_ref, l2_ref, ylo_ref, yhi_ref, one_ref, two_ref):
    l2_ref[...] = l_ref[...]

    def receive(even):
        ylo_ref[...] = ytwo_ref[...] if even else yone_ref[...]
        yhi_ref[...] = yone_ref[...] if even else ytwo_ref[...]

    by_parity("cross", receive)
    for x in range(D + 2):
        l2_ref[x, 1:5, :] += ylo_ref[12 + x]
        l2_ref[x, 35:39, :] += yhi_ref[12 + x]

    def send(even):
        up_ref, down_ref = (one_ref, two_ref) if even else (two_ref, one_ref)
        for x in range(3):
            up_ref[R * x : R * x + R, :] = l2_ref[x + 3]
            down_ref[R * x : R * x + R, :] = l2_ref[x]
        for k in range(3):
            for ref, first in ((up_ref, D - 3), (down_ref, 0)):
                for x in range(3):
                    at = 3 * R + 8 * (3 * k + x)
                    ref[at : at + 4, :] = ylo_ref[4 * k + first + x]
                    ref[at + 4 : at + 8, :] = yhi_ref[4 * k + first + x]

    by_parity("slab", send)


def stage_a(v_ref, base, yz_ref, first, last):
    def plane(x, carry):
        for k in range(3):
            v = v_ref[k, x - base]
            z = pltpu.roll(v, Z - 1, 1)
            s = v + z
            d = z - v
            sy = pltpu.roll(s, R - 1, 0)
            dy = pltpu.roll(d, R - 1, 0)
            yz_ref[4 * k, x] = s + sy
            yz_ref[4 * k + 1, x] = sy - s
            yz_ref[4 * k + 2, x] = d + dy
            yz_ref[4 * k + 3, x] = dy - d
        return carry

    lax.fori_loop(first, last + 1, plane, 0)


def along_x(low, high):
    a = {}
    for k in range(3):
        for f in range(4):
            v0, v1 = low[4 * k + f], high[4 * k + f]
            if f:
                a[0, f, k] = v0 + v1
            a[1, f, k] = v1 - v0
    return a


def hooke(a, s):
    def scaled(value):
        return value if s is None else s * value

    lam, two_mu, mu = scaled(lame / 16), scaled(shear / 8), scaled(shear / 16)
    lam3, mu3, last = scaled(lame / 48), scaled(shear / 48), scaled((lame + 4 * shear) / 144)
    x, y, z = 0, 1, 2
    out = {}
    n = ((1, 0, x), (0, 1, y), (0, 2, z))
    trace = lam * (a[n[0]] + a[n[1]] + a[n[2]])
    for m in n:
        out[m] = trace + two_mu * a[m]
    for m, o in (((0, 1, x), (1, 0, y)), ((0, 2, x), (1, 0, z)), ((0, 2, y), (0, 1, z))):
        out[m] = out[o] = mu * (a[m] + a[o])
    for m, o in (((1, 1, x), (0, 3, z)), ((1, 1, y), (1, 2, z)), ((1, 2, x), (0, 3, y))):
        both = lam3 * (a[m] + a[o])
        out[m] = both + mu * a[m]
        out[o] = both + mu * a[o]
    m = ((0, 3, x), (1, 2, y), (1, 1, z))
    three = a[m[0]] + a[m[1]] + a[m[2]]
    for o in m:
        out[o] = mu3 * (three + a[o])
    for k in range(3):
        out[1, 3, k] = last * a[1, 3, k]
    return out


def tiles(body):
    def step(j, carry):
        rows = pl.ds(pl.multiple_of(8 * j, 8), 8)
        for half in range(2):
            body(rows, pl.ds(128 * half, 128))
        return carry

    lax.fori_loop(0, TILES, step, 0)


def stage_b(yz_ref, s_ref, g_ref, first, last):
    def tile(rows, lanes):
        low = [yz_ref[i, first, rows, lanes] for i in range(12)]
        carried = None
        for x in range(first, last + 1):
            high = [yz_ref[i, x + 1, rows, lanes] for i in range(12)]
            force = hooke(along_x(low, high), s_ref[x, rows, lanes])
            kept = []
            for k in range(3):
                for f in range(4):
                    diff = force[1, f, k]
                    if f:
                        near, far = force[0, f, k] - diff, force[0, f, k] + diff
                    else:
                        near, far = -diff, diff
                    if carried is not None:
                        g_ref[4 * k + f, x, rows, lanes] = near + carried[4 * k + f]
                    kept.append(far)
            carried = kept
            low = high

    tiles(tile)


def stage_c(g_ref, v_ref, m_ref, out_ref, base, first, last):
    def plane(x, carry):
        for k in range(3):
            g = [g_ref[4 * k + f, x] for f in range(4)]
            s = (g[0] - g[1]) + pltpu.roll(g[0] + g[1], 1, 0)
            d = (g[2] - g[3]) + pltpu.roll(g[2] + g[3], 1, 0)
            out = (s - d) + pltpu.roll(s + d, 1, 1)
            out_ref[k, x - base] = m_ref[k, x] * out + (spring - shift) * v_ref[k, x]
        return carry

    lax.fori_loop(first, last + 1, plane, 0)


def energy_of(a):
    force = hooke(a, None)
    total = None
    for key in a:
        term = a[key] * force[key]
        total = term if total is None else total + term
    return total


def krylov_kernel(
    qone_ref, q_ref, qtwo_ref, l_ref, one_ref, two_ref, ylo_ref, yhi_ref,
    v0_ref, v1_ref, v2_ref, pone_ref, ptwo_ref, gain_ref, dots_ref,
    m_ref, s_ref, yz_ref, g_ref, acc_ref,
):
    for k in range(3):
        for x in range(D):
            v1_ref[k, x + 2, 0:4, :] = ylo_ref[4 * k + x]
            v1_ref[k, x + 2, 4 : 4 + H, :] = q_ref[k, x]
            v1_ref[k, x + 2, 4 + H :, :] = yhi_ref[4 * k + x]
    for x in range(1, 7):
        s_ref[x] = l_ref[x - 1]

    def receive(even):
        low = (two_ref, qtwo_ref) if even else (one_ref, qone_ref)
        high = (one_ref, qone_ref) if even else (two_ref, qtwo_ref)
        for k in range(3):
            for (ref, main), places in ((low, ((1, 0), (2, 1))), (high, ((0, 6), (1, 7), (2, 8)))):
                for source, x in places:
                    at = 3 * R + 8 * (3 * k + source)
                    v1_ref[k, x, 0:4, :] = ref[at : at + 4, :]
                    v1_ref[k, x, 4 : 4 + H, :] = main[k, source]
                    v1_ref[k, x, 4 + H :, :] = ref[at + 4 : at + 8, :]
        s_ref[0] = low[0][0:R, :]
        s_ref[7] = high[0][2 * R : 3 * R, :]
        for x in (1, 2):
            s_ref[x] += low[0][R * x : R * x + R, :]
        for x in (5, 6):
            s_ref[x] += high[0][R * (x - 5) : R * (x - 5) + R, :]

    by_parity("slab", receive)

    def split(x, carry):
        for k in range(3):
            v = v1_ref[k, x]
            fixed = v > 0.5 * held
            v0_ref[k, x] = jnp.where(fixed, 0.0, v)
            m_ref[k, x] = jnp.where(fixed, 0.0, 1.0)
        return carry

    lax.fori_loop(0, 9, split, 0)

    row = iota((R, Z), 0) - 4
    first_y = jnp.where(is_edge("cross", False), 0, -4)
    last_y = jnp.where(is_edge("cross", True), H - 1, R)
    outside_y = (row < first_y) | (row > last_y)
    for x in range(8):
        logit = s_ref[x]
        gone = (logit < 0.1 * dead) | outside_y
        if x < 2:
            gone = gone | is_edge("slab", False)
        if x > 5:
            gone = gone | is_edge("slab", True)
        density = 1.0 / (1.0 + jnp.exp(-logit))
        cube = density * density * density
        s_ref[x] = jnp.where(gone, 0.0, void_modulus + cube * (1.0 - void_modulus))
        if 1 <= x <= 6:
            factor = (-3.0 * (1.0 - void_modulus)) * cube * (1.0 - density)
            gain_ref[x - 1] = jnp.where(gone, 0.0, factor)

    stage_a(v0_ref, 0, yz_ref, 0, 8)
    stage_b(yz_ref, s_ref, g_ref, 0, 7)
    stage_c(g_ref, v0_ref, m_ref, v1_ref, 0, 1, 7)
    stage_a(v1_ref, 0, yz_ref, 1, 7)
    stage_b(yz_ref, s_ref, g_ref, 1, 6)
    stage_c(g_ref, v1_ref, m_ref, v2_ref, 0, 2, 6)

    def send(even):
        pone_ref[...] = v2_ref[:, 5 if even else 3]
        ptwo_ref[...] = v2_ref[:, 3 if even else 5]

    by_parity("slab", send)
    stage_a(v2_ref, 0, yz_ref, 2, 6)

    acc_ref[...] = jnp.zeros_like(acc_ref)

    def sums(rows, lanes):
        row = iota((8, 128), 0) + rows.start
        own = (row >= 4) & (row < 4 + H)
        total = [jnp.zeros((8, 128), f32) for _ in range(6)]
        for x in range(2, 6):
            for k in range(3):
                v0 = v0_ref[k, x, rows, lanes]
                v1 = v1_ref[k, x, rows, lanes]
                v2 = v2_ref[k, x, rows, lanes]
                pairs = ((v0, v0), (v0, v1), (v1, v1), (v1, v2), (v2, v2))
                for i, (left, right) in enumerate(pairs):
                    total[i] = total[i] + left * right
        low = [yz_ref[i, 2, rows, lanes] for i in range(12)]
        for x in range(2, 6):
            high = [yz_ref[i, x + 1, rows, lanes] for i in range(12)]
            total[5] = total[5] + s_ref[x, rows, lanes] * energy_of(along_x(low, high))
            low = high
        total[5] = total[5] + spring * total[4]
        for i in range(6):
            acc_ref[i] += jnp.where(own, total[i], 0.0)

    tiles(sums)
    lane = iota((1, 128), 1)
    dots = jnp.zeros((1, 128), f32)
    for i in range(6):
        total = jnp.sum(jnp.sum(acc_ref[i], axis=0, keepdims=True), axis=1, keepdims=True)
        dots = jnp.where(lane == i, total, dots)
    dots_ref[...] = jnp.broadcast_to(dots[None], dots_ref.shape)


def coefficients(dots_ref):
    dots = jnp.sum(dots_ref[...], axis=0)
    total = [dots[:, i : i + 1] for i in range(6)]
    d00, d01, d11, d12, d22, g22 = total
    d02 = d11
    g00 = d01 + shift * d00
    g01 = d02 + shift * d01
    g02 = d12 + shift * d02
    g11 = d12 + shift * d11
    g12 = d22 + shift * d12
    tiny = 4e-6

    def inverse(pivot, scale):
        fine = pivot > tiny * scale
        return jnp.where(fine, 1.0 / jnp.where(fine, pivot, 1.0), 0.0)

    i0 = 1.0 / g00
    l1, l2 = g01 * i0, g02 * i0
    i1 = inverse(g11 - l1 * g01, g11)
    m = g12 - l2 * g01
    l3 = m * i1
    i2 = inverse(g22 - l2 * g02 - l3 * m, g22)
    b0 = d00
    b1 = d01 - l1 * b0
    b2 = d02 - l2 * b0 - l3 * b1
    c2 = b2 * i2
    c1 = b1 * i1 - l3 * c2
    c0 = b0 * i0 - l1 * c1 - l2 * c2
    return c0, c1, c2


def adjoint_kernel(
    p0_ref, p1_ref, p2_ref, pone_ref, ptwo_ref, gain_ref, dots_ref, f_ref,
    disp_ref, shifted_ref, wpart_ref,
    u_ref, yz_ref, lg_ref, s32_ref,
):
    c0, c1, c2 = coefficients(dots_ref)

    def combine(x, carry):
        for k in range(3):
            u_ref[k, x] += c0 * p0_ref[k, x + 1] + c1 * p1_ref[k, x + 1]
        return carry

    for k in range(3):
        for x in range(1, 6):
            u_ref[k, x] = c2 * p2_ref[k, x + 1]

    def receive(even):
        u_ref[:, 0] = c2 * (ptwo_ref if even else pone_ref)[...]
        u_ref[:, 6] = c2 * (pone_ref if even else ptwo_ref)[...]

    by_parity("slab", receive)
    lax.fori_loop(0, 7, combine, 0)
    for k in range(3):
        for x in range(D):
            disp_ref[k, x] = u_ref[k, x + 1, 4 : 4 + H, :]
    stage_a(u_ref, 0, yz_ref, 0, 6)

    def tile(rows, lanes):
        low = [yz_ref[i, 0, rows, lanes] for i in range(12)]
        for x in range(6):
            high = [yz_ref[i, x + 1, rows, lanes] for i in range(12)]
            grad = gain_ref[x, rows, lanes] * energy_of(along_x(low, high))
            lg_ref[1, x, rows, lanes] = grad.astype(bf16).astype(f32)
            low = high

    tiles(tile)
    lane = iota((R, Z), 1)
    row = iota((R, Z), 0) - 4
    reach = (row >= -1) & (row <= H)
    for x in range(6):
        grad = jnp.where(reach, lg_ref[1, x], 0.0)
        lg_ref[1, x] = grad
        lg_ref[0, x] = jnp.where(lane < Z - 1, pltpu.roll(grad, Z - 1, 1), 0.0)
        lg_ref[2, x] = jnp.where(lane > 0, pltpu.roll(grad, 1, 1), 0.0)
    cross = jnp.zeros((NT, KT), f32)
    for x in range(D):
        for ox in range(3):
            for oz in range(3):
                q = 3 * ox + oz
                s32_ref[q * R : (q + 1) * R, :] = lg_ref[oz, x - (ox - 1) + 1]
        rows = s32_ref[...].astype(bf16)
        shifted_ref[x] = rows
        cross = cross + lax.dot_general(
            rows,
            f_ref[:, x].reshape(KT, Z),
            (((1,), (1,)), ((), ())),
            preferred_element_type=f32,
        )
    away = iota((R, KT), 1) % H - (iota((R, KT), 0) - 4)
    wide = [None] * 27
    for ox in range(3):
        for oz in range(3):
            q = 3 * ox + oz
            block = cross[q * R : (q + 1) * R, :]
            for oy in range(3):
                picked = jnp.where(away == oy - 1, block, 0.0)
                wide[9 * ox + 3 * oy + oz] = jnp.sum(picked, axis=0, keepdims=True)
    for t in range(27):
        s32_ref[t : t + 1, :] = wide[t][:, :Z]
        s32_ref[32 + t : 33 + t, :] = wide[t][:, Z:]
    s32_ref[27:32, :] = jnp.zeros((5, Z), f32)
    gather = (iota((Z, 128), 0) // H == iota((Z, 128), 1)).astype(f32)
    other = (iota((Z, 128), 0) // H + 8 == iota((Z, 128), 1)).astype(f32)
    narrow = jnp.dot(
        s32_ref[0:32, :], gather, precision=lax.Precision.HIGHEST, preferred_element_type=f32
    ) + jnp.dot(
        s32_ref[32:64, :], other, precision=lax.Precision.HIGHEST, preferred_element_type=f32
    )
    packed = narrow[0:4, :]
    for g in range(1, 8):
        packed = packed + pltpu.roll(narrow[4 * g : 4 * g + 4, :], C * g, 1)
    wpart_ref[...] = jnp.broadcast_to(packed[None], wpart_ref.shape)


def finish_kernel(parts_ref, out_ref):
    total = jnp.sum(parts_ref[...], axis=0)
    count = lax.axis_size("slab") * D * lax.axis_size("cross") * H * Z
    taps = [total[:, 0:C]]
    for g in range(1, 8):
        taps.append(pltpu.roll(total, 128 - C * g, 1)[:, 0:C])
    turned = jnp.concatenate(taps, axis=0).T
    out_ref[...] = turned[:, 0:27] * (1.0 / math.sqrt(count))


def feature_kernel(table_ref, shifted_ref, out_ref):
    turned = table_ref[...].astype(f32).T.astype(bf16)
    for x in range(D):
        product = jnp.dot(turned, shifted_ref[x], preferred_element_type=f32)
        out_ref[:, x] = product.astype(bf16).reshape(C, H, Z)


def share(x):
    return lax.all_to_all(x, ("slab", "cross"), 0, 0)


def on_device(load, fixed_dofs, features, conv_weight, active_bricks):
    def swap(x, axis, start):
        pairs = [(i, i + 1) for i in range(start, lax.axis_size(axis) - 1, 2)]
        return lax.ppermute(x, axis, pairs + [(j, i) for i, j in pairs])

    def exchange(first, second, axis):
        return swap(first, axis, 0), swap(second, axis, 1)

    devices = lax.axis_size(("slab", "cross"))
    ids = active_bricks.reshape(1, 256)
    rows = shape_of(12 + D + 2, 4, Z)
    logits = shape_of(D + 2, R, Z)
    q, qone, qtwo, logit, yone, ytwo, table = call(
        conv_kernel,
        [
            shape_of(3, D, H, Z),
            shape_of(3, 3, H, Z),
            shape_of(3, 3, H, Z),
            logits,
            rows,
            rows,
            shape_of(NT, KT, dtype=bf16),
        ],
        [pltpu.VMEM((NT, KT), f32), pltpu.VMEM((3, D + 2, R, Z), f32)],
        ids, conv_weight.T, features, load, fixed_dofs,
        resident=False,
    )
    yone, ytwo = exchange(yone, ytwo, "cross")
    qone, qtwo = exchange(qone, qtwo, "slab")
    wide = shape_of(3 * R + 72, Z)
    logit, ylo, yhi, xone, xtwo = call(
        pack_kernel, [logits, rows, rows, wide, wide], [], logit, yone, ytwo
    )
    xone, xtwo = exchange(xone, xtwo, "slab")
    field = shape_of(3, 9, R, Z)
    plane = shape_of(3, R, Z)
    p0, p1, p2, pone, ptwo, gain, dots = call(
        krylov_kernel,
        [field, field, field, plane, plane, logits, shape_of(devices, 1, 128)],
        [
            pltpu.VMEM((3, 9, R, Z), f32),
            pltpu.VMEM((8, R, Z), f32),
            pltpu.VMEM((12, 9, R, Z), f32),
            pltpu.VMEM((12, 9, R, Z), f32),
            pltpu.VMEM((6, 8, 128), f32),
        ],
        qone, q, qtwo, logit, xone, xtwo, ylo, yhi,
    )
    dots = share(dots)
    pone, ptwo = exchange(pone, ptwo, "slab")
    displacement, shifted, wpart = call(
        adjoint_kernel,
        [shape_of(3, D, H, Z), shape_of(D, NT, Z, dtype=bf16), shape_of(devices, 4, 128)],
        [
            pltpu.VMEM((3, 7, R, Z), f32),
            pltpu.VMEM((12, 7, R, Z), f32),
            pltpu.VMEM((3, 6, R, Z), f32),
            pltpu.VMEM((NT, Z), f32),
        ],
        p0, p1, p2, pone, ptwo, gain, dots, features,
    )
    parts = share(wpart)
    (feature_grad,) = call(
        feature_kernel, [jax.ShapeDtypeStruct((C, D, H, Z), bf16)], [], table, shifted
    )
    (weight_grad,) = call(finish_kernel, [jax.ShapeDtypeStruct((C, 27), f32)], [], parts)
    return displacement, feature_grad, weight_grad.T


def sharded(mesh):
    in_specs = (
        P(None, "slab", "cross", None),
        P(None, "slab", "cross", None),
        P(None, "slab", "cross", None),
        P(),
        P("slab", "cross", None),
    )
    out_specs = (P(None, "slab", "cross", None), P(None, "slab", "cross", None), P())

    return jax.shard_map(
        on_device, mesh=mesh, in_specs=in_specs, out_specs=out_specs, check_vma=False
    )


def solution(mesh):
    return sharded(mesh)
```

```python
import math

import jax
import jax.numpy as jnp
from jax import lax
from jax.experimental import pallas as pl
from jax.experimental.pallas import tpu as pltpu
from jax.sharding import PartitionSpec as P


INTERPRET = False

void_modulus = 0.001
spring = 0.1
shift = 0.4
held = 64.0
dead = -1e30
poisson = 0.3
lame = poisson / ((1.0 + poisson) * (1.0 - 2.0 * poisson))
shear = 0.5 / (1.0 + poisson)

D, H, Z, C = 4, 32, 256, 16
R = 40
TILES = R // 8
KT = C * H
NT = 9 * R

f32 = jnp.float32
bf16 = jnp.bfloat16


def iota(shape, dim):
    return lax.broadcasted_iota(jnp.int32, shape, dim)


def call(kernel, out_shape, scratch, *args, outside=0):
    vmem = pl.BlockSpec(memory_space=pltpu.VMEM)
    if not INTERPRET:
        spaces = [pltpu.HBM] * outside + [pltpu.VMEM] * (len(args) - outside)
        args = [pltpu.with_memory_space_constraint(x, s) for x, s in zip(args, spaces)]
    return pl.pallas_call(
        kernel,
        out_shape=out_shape,
        in_specs=[vmem] * len(args),
        out_specs=[vmem] * len(out_shape),
        scratch_shapes=scratch,
        compiler_params=pltpu.CompilerParams(vmem_limit_bytes=24 * 1024 * 1024),
        interpret=INTERPRET,
    )(*args)


def shape_of(*dims, dtype=f32):
    if INTERPRET:
        return jax.ShapeDtypeStruct(dims, dtype)
    return pltpu.VMEM(dims, dtype)


def toeplitz(w_ref, t_ref):
    spread = (iota((C, KT), 1) // H == iota((C, KT), 0)).astype(bf16)
    wide = lax.dot_general(
        w_ref[...], spread, (((0,), (0,)), ((), ())), preferred_element_type=f32
    )
    away = iota((R, KT), 1) % H - (iota((R, KT), 0) - 4)
    for ox in range(3):
        for oz in range(3):
            block = jnp.zeros((R, KT), f32)
            for oy in range(3):
                t = 9 * ox + 3 * oy + oz
                block = jnp.where(away == oy - 1, wide[t : t + 1, :], block)
            t_ref[(3 * ox + oz) * R : (3 * ox + oz + 1) * R, :] = block


def is_edge(axis, last):
    return lax.axis_index(axis) == (lax.axis_size(axis) - 1 if last else 0)


def by_parity(axis, body):
    even = lax.axis_index(axis) % 2 == 0
    pl.when(even)(lambda: body(True))
    pl.when(jnp.logical_not(even))(lambda: body(False))


def residual_kernel(load_ref, fixed_ref, q_ref, qone_ref, qtwo_ref):
    q_ref[...] = jnp.where(fixed_ref[...] != 0, held, load_ref[...])

    def send_length(even):
        up_ref, down_ref = (qone_ref, qtwo_ref) if even else (qtwo_ref, qone_ref)
        up_ref[...] = q_ref[:, D - 3 : D]
        down_ref[...] = q_ref[:, 0:3]

    by_parity("slab", send_length)


def conv_kernel(
    ids_ref, w_ref, f_ref, q_ref, l_ref, yone_ref, ytwo_ref, tout_ref, t_ref, acc_ref
):
    toeplitz(w_ref, t_ref)
    table = t_ref[...].astype(bf16)
    tout_ref[...] = table
    acc_ref[...] = jnp.zeros_like(acc_ref)
    for xin in range(D):
        product = jnp.dot(table, f_ref[:, xin].reshape(KT, Z), preferred_element_type=f32)
        for ox in range(3):
            for oz in range(3):
                q = 3 * ox + oz
                acc_ref[oz, xin - (ox - 1) + 1] += product[q * R : (q + 1) * R, :]
    ids = jnp.broadcast_to(ids_ref[...], (R, 256))
    row = iota((R, 256), 0) - 4
    own = (row >= 0) & (row < H)
    pick_y = ((ids >> 6) == (row >> 2)) & own
    ids = jnp.broadcast_to(ids_ref[...], (Z, 256))
    pick_z = (ids >= 0) & ((ids & 63) == (iota((Z, 256), 0) >> 2))
    live = lax.dot_general(
        pick_y.astype(f32).astype(bf16),
        pick_z.astype(f32).astype(bf16),
        (((1,), (1,)), ((), ())),
        preferred_element_type=f32,
    )
    lane = iota((R, Z), 1)
    row = iota((R, Z), 0) - 4
    last_y = jnp.where(is_edge("cross", True), H - 1, H)
    killed = own & ((live < 0.5) | (lane == Z - 1) | (row >= last_y))
    for x in range(D + 2):
        behind = jnp.where(lane > 0, pltpu.roll(acc_ref[0, x], 1, 1), 0.0)
        ahead = jnp.where(lane < Z - 1, pltpu.roll(acc_ref[2, x], Z - 1, 1), 0.0)
        logit = acc_ref[1, x] + behind + ahead
        if 1 <= x <= D:
            gone = killed
            if x == D:
                gone = gone | (own & is_edge("slab", True))
            logit = jnp.where(gone, dead, logit)
        l_ref[x] = logit

    def send_section(even):
        up_ref, down_ref = (yone_ref, ytwo_ref) if even else (ytwo_ref, yone_ref)
        for k in range(3):
            for x in range(D):
                up_ref[4 * k + x] = q_ref[k, x, H - 4 : H, :]
                down_ref[4 * k + x] = q_ref[k, x, 0:4, :]
        for x in range(D + 2):
            up_ref[12 + x] = l_ref[x, 33:37, :]
            down_ref[12 + x] = l_ref[x, 3:7, :]

    by_parity("cross", send_section)


def pack_kernel(l_ref, yone_ref, ytwo_ref, l2_ref, ylo_ref, yhi_ref, one_ref, two_ref):
    l2_ref[...] = l_ref[...]

    def receive(even):
        ylo_ref[...] = ytwo_ref[...] if even else yone_ref[...]
        yhi_ref[...] = yone_ref[...] if even else ytwo_ref[...]

    by_parity("cross", receive)
    for x in range(D + 2):
        l2_ref[x, 1:5, :] += ylo_ref[12 + x]
        l2_ref[x, 35:39, :] += yhi_ref[12 + x]

    def send(even):
        up_ref, down_ref = (one_ref, two_ref) if even else (two_ref, one_ref)
        for x in range(3):
            up_ref[R * x : R * x + R, :] = l2_ref[x + 3]
            down_ref[R * x : R * x + R, :] = l2_ref[x]
        for k in range(3):
            for ref, first in ((up_ref, D - 3), (down_ref, 0)):
                for x in range(3):
                    at = 3 * R + 8 * (3 * k + x)
                    ref[at : at + 4, :] = ylo_ref[4 * k + first + x]
                    ref[at + 4 : at + 8, :] = yhi_ref[4 * k + first + x]

    by_parity("slab", send)


def stage_a(v_ref, base, yz_ref, first, last):
    def plane(x, carry):
        for k in range(3):
            v = v_ref[k, x - base]
            z = pltpu.roll(v, Z - 1, 1)
            s = v + z
            d = z - v
            sy = pltpu.roll(s, R - 1, 0)
            dy = pltpu.roll(d, R - 1, 0)
            yz_ref[4 * k, x] = s + sy
            yz_ref[4 * k + 1, x] = sy - s
            yz_ref[4 * k + 2, x] = d + dy
            yz_ref[4 * k + 3, x] = dy - d
        return carry

    lax.fori_loop(first, last + 1, plane, 0)


def along_x(low, high):
    a = {}
    for k in range(3):
        for f in range(4):
            v0, v1 = low[4 * k + f], high[4 * k + f]
            if f:
                a[0, f, k] = v0 + v1
            a[1, f, k] = v1 - v0
    return a


def hooke(a, s):
    def scaled(value):
        return value if s is None else s * value

    lam, two_mu, mu = scaled(lame / 16), scaled(shear / 8), scaled(shear / 16)
    lam3, mu3, last = scaled(lame / 48), scaled(shear / 48), scaled((lame + 4 * shear) / 144)
    x, y, z = 0, 1, 2
    out = {}
    n = ((1, 0, x), (0, 1, y), (0, 2, z))
    trace = lam * (a[n[0]] + a[n[1]] + a[n[2]])
    for m in n:
        out[m] = trace + two_mu * a[m]
    for m, o in (((0, 1, x), (1, 0, y)), ((0, 2, x), (1, 0, z)), ((0, 2, y), (0, 1, z))):
        out[m] = out[o] = mu * (a[m] + a[o])
    for m, o in (((1, 1, x), (0, 3, z)), ((1, 1, y), (1, 2, z)), ((1, 2, x), (0, 3, y))):
        both = lam3 * (a[m] + a[o])
        out[m] = both + mu * a[m]
        out[o] = both + mu * a[o]
    m = ((0, 3, x), (1, 2, y), (1, 1, z))
    three = a[m[0]] + a[m[1]] + a[m[2]]
    for o in m:
        out[o] = mu3 * (three + a[o])
    for k in range(3):
        out[1, 3, k] = last * a[1, 3, k]
    return out


def tiles(body):
    def step(j, carry):
        rows = pl.ds(pl.multiple_of(8 * j, 8), 8)
        for half in range(2):
            body(rows, pl.ds(128 * half, 128))
        return carry

    lax.fori_loop(0, TILES, step, 0)


def stage_b(yz_ref, s_ref, g_ref, first, last):
    def tile(rows, lanes):
        low = [yz_ref[i, first, rows, lanes] for i in range(12)]
        carried = None
        for x in range(first, last + 1):
            high = [yz_ref[i, x + 1, rows, lanes] for i in range(12)]
            force = hooke(along_x(low, high), s_ref[x, rows, lanes])
            kept = []
            for k in range(3):
                for f in range(4):
                    diff = force[1, f, k]
                    if f:
                        near, far = force[0, f, k] - diff, force[0, f, k] + diff
                    else:
                        near, far = -diff, diff
                    if carried is not None:
                        g_ref[4 * k + f, x, rows, lanes] = near + carried[4 * k + f]
                    kept.append(far)
            carried = kept
            low = high

    tiles(tile)


def stage_c(g_ref, v_ref, m_ref, out_ref, base, first, last):
    def plane(x, carry):
        for k in range(3):
            g = [g_ref[4 * k + f, x] for f in range(4)]
            s = (g[0] - g[1]) + pltpu.roll(g[0] + g[1], 1, 0)
            d = (g[2] - g[3]) + pltpu.roll(g[2] + g[3], 1, 0)
            out = (s - d) + pltpu.roll(s + d, 1, 1)
            out_ref[k, x - base] = m_ref[k, x] * out + (spring - shift) * v_ref[k, x]
        return carry

    lax.fori_loop(first, last + 1, plane, 0)


def energy_of(a):
    force = hooke(a, None)
    total = None
    for key in a:
        term = a[key] * force[key]
        total = term if total is None else total + term
    return total


def krylov_kernel(
    qone_ref, q_ref, qtwo_ref, l_ref, one_ref, two_ref, ylo_ref, yhi_ref,
    v0_ref, v1_ref, v2_ref, pone_ref, ptwo_ref, gain_ref, dots_ref,
    m_ref, s_ref, yz_ref, g_ref, acc_ref,
):
    for k in range(3):
        for x in range(D):
            v1_ref[k, x + 2, 0:4, :] = ylo_ref[4 * k + x]
            v1_ref[k, x + 2, 4 : 4 + H, :] = q_ref[k, x]
            v1_ref[k, x + 2, 4 + H :, :] = yhi_ref[4 * k + x]
    for x in range(1, 7):
        s_ref[x] = l_ref[x - 1]

    def receive(even):
        low = (two_ref, qtwo_ref) if even else (one_ref, qone_ref)
        high = (one_ref, qone_ref) if even else (two_ref, qtwo_ref)
        for k in range(3):
            for (ref, main), places in ((low, ((1, 0), (2, 1))), (high, ((0, 6), (1, 7), (2, 8)))):
                for source, x in places:
                    at = 3 * R + 8 * (3 * k + source)
                    v1_ref[k, x, 0:4, :] = ref[at : at + 4, :]
                    v1_ref[k, x, 4 : 4 + H, :] = main[k, source]
                    v1_ref[k, x, 4 + H :, :] = ref[at + 4 : at + 8, :]
        s_ref[0] = low[0][0:R, :]
        s_ref[7] = high[0][2 * R : 3 * R, :]
        for x in (1, 2):
            s_ref[x] += low[0][R * x : R * x + R, :]
        for x in (5, 6):
            s_ref[x] += high[0][R * (x - 5) : R * (x - 5) + R, :]

    by_parity("slab", receive)

    def split(x, carry):
        for k in range(3):
            v = v1_ref[k, x]
            fixed = v > 0.5 * held
            v0_ref[k, x] = jnp.where(fixed, 0.0, v)
            m_ref[k, x] = jnp.where(fixed, 0.0, 1.0)
        return carry

    lax.fori_loop(0, 9, split, 0)

    row = iota((R, Z), 0) - 4
    first_y = jnp.where(is_edge("cross", False), 0, -4)
    last_y = jnp.where(is_edge("cross", True), H - 1, R)
    outside_y = (row < first_y) | (row > last_y)
    for x in range(8):
        logit = s_ref[x]
        gone = (logit < 0.1 * dead) | outside_y
        if x < 2:
            gone = gone | is_edge("slab", False)
        if x > 5:
            gone = gone | is_edge("slab", True)
        density = 1.0 / (1.0 + jnp.exp(-logit))
        cube = density * density * density
        s_ref[x] = jnp.where(gone, 0.0, void_modulus + cube * (1.0 - void_modulus))
        if 1 <= x <= 6:
            factor = (-3.0 * (1.0 - void_modulus)) * cube * (1.0 - density)
            gain_ref[x - 1] = jnp.where(gone, 0.0, factor)

    stage_a(v0_ref, 0, yz_ref, 0, 8)
    stage_b(yz_ref, s_ref, g_ref, 0, 7)
    stage_c(g_ref, v0_ref, m_ref, v1_ref, 0, 1, 7)
    stage_a(v1_ref, 0, yz_ref, 1, 7)
    stage_b(yz_ref, s_ref, g_ref, 1, 6)
    stage_c(g_ref, v1_ref, m_ref, v2_ref, 0, 2, 6)

    def send(even):
        pone_ref[...] = v2_ref[:, 5 if even else 3]
        ptwo_ref[...] = v2_ref[:, 3 if even else 5]

    by_parity("slab", send)
    stage_a(v2_ref, 0, yz_ref, 2, 6)

    acc_ref[...] = jnp.zeros_like(acc_ref)

    def sums(rows, lanes):
        row = iota((8, 128), 0) + rows.start
        own = (row >= 4) & (row < 4 + H)
        total = [jnp.zeros((8, 128), f32) for _ in range(6)]
        for x in range(2, 6):
            for k in range(3):
                v0 = v0_ref[k, x, rows, lanes]
                v1 = v1_ref[k, x, rows, lanes]
                v2 = v2_ref[k, x, rows, lanes]
                pairs = ((v0, v0), (v0, v1), (v1, v1), (v1, v2), (v2, v2))
                for i, (left, right) in enumerate(pairs):
                    total[i] = total[i] + left * right
        low = [yz_ref[i, 2, rows, lanes] for i in range(12)]
        for x in range(2, 6):
            high = [yz_ref[i, x + 1, rows, lanes] for i in range(12)]
            total[5] = total[5] + s_ref[x, rows, lanes] * energy_of(along_x(low, high))
            low = high
        total[5] = total[5] + spring * total[4]
        for i in range(6):
            acc_ref[i] += jnp.where(own, total[i], 0.0)

    tiles(sums)
    lane = iota((1, 128), 1)
    dots = jnp.zeros((1, 128), f32)
    for i in range(6):
        total = jnp.sum(jnp.sum(acc_ref[i], axis=0, keepdims=True), axis=1, keepdims=True)
        dots = jnp.where(lane == i, total, dots)
    dots_ref[...] = jnp.broadcast_to(dots[None], dots_ref.shape)


def coefficients(dots_ref):
    dots = jnp.sum(dots_ref[...], axis=0, keepdims=True)
    total = [dots[:, i : i + 1] for i in range(6)]
    d00, d01, d11, d12, d22, g22 = total
    d02 = d11
    g00 = d01 + shift * d00
    g01 = d02 + shift * d01
    g02 = d12 + shift * d02
    g11 = d12 + shift * d11
    g12 = d22 + shift * d12
    tiny = 4e-6

    def inverse(pivot, scale):
        fine = pivot > tiny * scale
        return jnp.where(fine, 1.0 / jnp.where(fine, pivot, 1.0), 0.0)

    i0 = 1.0 / g00
    l1, l2 = g01 * i0, g02 * i0
    i1 = inverse(g11 - l1 * g01, g11)
    m = g12 - l2 * g01
    l3 = m * i1
    i2 = inverse(g22 - l2 * g02 - l3 * m, g22)
    b0 = d00
    b1 = d01 - l1 * b0
    b2 = d02 - l2 * b0 - l3 * b1
    c2 = b2 * i2
    c1 = b1 * i1 - l3 * c2
    c0 = b0 * i0 - l1 * c1 - l2 * c2
    return c0, c1, c2


def adjoint_kernel(
    p0_ref, p1_ref, p2_ref, pone_ref, ptwo_ref, gain_ref, dots_ref, f_ref,
    disp_ref, shifted_ref, wpart_ref,
    u_ref, yz_ref, lg_ref, s32_ref,
):
    c0, c1, c2 = coefficients(dots_ref)

    def combine(x, carry):
        for k in range(3):
            u_ref[k, x] += c0 * p0_ref[k, x + 1] + c1 * p1_ref[k, x + 1]
        return carry

    for k in range(3):
        for x in range(1, 6):
            u_ref[k, x] = c2 * p2_ref[k, x + 1]

    def receive(even):
        u_ref[:, 0] = c2 * (ptwo_ref if even else pone_ref)[...]
        u_ref[:, 6] = c2 * (pone_ref if even else ptwo_ref)[...]

    by_parity("slab", receive)
    lax.fori_loop(0, 7, combine, 0)
    for k in range(3):
        for x in range(D):
            disp_ref[k, x] = u_ref[k, x + 1, 4 : 4 + H, :]
    stage_a(u_ref, 0, yz_ref, 0, 6)

    def tile(rows, lanes):
        low = [yz_ref[i, 0, rows, lanes] for i in range(12)]
        for x in range(6):
            high = [yz_ref[i, x + 1, rows, lanes] for i in range(12)]
            grad = gain_ref[x, rows, lanes] * energy_of(along_x(low, high))
            lg_ref[1, x, rows, lanes] = grad.astype(bf16).astype(f32)
            low = high

    tiles(tile)
    lane = iota((R, Z), 1)
    row = iota((R, Z), 0) - 4
    reach = (row >= -1) & (row <= H)
    for x in range(6):
        grad = jnp.where(reach, lg_ref[1, x], 0.0)
        lg_ref[1, x] = grad
        lg_ref[0, x] = jnp.where(lane < Z - 1, pltpu.roll(grad, Z - 1, 1), 0.0)
        lg_ref[2, x] = jnp.where(lane > 0, pltpu.roll(grad, 1, 1), 0.0)
    cross = jnp.zeros((NT, KT), f32)
    for x in range(D):
        for ox in range(3):
            for oz in range(3):
                q = 3 * ox + oz
                s32_ref[q * R : (q + 1) * R, :] = lg_ref[oz, x - (ox - 1) + 1]
        rows = s32_ref[...].astype(bf16)
        shifted_ref[x] = rows
        cross = cross + lax.dot_general(
            rows,
            f_ref[:, x].reshape(KT, Z),
            (((1,), (1,)), ((), ())),
            preferred_element_type=f32,
        )
    away = iota((R, KT), 1) % H - (iota((R, KT), 0) - 4)
    wide = [None] * 27
    for ox in range(3):
        for oz in range(3):
            q = 3 * ox + oz
            block = cross[q * R : (q + 1) * R, :]
            for oy in range(3):
                picked = jnp.where(away == oy - 1, block, 0.0)
                wide[9 * ox + 3 * oy + oz] = jnp.sum(picked, axis=0, keepdims=True)
    for t in range(27):
        s32_ref[t : t + 1, :] = wide[t][:, :Z]
        s32_ref[32 + t : 33 + t, :] = wide[t][:, Z:]
    s32_ref[27:32, :] = jnp.zeros((5, Z), f32)
    s32_ref[59:64, :] = jnp.zeros((5, Z), f32)
    value = s32_ref[0:64, :]
    terms = []
    for _ in range(3):
        terms.append(value.astype(bf16))
        value = value - terms[-1].astype(f32)
    terms = jnp.concatenate(terms, axis=0)
    gather = (iota((Z, 128), 0) // H == iota((Z, 128), 1)).astype(f32).astype(bf16)
    summed = jnp.dot(terms, gather, preferred_element_type=f32)
    summed = summed[0:64] + summed[64:128] + summed[128:192]
    narrow = summed[0:32, :] + pltpu.roll(summed[32:64, :], 8, 1)
    packed = narrow[0:4, :]
    for g in range(1, 8):
        packed = packed + pltpu.roll(narrow[4 * g : 4 * g + 4, :], C * g, 1)
    wpart_ref[...] = jnp.broadcast_to(packed[None], wpart_ref.shape)


def finish_kernel(parts_ref, out_ref):
    total = jnp.sum(parts_ref[...].reshape(parts_ref.shape[0] // 8, 8, 128), axis=0)
    total = total[0:4, :] + total[4:8, :]
    count = lax.axis_size("slab") * D * lax.axis_size("cross") * H * Z
    taps = [total[:, 0:C]]
    for g in range(1, 8):
        taps.append(pltpu.roll(total, 128 - C * g, 1)[:, 0:C])
    turned = jnp.concatenate(taps, axis=0).T
    out_ref[...] = turned[:, 0:27] * (1.0 / math.sqrt(count))


def feature_kernel(table_ref, shifted_ref, out_ref):
    turned = table_ref[...].astype(f32).T.astype(bf16)
    for x in range(D):
        product = jnp.dot(turned, shifted_ref[x], preferred_element_type=f32)
        out_ref[:, x] = product.astype(bf16).reshape(C, H, Z)


def share(x):
    return lax.all_to_all(x, ("slab", "cross"), 0, 0)


def on_device(load, fixed_dofs, features, conv_weight, active_bricks):
    def swap(x, axis, start):
        pairs = [(i, i + 1) for i in range(start, lax.axis_size(axis) - 1, 2)]
        return lax.ppermute(x, axis, pairs + [(j, i) for i, j in pairs])

    def exchange(first, second, axis):
        return swap(first, axis, 0), swap(second, axis, 1)

    devices = lax.axis_size(("slab", "cross"))
    ids = active_bricks.reshape(1, 256)
    rows = shape_of(12 + D + 2, 4, Z)
    logits = shape_of(D + 2, R, Z)
    part = shape_of(3, 3, H, Z)
    q, qone, qtwo = call(
        residual_kernel, [shape_of(3, D, H, Z), part, part], [], load, fixed_dofs, outside=2
    )
    qone, qtwo = exchange(qone, qtwo, "slab")
    logit, yone, ytwo, table = call(
        conv_kernel,
        [logits, rows, rows, shape_of(NT, KT, dtype=bf16)],
        [pltpu.VMEM((NT, KT), f32), pltpu.VMEM((3, D + 2, R, Z), f32)],
        ids, conv_weight.T, features, q,
        outside=3,
    )
    yone, ytwo = exchange(yone, ytwo, "cross")
    wide = shape_of(3 * R + 72, Z)
    logit, ylo, yhi, xone, xtwo = call(
        pack_kernel, [logits, rows, rows, wide, wide], [], logit, yone, ytwo
    )
    xone, xtwo = exchange(xone, xtwo, "slab")
    field = shape_of(3, 9, R, Z)
    plane = shape_of(3, R, Z)
    p0, p1, p2, pone, ptwo, gain, dots = call(
        krylov_kernel,
        [field, field, field, plane, plane, logits, shape_of(devices, 1, 128)],
        [
            pltpu.VMEM((3, 9, R, Z), f32),
            pltpu.VMEM((8, R, Z), f32),
            pltpu.VMEM((12, 9, R, Z), f32),
            pltpu.VMEM((12, 9, R, Z), f32),
            pltpu.VMEM((6, 8, 128), f32),
        ],
        qone, q, qtwo, logit, xone, xtwo, ylo, yhi,
    )
    dots = share(dots).reshape(devices, 128)
    pone, ptwo = exchange(pone, ptwo, "slab")
    displacement, shifted, wpart = call(
        adjoint_kernel,
        [shape_of(3, D, H, Z), shape_of(D, NT, Z, dtype=bf16), shape_of(devices, 4, 128)],
        [
            pltpu.VMEM((3, 7, R, Z), f32),
            pltpu.VMEM((12, 7, R, Z), f32),
            pltpu.VMEM((3, 6, R, Z), f32),
            pltpu.VMEM((NT, Z), f32),
        ],
        p0, p1, p2, pone, ptwo, gain, dots, features,
    )
    parts = share(wpart).reshape(4 * devices, 128)
    (feature_grad,) = call(
        feature_kernel, [jax.ShapeDtypeStruct((C, D, H, Z), bf16)], [], table, shifted
    )
    (weight_grad,) = call(finish_kernel, [jax.ShapeDtypeStruct((C, 27), f32)], [], parts)
    return displacement, feature_grad, weight_grad.T


def sharded(mesh):
    in_specs = (
        P(None, "slab", "cross", None),
        P(None, "slab", "cross", None),
        P(None, "slab", "cross", None),
        P(),
        P("slab", "cross", None),
    )
    out_specs = (P(None, "slab", "cross", None), P(None, "slab", "cross", None), P())

    return jax.shard_map(
        on_device, mesh=mesh, in_specs=in_specs, out_specs=out_specs, check_vma=False
    )


def solution(mesh):
    return sharded(mesh)
```

```python
import math

import jax
import jax.numpy as jnp
from jax import lax
from jax.experimental import pallas as pl
from jax.experimental.pallas import tpu as pltpu
from jax.sharding import PartitionSpec as P


INTERPRET = False

void_modulus = 0.001
spring = 0.1
shift = 0.4
held = 64.0
dead = -1e30
poisson = 0.3
lame = poisson / ((1.0 + poisson) * (1.0 - 2.0 * poisson))
shear = 0.5 / (1.0 + poisson)

D, H, Z, C = 4, 32, 256, 16
R = 40
TILES = R // 8
KT = C * H
NT = 9 * R

f32 = jnp.float32
bf16 = jnp.bfloat16


def iota(shape, dim):
    return lax.broadcasted_iota(jnp.int32, shape, dim)


def call(kernel, out_shape, scratch, *args, outside=0):
    vmem = pl.BlockSpec(memory_space=pltpu.VMEM)
    if not INTERPRET:
        spaces = [pltpu.HBM] * outside + [pltpu.VMEM] * (len(args) - outside)
        args = [pltpu.with_memory_space_constraint(x, s) for x, s in zip(args, spaces)]
    return pl.pallas_call(
        kernel,
        out_shape=out_shape,
        in_specs=[vmem] * len(args),
        out_specs=[vmem] * len(out_shape),
        scratch_shapes=scratch,
        compiler_params=pltpu.CompilerParams(vmem_limit_bytes=24 * 1024 * 1024),
        interpret=INTERPRET,
    )(*args)


def shape_of(*dims, dtype=f32):
    if INTERPRET:
        return jax.ShapeDtypeStruct(dims, dtype)
    return pltpu.VMEM(dims, dtype)


def toeplitz(w_ref, t_ref):
    spread = (iota((C, KT), 1) // H == iota((C, KT), 0)).astype(bf16)
    wide = lax.dot_general(
        w_ref[...], spread, (((0,), (0,)), ((), ())), preferred_element_type=f32
    )
    away = iota((R, KT), 1) % H - (iota((R, KT), 0) - 4)
    for ox in range(3):
        for oz in range(3):
            block = jnp.zeros((R, KT), f32)
            for oy in range(3):
                t = 9 * ox + 3 * oy + oz
                block = jnp.where(away == oy - 1, wide[t : t + 1, :], block)
            t_ref[(3 * ox + oz) * R : (3 * ox + oz + 1) * R, :] = block


def is_edge(axis, last):
    return lax.axis_index(axis) == (lax.axis_size(axis) - 1 if last else 0)


def by_parity(axis, body):
    even = lax.axis_index(axis) % 2 == 0
    pl.when(even)(lambda: body(True))
    pl.when(jnp.logical_not(even))(lambda: body(False))


def conv_kernel(
    ids_ref, w_ref, f_ref, load_ref, fixed_ref,
    q_ref, qone_ref, qtwo_ref, l_ref, yone_ref, ytwo_ref, tout_ref, t_ref, acc_ref,
):
    q_ref[...] = jnp.where(fixed_ref[...] != 0, held, load_ref[...])

    def send_length(even):
        up_ref, down_ref = (qone_ref, qtwo_ref) if even else (qtwo_ref, qone_ref)
        up_ref[...] = q_ref[:, D - 3 : D]
        down_ref[...] = q_ref[:, 0:3]

    by_parity("slab", send_length)
    toeplitz(w_ref, t_ref)
    table = t_ref[...].astype(bf16)
    tout_ref[...] = table
    acc_ref[...] = jnp.zeros_like(acc_ref)
    for xin in range(D):
        product = jnp.dot(table, f_ref[:, xin].reshape(KT, Z), preferred_element_type=f32)
        for ox in range(3):
            for oz in range(3):
                q = 3 * ox + oz
                acc_ref[oz, xin - (ox - 1) + 1] += product[q * R : (q + 1) * R, :]
    ids = jnp.broadcast_to(ids_ref[...], (R, 256))
    row = iota((R, 256), 0) - 4
    own = (row >= 0) & (row < H)
    pick_y = ((ids >> 6) == (row >> 2)) & own
    ids = jnp.broadcast_to(ids_ref[...], (Z, 256))
    pick_z = (ids >= 0) & ((ids & 63) == (iota((Z, 256), 0) >> 2))
    live = lax.dot_general(
        pick_y.astype(f32).astype(bf16),
        pick_z.astype(f32).astype(bf16),
        (((1,), (1,)), ((), ())),
        preferred_element_type=f32,
    )
    lane = iota((R, Z), 1)
    row = iota((R, Z), 0) - 4
    last_y = jnp.where(is_edge("cross", True), H - 1, H)
    killed = own & ((live < 0.5) | (lane == Z - 1) | (row >= last_y))
    for x in range(D + 2):
        behind = jnp.where(lane > 0, pltpu.roll(acc_ref[0, x], 1, 1), 0.0)
        ahead = jnp.where(lane < Z - 1, pltpu.roll(acc_ref[2, x], Z - 1, 1), 0.0)
        logit = acc_ref[1, x] + behind + ahead
        if 1 <= x <= D:
            gone = killed
            if x == D:
                gone = gone | (own & is_edge("slab", True))
            logit = jnp.where(gone, dead, logit)
        l_ref[x] = logit

    def send_section(even):
        up_ref, down_ref = (yone_ref, ytwo_ref) if even else (ytwo_ref, yone_ref)
        for k in range(3):
            for x in range(D):
                up_ref[4 * k + x] = q_ref[k, x, H - 4 : H, :]
                down_ref[4 * k + x] = q_ref[k, x, 0:4, :]
        for x in range(D + 2):
            up_ref[12 + x] = l_ref[x, 33:37, :]
            down_ref[12 + x] = l_ref[x, 3:7, :]

    by_parity("cross", send_section)


def pack_kernel(l_ref, yone_ref, ytwo_ref, l2_ref, ylo_ref, yhi_ref, one_ref, two_ref):
    l2_ref[...] = l_ref[...]

    def receive(even):
        ylo_ref[...] = ytwo_ref[...] if even else yone_ref[...]
        yhi_ref[...] = yone_ref[...] if even else ytwo_ref[...]

    by_parity("cross", receive)
    for x in range(D + 2):
        l2_ref[x, 1:5, :] += ylo_ref[12 + x]
        l2_ref[x, 35:39, :] += yhi_ref[12 + x]

    def send(even):
        up_ref, down_ref = (one_ref, two_ref) if even else (two_ref, one_ref)
        for x in range(3):
            up_ref[R * x : R * x + R, :] = l2_ref[x + 3]
            down_ref[R * x : R * x + R, :] = l2_ref[x]
        for k in range(3):
            for ref, first in ((up_ref, D - 3), (down_ref, 0)):
                for x in range(3):
                    at = 3 * R + 8 * (3 * k + x)
                    ref[at : at + 4, :] = ylo_ref[4 * k + first + x]
                    ref[at + 4 : at + 8, :] = yhi_ref[4 * k + first + x]

    by_parity("slab", send)


def section_sums(v_ref, x, tile):
    rows, below, half = tile
    lanes, others = pl.ds(128 * half, 128), pl.ds(128 - 128 * half, 128)
    last_lane = iota((8, 128), 1) == 127
    last_row = iota((8, 128), 0) == 7
    out = []
    for k in range(3):
        pair = []
        for where in (rows, below):
            v = v_ref[k, x, where, lanes]
            wrapped = pltpu.roll(v_ref[k, x, where, others], 127, 1)
            z = jnp.where(last_lane, wrapped, pltpu.roll(v, 127, 1))
            pair.append((v + z, z - v))
        (s, d), (s1, d1) = pair
        sy = jnp.where(last_row, pltpu.roll(s1, 7, 0), pltpu.roll(s, 7, 0))
        dy = jnp.where(last_row, pltpu.roll(d1, 7, 0), pltpu.roll(d, 7, 0))
        out += [s + sy, sy - s, d + dy, dy - d]
    return out


def along_x(low, high):
    a = {}
    for k in range(3):
        for f in range(4):
            v0, v1 = low[4 * k + f], high[4 * k + f]
            if f:
                a[0, f, k] = v0 + v1
            a[1, f, k] = v1 - v0
    return a


def hooke(a, s):
    def scaled(value):
        return value if s is None else s * value

    lam, two_mu, mu = scaled(lame / 16), scaled(shear / 8), scaled(shear / 16)
    lam3, mu3, last = scaled(lame / 48), scaled(shear / 48), scaled((lame + 4 * shear) / 144)
    x, y, z = 0, 1, 2
    out = {}
    n = ((1, 0, x), (0, 1, y), (0, 2, z))
    trace = lam * (a[n[0]] + a[n[1]] + a[n[2]])
    for m in n:
        out[m] = trace + two_mu * a[m]
    for m, o in (((0, 1, x), (1, 0, y)), ((0, 2, x), (1, 0, z)), ((0, 2, y), (0, 1, z))):
        out[m] = out[o] = mu * (a[m] + a[o])
    for m, o in (((1, 1, x), (0, 3, z)), ((1, 1, y), (1, 2, z)), ((1, 2, x), (0, 3, y))):
        both = lam3 * (a[m] + a[o])
        out[m] = both + mu * a[m]
        out[o] = both + mu * a[o]
    m = ((0, 3, x), (1, 2, y), (1, 1, z))
    three = a[m[0]] + a[m[1]] + a[m[2]]
    for o in m:
        out[o] = mu3 * (three + a[o])
    for k in range(3):
        out[1, 3, k] = last * a[1, 3, k]
    return out


def tiles(body):
    def step(j, carry):
        rows = pl.ds(pl.multiple_of(8 * j, 8), 8)
        below = pl.ds(pl.multiple_of(8 * lax.rem(j + 1, TILES), 8), 8)
        for half in range(2):
            body((rows, below, half))
        return carry

    lax.fori_loop(0, TILES, step, 0)


def stage_b(v_ref, s_ref, g_ref, first, last):
    def body(tile):
        rows, lanes = tile[0], pl.ds(128 * tile[2], 128)
        low = section_sums(v_ref, first, tile)
        carried = None
        for x in range(first, last + 1):
            high = section_sums(v_ref, x + 1, tile)
            force = hooke(along_x(low, high), s_ref[x, rows, lanes])
            kept = []
            for k in range(3):
                for f in range(4):
                    diff = force[1, f, k]
                    near = carried[4 * k + f] - diff if carried is not None else None
                    if f:
                        both = force[0, f, k]
                        near = near + both if carried is not None else None
                        kept.append(both + diff)
                    else:
                        kept.append(diff)
                    if carried is not None:
                        g_ref[4 * k + f, x, rows, lanes] = near
            carried = kept
            low = high

    tiles(body)


def stage_c(g_ref, v_ref, m_ref, out_ref, base, first, last):
    def plane(x, carry):
        for k in range(3):
            g = [g_ref[4 * k + f, x] for f in range(4)]
            s = (g[0] - g[1]) + pltpu.roll(g[0] + g[1], 1, 0)
            d = (g[2] - g[3]) + pltpu.roll(g[2] + g[3], 1, 0)
            out = (s - d) + pltpu.roll(s + d, 1, 1)
            out_ref[k, x - base] = m_ref[k, x] * out + (spring - shift) * v_ref[k, x]
        return carry

    lax.fori_loop(first, last + 1, plane, 0)


def energy_of(a):
    force = hooke(a, None)
    total = None
    for key in a:
        term = a[key] * force[key]
        total = term if total is None else total + term
    return total


def krylov_kernel(
    qone_ref, q_ref, qtwo_ref, l_ref, one_ref, two_ref, ylo_ref, yhi_ref,
    v0_ref, v1_ref, v2_ref, pone_ref, ptwo_ref, gain_ref, dots_ref,
    m_ref, s_ref, g_ref, acc_ref,
):
    for k in range(3):
        for x in range(D):
            v1_ref[k, x + 2, 0:4, :] = ylo_ref[4 * k + x]
            v1_ref[k, x + 2, 4 : 4 + H, :] = q_ref[k, x]
            v1_ref[k, x + 2, 4 + H :, :] = yhi_ref[4 * k + x]
    for x in range(1, 7):
        s_ref[x] = l_ref[x - 1]

    def receive(even):
        low = (two_ref, qtwo_ref) if even else (one_ref, qone_ref)
        high = (one_ref, qone_ref) if even else (two_ref, qtwo_ref)
        for k in range(3):
            for (ref, main), places in ((low, ((1, 0), (2, 1))), (high, ((0, 6), (1, 7), (2, 8)))):
                for source, x in places:
                    at = 3 * R + 8 * (3 * k + source)
                    v1_ref[k, x, 0:4, :] = ref[at : at + 4, :]
                    v1_ref[k, x, 4 : 4 + H, :] = main[k, source]
                    v1_ref[k, x, 4 + H :, :] = ref[at + 4 : at + 8, :]
        s_ref[0] = low[0][0:R, :]
        s_ref[7] = high[0][2 * R : 3 * R, :]
        for x in (1, 2):
            s_ref[x] += low[0][R * x : R * x + R, :]
        for x in (5, 6):
            s_ref[x] += high[0][R * (x - 5) : R * (x - 5) + R, :]

    by_parity("slab", receive)

    def split(x, carry):
        for k in range(3):
            v = v1_ref[k, x]
            fixed = v > 0.5 * held
            v0_ref[k, x] = jnp.where(fixed, 0.0, v)
            m_ref[k, x] = jnp.where(fixed, 0.0, 1.0)
        return carry

    lax.fori_loop(0, 9, split, 0)

    row = iota((R, Z), 0) - 4
    first_y = jnp.where(is_edge("cross", False), 0, -4)
    last_y = jnp.where(is_edge("cross", True), H - 1, R)
    outside_y = (row < first_y) | (row > last_y)
    for x in range(8):
        logit = s_ref[x]
        gone = (logit < 0.1 * dead) | outside_y
        if x < 2:
            gone = gone | is_edge("slab", False)
        if x > 5:
            gone = gone | is_edge("slab", True)
        density = 1.0 / (1.0 + jnp.exp(-logit))
        cube = density * density * density
        s_ref[x] = jnp.where(gone, 0.0, void_modulus + cube * (1.0 - void_modulus))
        if 1 <= x <= 6:
            factor = (-3.0 * (1.0 - void_modulus)) * cube * (1.0 - density)
            gain_ref[x - 1] = jnp.where(gone, 0.0, factor)

    stage_b(v0_ref, s_ref, g_ref, 0, 7)
    stage_c(g_ref, v0_ref, m_ref, v1_ref, 0, 1, 7)
    stage_b(v1_ref, s_ref, g_ref, 1, 6)
    stage_c(g_ref, v1_ref, m_ref, v2_ref, 0, 2, 6)

    def send(even):
        pone_ref[...] = v2_ref[:, 5 if even else 3]
        ptwo_ref[...] = v2_ref[:, 3 if even else 5]

    by_parity("slab", send)
    acc_ref[...] = jnp.zeros_like(acc_ref)

    def sums(tile):
        rows, lanes = tile[0], pl.ds(128 * tile[2], 128)
        row = iota((8, 128), 0) + rows.start
        own = (row >= 4) & (row < 4 + H)
        total = [jnp.zeros((8, 128), f32) for _ in range(6)]
        for x in range(2, 6):
            for k in range(3):
                v0 = v0_ref[k, x, rows, lanes]
                v1 = v1_ref[k, x, rows, lanes]
                v2 = v2_ref[k, x, rows, lanes]
                pairs = ((v0, v0), (v0, v1), (v1, v1), (v1, v2), (v2, v2))
                for i, (left, right) in enumerate(pairs):
                    total[i] = total[i] + left * right
        low = section_sums(v2_ref, 2, tile)
        for x in range(2, 6):
            high = section_sums(v2_ref, x + 1, tile)
            total[5] = total[5] + s_ref[x, rows, lanes] * energy_of(along_x(low, high))
            low = high
        total[5] = total[5] + spring * total[4]
        for i in range(6):
            acc_ref[i] += jnp.where(own, total[i], 0.0)

    tiles(sums)
    lane = iota((1, 128), 1)
    dots = jnp.zeros((1, 128), f32)
    for i in range(6):
        total = jnp.sum(jnp.sum(acc_ref[i], axis=0, keepdims=True), axis=1, keepdims=True)
        dots = jnp.where(lane == i, total, dots)
    dots_ref[...] = jnp.broadcast_to(dots[None], dots_ref.shape)


def coefficients(dots_ref):
    dots = jnp.sum(dots_ref[...], axis=0, keepdims=True)
    total = [jnp.broadcast_to(dots[:, i : i + 1], (8, 128)) for i in range(6)]
    d00, d01, d11, d12, d22, g22 = total
    d02 = d11
    g00 = d01 + shift * d00
    g01 = d02 + shift * d01
    g02 = d12 + shift * d02
    g11 = d12 + shift * d11
    g12 = d22 + shift * d12
    tiny = 4e-6

    def inverse(pivot, scale):
        fine = pivot > tiny * scale
        return jnp.where(fine, 1.0 / jnp.where(fine, pivot, 1.0), 0.0)

    i0 = 1.0 / g00
    l1, l2 = g01 * i0, g02 * i0
    i1 = inverse(g11 - l1 * g01, g11)
    m = g12 - l2 * g01
    l3 = m * i1
    i2 = inverse(g22 - l2 * g02 - l3 * m, g22)
    b0 = d00
    b1 = d01 - l1 * b0
    b2 = d02 - l2 * b0 - l3 * b1
    c2 = b2 * i2
    c1 = b1 * i1 - l3 * c2
    c0 = b0 * i0 - l1 * c1 - l2 * c2
    return [jnp.tile(c, (TILES, Z // 128)) for c in (c0, c1, c2)]


def adjoint_kernel(
    p0_ref, p1_ref, p2_ref, pone_ref, ptwo_ref, gain_ref, dots_ref, f_ref,
    disp_ref, shifted_ref, wpart_ref,
    u_ref, lg_ref, s32_ref,
):
    c0, c1, c2 = coefficients(dots_ref)

    def combine(x, third):
        for k in range(3):
            u_ref[k, x] = c0 * p0_ref[k, x + 1] + c1 * p1_ref[k, x + 1] + c2 * third(k)

    def inner(x, carry):
        combine(x, lambda k: p2_ref[k, x + 1])
        return carry

    def receive(even):
        combine(0, lambda k: (ptwo_ref if even else pone_ref)[k])
        combine(6, lambda k: (pone_ref if even else ptwo_ref)[k])

    lax.fori_loop(1, 6, inner, 0)
    by_parity("slab", receive)
    for k in range(3):
        for x in range(D):
            disp_ref[k, x] = u_ref[k, x + 1, 4 : 4 + H, :]

    def energies(tile):
        rows, lanes = tile[0], pl.ds(128 * tile[2], 128)
        low = section_sums(u_ref, 0, tile)
        for x in range(6):
            high = section_sums(u_ref, x + 1, tile)
            grad = gain_ref[x, rows, lanes] * energy_of(along_x(low, high))
            lg_ref[1, x, rows, lanes] = grad.astype(bf16).astype(f32)
            low = high

    tiles(energies)
    lane = iota((R, Z), 1)
    row = iota((R, Z), 0) - 4
    reach = (row >= -1) & (row <= H)
    for x in range(6):
        grad = jnp.where(reach, lg_ref[1, x], 0.0)
        lg_ref[1, x] = grad
        lg_ref[0, x] = jnp.where(lane < Z - 1, pltpu.roll(grad, Z - 1, 1), 0.0)
        lg_ref[2, x] = jnp.where(lane > 0, pltpu.roll(grad, 1, 1), 0.0)
    cross = jnp.zeros((NT, KT), f32)
    for x in range(D):
        for ox in range(3):
            for oz in range(3):
                q = 3 * ox + oz
                s32_ref[q * R : (q + 1) * R, :] = lg_ref[oz, x - (ox - 1) + 1]
        rows = s32_ref[...].astype(bf16)
        shifted_ref[x] = rows
        cross = cross + lax.dot_general(
            rows,
            f_ref[:, x].reshape(KT, Z),
            (((1,), (1,)), ((), ())),
            preferred_element_type=f32,
        )
    away = iota((R, KT), 1) % H - (iota((R, KT), 0) - 4)
    wide = [None] * 27
    for ox in range(3):
        for oz in range(3):
            q = 3 * ox + oz
            block = cross[q * R : (q + 1) * R, :]
            for oy in range(3):
                picked = jnp.where(away == oy - 1, block, 0.0)
                wide[9 * ox + 3 * oy + oz] = jnp.sum(picked, axis=0, keepdims=True)
    for t in range(27):
        s32_ref[t : t + 1, :] = wide[t][:, :Z]
        s32_ref[32 + t : 33 + t, :] = wide[t][:, Z:]
    s32_ref[27:32, :] = jnp.zeros((5, Z), f32)
    s32_ref[59:64, :] = jnp.zeros((5, Z), f32)
    value = s32_ref[0:64, :]
    terms = []
    for _ in range(3):
        terms.append(value.astype(bf16))
        value = value - terms[-1].astype(f32)
    terms = jnp.concatenate(terms, axis=0)
    gather = (iota((Z, 128), 0) // H == iota((Z, 128), 1)).astype(f32).astype(bf16)
    summed = jnp.dot(terms, gather, preferred_element_type=f32)
    summed = summed[0:64] + summed[64:128] + summed[128:192]
    narrow = summed[0:32, :] + pltpu.roll(summed[32:64, :], 8, 1)
    packed = narrow[0:4, :]
    for g in range(1, 8):
        packed = packed + pltpu.roll(narrow[4 * g : 4 * g + 4, :], C * g, 1)
    wpart_ref[...] = jnp.broadcast_to(packed[None], wpart_ref.shape)


def finish_kernel(parts_ref, out_ref):
    total = jnp.sum(parts_ref[...].reshape(parts_ref.shape[0] // 8, 8, 128), axis=0)
    total = total[0:4, :] + total[4:8, :]
    count = lax.axis_size("slab") * D * lax.axis_size("cross") * H * Z
    taps = [total[:, 0:C]]
    for g in range(1, 8):
        taps.append(pltpu.roll(total, 128 - C * g, 1)[:, 0:C])
    turned = jnp.concatenate(taps, axis=0).T
    out_ref[...] = turned[:, 0:27] * (1.0 / math.sqrt(count))


def feature_kernel(table_ref, shifted_ref, out_ref):
    turned = table_ref[...].astype(f32).T.astype(bf16)
    for x in range(D):
        product = jnp.dot(turned, shifted_ref[x], preferred_element_type=f32)
        out_ref[:, x] = product.astype(bf16).reshape(C, H, Z)


def share(x):
    return lax.all_to_all(x, ("slab", "cross"), 0, 0)


def on_device(load, fixed_dofs, features, conv_weight, active_bricks):
    def swap(x, axis, start):
        pairs = [(i, i + 1) for i in range(start, lax.axis_size(axis) - 1, 2)]
        return lax.ppermute(x, axis, pairs + [(j, i) for i, j in pairs])

    def exchange(first, second, axis):
        return swap(first, axis, 0), swap(second, axis, 1)

    devices = lax.axis_size(("slab", "cross"))
    ids = active_bricks.reshape(1, 256)
    rows = shape_of(12 + D + 2, 4, Z)
    logits = shape_of(D + 2, R, Z)
    part = shape_of(3, 3, H, Z)
    q, qone, qtwo, logit, yone, ytwo, table = call(
        conv_kernel,
        [shape_of(3, D, H, Z), part, part, logits, rows, rows, shape_of(NT, KT, dtype=bf16)],
        [pltpu.VMEM((NT, KT), f32), pltpu.VMEM((3, D + 2, R, Z), f32)],
        ids, conv_weight.T, features, load, fixed_dofs,
        outside=5,
    )
    yone, ytwo = exchange(yone, ytwo, "cross")
    qone, qtwo = exchange(qone, qtwo, "slab")
    wide = shape_of(3 * R + 72, Z)
    logit, ylo, yhi, xone, xtwo = call(
        pack_kernel, [logits, rows, rows, wide, wide], [], logit, yone, ytwo
    )
    xone, xtwo = exchange(xone, xtwo, "slab")
    field = shape_of(3, 9, R, Z)
    plane = shape_of(3, R, Z)
    p0, p1, p2, pone, ptwo, gain, dots = call(
        krylov_kernel,
        [field, field, field, plane, plane, logits, shape_of(devices, 1, 128)],
        [
            pltpu.VMEM((3, 9, R, Z), f32),
            pltpu.VMEM((8, R, Z), f32),
            pltpu.VMEM((12, 9, R, Z), f32),
            pltpu.VMEM((6, 8, 128), f32),
        ],
        qone, q, qtwo, logit, xone, xtwo, ylo, yhi,
    )
    dots = share(dots).reshape(devices, 128)
    pone, ptwo = exchange(pone, ptwo, "slab")
    displacement, shifted, wpart = call(
        adjoint_kernel,
        [shape_of(3, D, H, Z), shape_of(D, NT, Z, dtype=bf16), shape_of(devices, 4, 128)],
        [
            pltpu.VMEM((3, 7, R, Z), f32),
            pltpu.VMEM((3, 6, R, Z), f32),
            pltpu.VMEM((NT, Z), f32),
        ],
        p0, p1, p2, pone, ptwo, gain, dots, features,
    )
    parts = share(wpart).reshape(4 * devices, 128)
    (feature_grad,) = call(
        feature_kernel, [jax.ShapeDtypeStruct((C, D, H, Z), bf16)], [], table, shifted
    )
    (weight_grad,) = call(finish_kernel, [jax.ShapeDtypeStruct((C, 27), f32)], [], parts)
    return displacement, feature_grad, weight_grad.T


def sharded(mesh):
    in_specs = (
        P(None, "slab", "cross", None),
        P(None, "slab", "cross", None),
        P(None, "slab", "cross", None),
        P(),
        P("slab", "cross", None),
    )
    out_specs = (P(None, "slab", "cross", None), P(None, "slab", "cross", None), P())

    return jax.shard_map(
        on_device, mesh=mesh, in_specs=in_specs, out_specs=out_specs, check_vma=False
    )


def solution(mesh):
    return sharded(mesh)
```

```python
import math

import jax
import jax.numpy as jnp
from jax import lax
from jax.experimental import pallas as pl
from jax.experimental.pallas import tpu as pltpu
from jax.sharding import PartitionSpec as P


INTERPRET = False

void_modulus = 0.001
spring = 0.1
shift = 0.4
held = 64.0
dead = -1e30
poisson = 0.3
lame = poisson / ((1.0 + poisson) * (1.0 - 2.0 * poisson))
shear = 0.5 / (1.0 + poisson)

D, H, Z, C = 4, 32, 256, 16
R = 40
TILES = R // 8
KT = C * H
NT = 9 * R

f32 = jnp.float32
bf16 = jnp.bfloat16


def iota(shape, dim):
    return lax.broadcasted_iota(jnp.int32, shape, dim)


def call(kernel, out_shape, scratch, *args, outside=0, raw=()):
    vmem = pl.BlockSpec(memory_space=pltpu.VMEM)
    if not INTERPRET:
        spaces = [pltpu.HBM] * outside + [pltpu.VMEM] * (len(args) - outside)
        args = [pltpu.with_memory_space_constraint(x, s) for x, s in zip(args, spaces)]
    return pl.pallas_call(
        kernel,
        out_shape=out_shape,
        in_specs=[pl.BlockSpec(memory_space=pl.ANY) if i in raw else vmem for i in range(len(args))],
        out_specs=[vmem] * len(out_shape),
        scratch_shapes=scratch,
        compiler_params=pltpu.CompilerParams(vmem_limit_bytes=24 * 1024 * 1024),
        interpret=INTERPRET,
    )(*args)


def shape_of(*dims, dtype=f32):
    if INTERPRET:
        return jax.ShapeDtypeStruct(dims, dtype)
    return pltpu.VMEM(dims, dtype)


def toeplitz(w_ref, t_ref):
    spread = (iota((C, KT), 1) // H == iota((C, KT), 0)).astype(bf16)
    wide = lax.dot_general(
        w_ref[...], spread, (((0,), (0,)), ((), ())), preferred_element_type=f32
    )
    away = iota((R, KT), 1) % H - (iota((R, KT), 0) - 4)
    for ox in range(3):
        for oz in range(3):
            block = jnp.zeros((R, KT), f32)
            for oy in range(3):
                t = 9 * ox + 3 * oy + oz
                block = jnp.where(away == oy - 1, wide[t : t + 1, :], block)
            t_ref[(3 * ox + oz) * R : (3 * ox + oz + 1) * R, :] = block


def is_edge(axis, last):
    return lax.axis_index(axis) == (lax.axis_size(axis) - 1 if last else 0)


def by_parity(axis, body):
    even = lax.axis_index(axis) % 2 == 0
    pl.when(even)(lambda: body(True))
    pl.when(jnp.logical_not(even))(lambda: body(False))


def conv_kernel(
    ids_ref, w_ref, f_ref, load_ref, fixed_ref,
    q_ref, qone_ref, qtwo_ref, l_ref, yone_ref, ytwo_ref, tout_ref,
    t_ref, acc_ref, planes_ref, load_sem,
):
    loads = [
        pltpu.make_async_copy(f_ref.at[:, x], planes_ref.at[x], load_sem.at[x]) for x in range(D)
    ]
    for load in loads:
        load.start()
    q_ref[...] = jnp.where(fixed_ref[...] != 0, held, load_ref[...])

    def send_length(even):
        up_ref, down_ref = (qone_ref, qtwo_ref) if even else (qtwo_ref, qone_ref)
        up_ref[...] = q_ref[:, D - 3 : D]
        down_ref[...] = q_ref[:, 0:3]

    by_parity("slab", send_length)
    toeplitz(w_ref, t_ref)
    table = t_ref[...].astype(bf16)
    tout_ref[...] = table
    acc_ref[...] = jnp.zeros_like(acc_ref)
    for xin in range(D):
        loads[xin].wait()
        product = jnp.dot(table, planes_ref[xin].reshape(KT, Z), preferred_element_type=f32)
        for ox in range(3):
            for oz in range(3):
                q = 3 * ox + oz
                acc_ref[oz, xin - (ox - 1) + 1] += product[q * R : (q + 1) * R, :]
    ids = jnp.broadcast_to(ids_ref[...], (R, 256))
    row = iota((R, 256), 0) - 4
    own = (row >= 0) & (row < H)
    pick_y = ((ids >> 6) == (row >> 2)) & own
    ids = jnp.broadcast_to(ids_ref[...], (Z, 256))
    pick_z = (ids >= 0) & ((ids & 63) == (iota((Z, 256), 0) >> 2))
    live = lax.dot_general(
        pick_y.astype(f32).astype(bf16),
        pick_z.astype(f32).astype(bf16),
        (((1,), (1,)), ((), ())),
        preferred_element_type=f32,
    )
    lane = iota((R, Z), 1)
    row = iota((R, Z), 0) - 4
    last_y = jnp.where(is_edge("cross", True), H - 1, H)
    killed = own & ((live < 0.5) | (lane == Z - 1) | (row >= last_y))
    for x in range(D + 2):
        behind = jnp.where(lane > 0, pltpu.roll(acc_ref[0, x], 1, 1), 0.0)
        ahead = jnp.where(lane < Z - 1, pltpu.roll(acc_ref[2, x], Z - 1, 1), 0.0)
        logit = acc_ref[1, x] + behind + ahead
        if 1 <= x <= D:
            gone = killed
            if x == D:
                gone = gone | (own & is_edge("slab", True))
            logit = jnp.where(gone, dead, logit)
        l_ref[x] = logit

    def send_section(even):
        up_ref, down_ref = (yone_ref, ytwo_ref) if even else (ytwo_ref, yone_ref)
        for k in range(3):
            for x in range(D):
                up_ref[4 * k + x] = q_ref[k, x, H - 4 : H, :]
                down_ref[4 * k + x] = q_ref[k, x, 0:4, :]
        for x in range(D + 2):
            up_ref[12 + x] = l_ref[x, 33:37, :]
            down_ref[12 + x] = l_ref[x, 3:7, :]

    by_parity("cross", send_section)


def pack_kernel(l_ref, yone_ref, ytwo_ref, l2_ref, ylo_ref, yhi_ref, one_ref, two_ref):
    l2_ref[...] = l_ref[...]

    def receive(even):
        ylo_ref[...] = ytwo_ref[...] if even else yone_ref[...]
        yhi_ref[...] = yone_ref[...] if even else ytwo_ref[...]

    by_parity("cross", receive)
    for x in range(D + 2):
        l2_ref[x, 1:5, :] += ylo_ref[12 + x]
        l2_ref[x, 35:39, :] += yhi_ref[12 + x]

    def send(even):
        up_ref, down_ref = (one_ref, two_ref) if even else (two_ref, one_ref)
        for x in range(3):
            up_ref[R * x : R * x + R, :] = l2_ref[x + 3]
            down_ref[R * x : R * x + R, :] = l2_ref[x]
        for k in range(3):
            for ref, first in ((up_ref, D - 3), (down_ref, 0)):
                for x in range(3):
                    at = 3 * R + 8 * (3 * k + x)
                    ref[at : at + 4, :] = ylo_ref[4 * k + first + x]
                    ref[at + 4 : at + 8, :] = yhi_ref[4 * k + first + x]

    by_parity("slab", send)


def section_sums(v_ref, x, tile):
    rows, half, below = tile
    lanes, others = pl.ds(128 * half, 128), pl.ds(128 - 128 * half, 128)
    last_lane = iota((8, 128), 1) == 127
    last_row = iota((8, 128), 0) == 7
    out = []
    for k in range(3):
        v = v_ref[k, x, rows, lanes]
        wrapped = pltpu.roll(v_ref[k, x, rows, others], 127, 1)
        z = jnp.where(last_lane, wrapped, pltpu.roll(v, 127, 1))
        for i, w in enumerate((v + z, z - v)):
            turned = pltpu.roll(w, 7, 0)
            y = jnp.where(last_row, below[half, x, 2 * k + i], turned)
            below[half, x, 2 * k + i] = turned
            out += [w + y, y - w]
    return out


def along_x(low, high):
    a = {}
    for k in range(3):
        for f in range(4):
            v0, v1 = low[4 * k + f], high[4 * k + f]
            if f:
                a[0, f, k] = v0 + v1
            a[1, f, k] = v1 - v0
    return a


def hooke(a, s):
    def scaled(value):
        return value if s is None else s * value

    lam, two_mu, mu = scaled(lame / 16), scaled(shear / 8), scaled(shear / 16)
    lam3, mu3, last = scaled(lame / 48), scaled(shear / 48), scaled((lame + 4 * shear) / 144)
    x, y, z = 0, 1, 2
    out = {}
    n = ((1, 0, x), (0, 1, y), (0, 2, z))
    trace = lam * (a[n[0]] + a[n[1]] + a[n[2]])
    for m in n:
        out[m] = trace + two_mu * a[m]
    for m, o in (((0, 1, x), (1, 0, y)), ((0, 2, x), (1, 0, z)), ((0, 2, y), (0, 1, z))):
        out[m] = out[o] = mu * (a[m] + a[o])
    for m, o in (((1, 1, x), (0, 3, z)), ((1, 1, y), (1, 2, z)), ((1, 2, x), (0, 3, y))):
        both = lam3 * (a[m] + a[o])
        out[m] = both + mu * a[m]
        out[o] = both + mu * a[o]
    m = ((0, 3, x), (1, 2, y), (1, 1, z))
    three = a[m[0]] + a[m[1]] + a[m[2]]
    for o in m:
        out[o] = mu3 * (three + a[o])
    for k in range(3):
        out[1, 3, k] = last * a[1, 3, k]
    return out


def tiles(body, below):
    def step(i, carry):
        rows = pl.ds(pl.multiple_of(8 * (TILES - 1 - i), 8), 8)
        for half in range(2):
            body((rows, half, below))
        return carry

    lax.fori_loop(0, TILES, step, 0)


def stage_b(v_ref, s_ref, g_ref, below, first, last):
    def body(tile):
        rows, lanes = tile[0], pl.ds(128 * tile[1], 128)
        low = section_sums(v_ref, first, tile)
        carried = None
        for x in range(first, last + 1):
            high = section_sums(v_ref, x + 1, tile)
            force = hooke(along_x(low, high), s_ref[x, rows, lanes])
            kept = []
            for k in range(3):
                for f in range(4):
                    diff = force[1, f, k]
                    near = carried[4 * k + f] - diff if carried is not None else None
                    if f:
                        both = force[0, f, k]
                        near = near + both if carried is not None else None
                        kept.append(both + diff)
                    else:
                        kept.append(diff)
                    if carried is not None:
                        g_ref[4 * k + f, x, rows, lanes] = near
            carried = kept
            low = high

    tiles(body, below)


def stage_c(g_ref, v_ref, m_ref, out_ref, base, first, last):
    def plane(x, carry):
        for k in range(3):
            g = [g_ref[4 * k + f, x] for f in range(4)]
            s = (g[0] - g[1]) + pltpu.roll(g[0] + g[1], 1, 0)
            d = (g[2] - g[3]) + pltpu.roll(g[2] + g[3], 1, 0)
            out = (s - d) + pltpu.roll(s + d, 1, 1)
            out_ref[k, x - base] = m_ref[k, x] * out + (spring - shift) * v_ref[k, x]
        return carry

    lax.fori_loop(first, last + 1, plane, 0)


def energy_of(a):
    force = hooke(a, None)
    total = None
    for key in a:
        term = a[key] * force[key]
        total = term if total is None else total + term
    return total


def krylov_kernel(
    qone_ref, q_ref, qtwo_ref, l_ref, one_ref, two_ref, ylo_ref, yhi_ref,
    v0_ref, v1_ref, v2_ref, pone_ref, ptwo_ref, gain_ref, dots_ref,
    m_ref, s_ref, g_ref, acc_ref, below,
):
    for k in range(3):
        for x in range(D):
            v1_ref[k, x + 2, 0:4, :] = ylo_ref[4 * k + x]
            v1_ref[k, x + 2, 4 : 4 + H, :] = q_ref[k, x]
            v1_ref[k, x + 2, 4 + H :, :] = yhi_ref[4 * k + x]
    for x in range(1, 7):
        s_ref[x] = l_ref[x - 1]

    def receive(even):
        low = (two_ref, qtwo_ref) if even else (one_ref, qone_ref)
        high = (one_ref, qone_ref) if even else (two_ref, qtwo_ref)
        for k in range(3):
            for (ref, main), places in ((low, ((1, 0), (2, 1))), (high, ((0, 6), (1, 7), (2, 8)))):
                for source, x in places:
                    at = 3 * R + 8 * (3 * k + source)
                    v1_ref[k, x, 0:4, :] = ref[at : at + 4, :]
                    v1_ref[k, x, 4 : 4 + H, :] = main[k, source]
                    v1_ref[k, x, 4 + H :, :] = ref[at + 4 : at + 8, :]
        s_ref[0] = low[0][0:R, :]
        s_ref[7] = high[0][2 * R : 3 * R, :]
        for x in (1, 2):
            s_ref[x] += low[0][R * x : R * x + R, :]
        for x in (5, 6):
            s_ref[x] += high[0][R * (x - 5) : R * (x - 5) + R, :]

    by_parity("slab", receive)

    def split(x, carry):
        for k in range(3):
            v = v1_ref[k, x]
            fixed = v > 0.5 * held
            v0_ref[k, x] = jnp.where(fixed, 0.0, v)
            m_ref[k, x] = jnp.where(fixed, 0.0, 1.0)
        return carry

    lax.fori_loop(0, 9, split, 0)

    row = iota((R, Z), 0) - 4
    first_y = jnp.where(is_edge("cross", False), 0, -4)
    last_y = jnp.where(is_edge("cross", True), H - 1, R)
    outside_y = (row < first_y) | (row > last_y)
    for x in range(8):
        logit = s_ref[x]
        gone = (logit < 0.1 * dead) | outside_y
        if x < 2:
            gone = gone | is_edge("slab", False)
        if x > 5:
            gone = gone | is_edge("slab", True)
        density = 1.0 / (1.0 + jnp.exp(-logit))
        cube = density * density * density
        s_ref[x] = jnp.where(gone, 0.0, void_modulus + cube * (1.0 - void_modulus))
        if 1 <= x <= 6:
            factor = (-3.0 * (1.0 - void_modulus)) * cube * (1.0 - density)
            gain_ref[x - 1] = jnp.where(gone, 0.0, factor)

    below[...] = jnp.zeros_like(below)
    stage_b(v0_ref, s_ref, g_ref, below, 0, 7)
    stage_c(g_ref, v0_ref, m_ref, v1_ref, 0, 1, 7)
    stage_b(v1_ref, s_ref, g_ref, below, 1, 6)
    stage_c(g_ref, v1_ref, m_ref, v2_ref, 0, 2, 6)

    def send(even):
        pone_ref[...] = v2_ref[:, 5 if even else 3]
        ptwo_ref[...] = v2_ref[:, 3 if even else 5]

    by_parity("slab", send)
    acc_ref[...] = jnp.zeros_like(acc_ref)

    def sums(tile):
        rows, lanes = tile[0], pl.ds(128 * tile[1], 128)
        row = iota((8, 128), 0) + rows.start
        own = (row >= 4) & (row < 4 + H)
        total = [jnp.zeros((8, 128), f32) for _ in range(6)]
        for x in range(2, 6):
            for k in range(3):
                v0 = v0_ref[k, x, rows, lanes]
                v1 = v1_ref[k, x, rows, lanes]
                v2 = v2_ref[k, x, rows, lanes]
                pairs = ((v0, v0), (v0, v1), (v1, v1), (v1, v2), (v2, v2))
                for i, (left, right) in enumerate(pairs):
                    total[i] = total[i] + left * right
        low = section_sums(v2_ref, 2, tile)
        for x in range(2, 6):
            high = section_sums(v2_ref, x + 1, tile)
            total[5] = total[5] + s_ref[x, rows, lanes] * energy_of(along_x(low, high))
            low = high
        total[5] = total[5] + spring * total[4]
        for i in range(6):
            acc_ref[i] += jnp.where(own, total[i], 0.0)

    tiles(sums, below)
    lane = iota((1, 128), 1)
    dots = jnp.zeros((1, 128), f32)
    for i in range(6):
        total = jnp.sum(jnp.sum(acc_ref[i], axis=0, keepdims=True), axis=1, keepdims=True)
        dots = jnp.where(lane == i, total, dots)
    dots_ref[...] = jnp.broadcast_to(dots, dots_ref.shape)


def coefficients(dots_ref):
    dots = jnp.sum(dots_ref[...], axis=0, keepdims=True)
    total = [jnp.broadcast_to(dots[:, i : i + 1], (8, 128)) for i in range(6)]
    d00, d01, d11, d12, d22, g22 = total
    d02 = d11
    g00 = d01 + shift * d00
    g01 = d02 + shift * d01
    g02 = d12 + shift * d02
    g11 = d12 + shift * d11
    g12 = d22 + shift * d12
    tiny = 4e-6

    def inverse(pivot, scale):
        fine = pivot > tiny * scale
        return jnp.where(fine, 1.0 / jnp.where(fine, pivot, 1.0), 0.0)

    i0 = 1.0 / g00
    l1, l2 = g01 * i0, g02 * i0
    i1 = inverse(g11 - l1 * g01, g11)
    m = g12 - l2 * g01
    l3 = m * i1
    i2 = inverse(g22 - l2 * g02 - l3 * m, g22)
    b0 = d00
    b1 = d01 - l1 * b0
    b2 = d02 - l2 * b0 - l3 * b1
    c2 = b2 * i2
    c1 = b1 * i1 - l3 * c2
    c0 = b0 * i0 - l1 * c1 - l2 * c2
    return [jnp.tile(c, (TILES, Z // 128)) for c in (c0, c1, c2)]


def adjoint_kernel(
    p0_ref, p1_ref, p2_ref, pone_ref, ptwo_ref, gain_ref, dots_ref, f_ref,
    disp_ref, shifted_ref, wpart_ref,
    u_ref, lg_ref, s32_ref, below,
):
    c0, c1, c2 = coefficients(dots_ref)

    def combine(x, third):
        for k in range(3):
            u_ref[k, x] = c0 * p0_ref[k, x + 1] + c1 * p1_ref[k, x + 1] + c2 * third(k)

    def inner(x, carry):
        combine(x, lambda k: p2_ref[k, x + 1])
        return carry

    def receive(even):
        combine(0, lambda k: (ptwo_ref if even else pone_ref)[k])
        combine(6, lambda k: (pone_ref if even else ptwo_ref)[k])

    lax.fori_loop(1, 6, inner, 0)
    by_parity("slab", receive)
    for k in range(3):
        for x in range(D):
            disp_ref[k, x] = u_ref[k, x + 1, 4 : 4 + H, :]

    def energies(tile):
        rows, lanes = tile[0], pl.ds(128 * tile[1], 128)
        low = section_sums(u_ref, 0, tile)
        for x in range(6):
            high = section_sums(u_ref, x + 1, tile)
            grad = gain_ref[x, rows, lanes] * energy_of(along_x(low, high))
            lg_ref[1, x, rows, lanes] = grad.astype(bf16).astype(f32)
            low = high

    below[...] = jnp.zeros_like(below)
    tiles(energies, below)
    lane = iota((R, Z), 1)
    row = iota((R, Z), 0) - 4
    reach = (row >= -1) & (row <= H)
    for x in range(6):
        grad = jnp.where(reach, lg_ref[1, x], 0.0)
        lg_ref[1, x] = grad
        lg_ref[0, x] = jnp.where(lane < Z - 1, pltpu.roll(grad, Z - 1, 1), 0.0)
        lg_ref[2, x] = jnp.where(lane > 0, pltpu.roll(grad, 1, 1), 0.0)
    cross = jnp.zeros((NT, KT), f32)
    for x in range(D):
        for ox in range(3):
            for oz in range(3):
                q = 3 * ox + oz
                s32_ref[q * R : (q + 1) * R, :] = lg_ref[oz, x - (ox - 1) + 1]
        rows = s32_ref[...].astype(bf16)
        shifted_ref[x] = rows
        cross = cross + lax.dot_general(
            rows,
            f_ref[:, x].reshape(KT, Z),
            (((1,), (1,)), ((), ())),
            preferred_element_type=f32,
        )
    away = iota((R, KT), 1) % H - (iota((R, KT), 0) - 4)
    wide = [None] * 27
    for ox in range(3):
        for oz in range(3):
            q = 3 * ox + oz
            block = cross[q * R : (q + 1) * R, :]
            for oy in range(3):
                picked = jnp.where(away == oy - 1, block, 0.0)
                wide[9 * ox + 3 * oy + oz] = jnp.sum(picked, axis=0, keepdims=True)
    for t in range(27):
        s32_ref[t : t + 1, :] = wide[t][:, :Z]
        s32_ref[32 + t : 33 + t, :] = wide[t][:, Z:]
    s32_ref[27:32, :] = jnp.zeros((5, Z), f32)
    s32_ref[59:64, :] = jnp.zeros((5, Z), f32)
    value = s32_ref[0:64, :]
    terms = []
    for _ in range(3):
        terms.append(value.astype(bf16))
        value = value - terms[-1].astype(f32)
    terms = jnp.concatenate(terms, axis=0)
    gather = (iota((Z, 128), 0) // H == iota((Z, 128), 1)).astype(f32).astype(bf16)
    summed = jnp.dot(terms, gather, preferred_element_type=f32)
    summed = summed[0:64] + summed[64:128] + summed[128:192]
    narrow = summed[0:32, :] + pltpu.roll(summed[32:64, :], 8, 1)
    packed = narrow[0:4, :]
    for g in range(1, 8):
        packed = packed + pltpu.roll(narrow[4 * g : 4 * g + 4, :], C * g, 1)
    twice = jnp.concatenate([packed, packed], axis=0)
    wpart_ref[...] = jnp.broadcast_to(twice[None], wpart_ref.shape)


def finish_kernel(parts_ref, out_ref):
    total = jnp.sum(parts_ref[...].reshape(parts_ref.shape[0] // 8, 8, 128), axis=0)
    total = total[0:4, :] + total[4:8, :]
    count = lax.axis_size("slab") * D * lax.axis_size("cross") * H * Z
    taps = [total[:, 0:C]]
    for g in range(1, 8):
        taps.append(pltpu.roll(total, 128 - C * g, 1)[:, 0:C])
    turned = jnp.concatenate(taps, axis=0).T
    out_ref[...] = turned[:, 0:27] * (1.0 / math.sqrt(count))


def feature_kernel(table_ref, shifted_ref, out_ref):
    turned = table_ref[...].astype(f32).T.astype(bf16)
    for x in range(D):
        product = jnp.dot(turned, shifted_ref[x], preferred_element_type=f32)
        out_ref[:, x] = product.astype(bf16).reshape(C, H, Z)


def share(x):
    return lax.all_to_all(x, ("slab", "cross"), 0, 0)


def on_device(load, fixed_dofs, features, conv_weight, active_bricks):
    def swap(x, axis, start):
        pairs = [(i, i + 1) for i in range(start, lax.axis_size(axis) - 1, 2)]
        return lax.ppermute(x, axis, pairs + [(j, i) for i, j in pairs])

    def exchange(first, second, axis):
        return swap(first, axis, 0), swap(second, axis, 1)

    devices = lax.axis_size(("slab", "cross"))
    ids = active_bricks.reshape(1, 256)
    rows = shape_of(12 + D + 2, 4, Z)
    logits = shape_of(D + 2, R, Z)
    part = shape_of(3, 3, H, Z)
    q, qone, qtwo, logit, yone, ytwo, table = call(
        conv_kernel,
        [shape_of(3, D, H, Z), part, part, logits, rows, rows, shape_of(NT, KT, dtype=bf16)],
        [
            pltpu.VMEM((NT, KT), f32),
            pltpu.VMEM((3, D + 2, R, Z), f32),
            pltpu.VMEM((D, C, H, Z), bf16),
            pltpu.SemaphoreType.DMA((D,)),
        ],
        ids, conv_weight.T, features, load, fixed_dofs,
        outside=5,
        raw=(2,),
    )
    yone, ytwo = exchange(yone, ytwo, "cross")
    qone, qtwo = exchange(qone, qtwo, "slab")
    wide = shape_of(3 * R + 72, Z)
    logit, ylo, yhi, xone, xtwo = call(
        pack_kernel, [logits, rows, rows, wide, wide], [], logit, yone, ytwo
    )
    xone, xtwo = exchange(xone, xtwo, "slab")
    field = shape_of(3, 9, R, Z)
    plane = shape_of(3, R, Z)
    p0, p1, p2, pone, ptwo, gain, dots = call(
        krylov_kernel,
        [field, field, field, plane, plane, logits, shape_of(devices, 128)],
        [
            pltpu.VMEM((3, 9, R, Z), f32),
            pltpu.VMEM((8, R, Z), f32),
            pltpu.VMEM((12, 9, R, Z), f32),
            pltpu.VMEM((6, 8, 128), f32),
            pltpu.VMEM((2, 9, 6, 8, 128), f32),
        ],
        qone, q, qtwo, logit, xone, xtwo, ylo, yhi,
    )
    dots = share(dots.reshape(devices, 1, 128)).reshape(devices, 128)
    pone, ptwo = exchange(pone, ptwo, "slab")
    displacement, shifted, wpart = call(
        adjoint_kernel,
        [shape_of(3, D, H, Z), shape_of(D, NT, Z, dtype=bf16), shape_of(devices // 2, 8, 128)],
        [
            pltpu.VMEM((3, 7, R, Z), f32),
            pltpu.VMEM((3, 6, R, Z), f32),
            pltpu.VMEM((NT, Z), f32),
            pltpu.VMEM((2, 7, 6, 8, 128), f32),
        ],
        p0, p1, p2, pone, ptwo, gain, dots, features,
    )
    parts = share(wpart.reshape(devices, 4, 128)).reshape(4 * devices, 128)
    (feature_grad,) = call(
        feature_kernel, [jax.ShapeDtypeStruct((C, D, H, Z), bf16)], [], table, shifted
    )
    (weight_grad,) = call(finish_kernel, [jax.ShapeDtypeStruct((C, 27), f32)], [], parts)
    return displacement, feature_grad, weight_grad.T


def sharded(mesh):
    in_specs = (
        P(None, "slab", "cross", None),
        P(None, "slab", "cross", None),
        P(None, "slab", "cross", None),
        P(),
        P("slab", "cross", None),
    )
    out_specs = (P(None, "slab", "cross", None), P(None, "slab", "cross", None), P())

    return jax.shard_map(
        on_device, mesh=mesh, in_specs=in_specs, out_specs=out_specs, check_vma=False
    )


def solution(mesh):
    return sharded(mesh)
```

```python
import math

import jax
import jax.numpy as jnp
from jax import lax
from jax.experimental import pallas as pl
from jax.experimental.pallas import tpu as pltpu
from jax.sharding import PartitionSpec as P


INTERPRET = False

void_modulus = 0.001
spring = 0.1
shift = 0.4
held = 64.0
dead = -1e30
poisson = 0.3
lame = poisson / ((1.0 + poisson) * (1.0 - 2.0 * poisson))
shear = 0.5 / (1.0 + poisson)

D, H, Z, C = 4, 32, 256, 16
R = 40
TILES = R // 8
KT = C * H
NT = 9 * R

f32 = jnp.float32
bf16 = jnp.bfloat16


def iota(shape, dim):
    return lax.broadcasted_iota(jnp.int32, shape, dim)


def call(kernel, out_shape, scratch, *args, outside=0):
    vmem = pl.BlockSpec(memory_space=pltpu.VMEM)
    if not INTERPRET:
        spaces = [pltpu.HBM] * outside + [pltpu.VMEM] * (len(args) - outside)
        args = [pltpu.with_memory_space_constraint(x, s) for x, s in zip(args, spaces)]
    return pl.pallas_call(
        kernel,
        out_shape=out_shape,
        in_specs=[vmem] * len(args),
        out_specs=[vmem] * len(out_shape),
        scratch_shapes=scratch,
        compiler_params=pltpu.CompilerParams(vmem_limit_bytes=24 * 1024 * 1024),
        interpret=INTERPRET,
    )(*args)


def shape_of(*dims, dtype=f32):
    if INTERPRET:
        return jax.ShapeDtypeStruct(dims, dtype)
    return pltpu.VMEM(dims, dtype)


def toeplitz(w_ref, t_ref):
    spread = (iota((C, KT), 1) // H == iota((C, KT), 0)).astype(bf16)
    wide = lax.dot_general(
        w_ref[...], spread, (((0,), (0,)), ((), ())), preferred_element_type=f32
    )
    away = iota((R, KT), 1) % H - (iota((R, KT), 0) - 4)
    for ox in range(3):
        for oz in range(3):
            block = jnp.zeros((R, KT), f32)
            for oy in range(3):
                t = 9 * ox + 3 * oy + oz
                block = jnp.where(away == oy - 1, wide[t : t + 1, :], block)
            t_ref[(3 * ox + oz) * R : (3 * ox + oz + 1) * R, :] = block


def is_edge(axis, last):
    return lax.axis_index(axis) == (lax.axis_size(axis) - 1 if last else 0)


def by_parity(axis, body):
    even = lax.axis_index(axis) % 2 == 0
    pl.when(even)(lambda: body(True))
    pl.when(jnp.logical_not(even))(lambda: body(False))


def conv_kernel(
    ids_ref, w_ref, f_ref, load_ref, fixed_ref,
    q_ref, qone_ref, qtwo_ref, l_ref, yone_ref, ytwo_ref, tout_ref,
    t_ref, acc_ref,
):
    q_ref[...] = jnp.where(fixed_ref[...] != 0, held, load_ref[...])

    def send_length(even):
        up_ref, down_ref = (qone_ref, qtwo_ref) if even else (qtwo_ref, qone_ref)
        up_ref[...] = q_ref[:, D - 3 : D]
        down_ref[...] = q_ref[:, 0:3]

    by_parity("slab", send_length)
    toeplitz(w_ref, t_ref)
    table = t_ref[...].astype(bf16)
    tout_ref[...] = table
    acc_ref[...] = jnp.zeros_like(acc_ref)
    for xin in range(D):
        product = jnp.dot(table, f_ref[:, xin].reshape(KT, Z), preferred_element_type=f32)
        for ox in range(3):
            for oz in range(3):
                q = 3 * ox + oz
                acc_ref[oz, xin - (ox - 1) + 1] += product[q * R : (q + 1) * R, :]
    ids = jnp.broadcast_to(ids_ref[...], (R, 256))
    row = iota((R, 256), 0) - 4
    own = (row >= 0) & (row < H)
    pick_y = ((ids >> 6) == (row >> 2)) & own
    ids = jnp.broadcast_to(ids_ref[...], (Z, 256))
    pick_z = (ids >= 0) & ((ids & 63) == (iota((Z, 256), 0) >> 2))
    live = lax.dot_general(
        pick_y.astype(f32).astype(bf16),
        pick_z.astype(f32).astype(bf16),
        (((1,), (1,)), ((), ())),
        preferred_element_type=f32,
    )
    lane = iota((R, Z), 1)
    row = iota((R, Z), 0) - 4
    last_y = jnp.where(is_edge("cross", True), H - 1, H)
    killed = own & ((live < 0.5) | (lane == Z - 1) | (row >= last_y))
    for x in range(D + 2):
        behind = jnp.where(lane > 0, pltpu.roll(acc_ref[0, x], 1, 1), 0.0)
        ahead = jnp.where(lane < Z - 1, pltpu.roll(acc_ref[2, x], Z - 1, 1), 0.0)
        logit = acc_ref[1, x] + behind + ahead
        if 1 <= x <= D:
            gone = killed
            if x == D:
                gone = gone | (own & is_edge("slab", True))
            logit = jnp.where(gone, dead, logit)
        l_ref[x] = logit

    def send_section(even):
        up_ref, down_ref = (yone_ref, ytwo_ref) if even else (ytwo_ref, yone_ref)
        for k in range(3):
            for x in range(D):
                up_ref[4 * k + x] = q_ref[k, x, H - 4 : H, :]
                down_ref[4 * k + x] = q_ref[k, x, 0:4, :]
        for x in range(D + 2):
            up_ref[12 + x] = l_ref[x, 33:37, :]
            down_ref[12 + x] = l_ref[x, 3:7, :]

    by_parity("cross", send_section)


def pack_kernel(l_ref, yone_ref, ytwo_ref, l2_ref, ylo_ref, yhi_ref, one_ref, two_ref):
    l2_ref[...] = l_ref[...]

    def receive(even):
        ylo_ref[...] = ytwo_ref[...] if even else yone_ref[...]
        yhi_ref[...] = yone_ref[...] if even else ytwo_ref[...]

    by_parity("cross", receive)
    for x in range(D + 2):
        l2_ref[x, 1:5, :] += ylo_ref[12 + x]
        l2_ref[x, 35:39, :] += yhi_ref[12 + x]

    def send(even):
        up_ref, down_ref = (one_ref, two_ref) if even else (two_ref, one_ref)
        for x in range(3):
            up_ref[R * x : R * x + R, :] = l2_ref[x + 3]
            down_ref[R * x : R * x + R, :] = l2_ref[x]
        for k in range(3):
            for ref, first in ((up_ref, D - 3), (down_ref, 0)):
                for x in range(3):
                    at = 3 * R + 8 * (3 * k + x)
                    ref[at : at + 4, :] = ylo_ref[4 * k + first + x]
                    ref[at + 4 : at + 8, :] = yhi_ref[4 * k + first + x]

    by_parity("slab", send)


def section_sums(v_ref, x, tile):
    rows, half, below = tile
    lanes, others = pl.ds(128 * half, 128), pl.ds(128 - 128 * half, 128)
    last_lane = iota((8, 128), 1) == 127
    last_row = iota((8, 128), 0) == 7
    out = []
    for k in range(3):
        v = v_ref[k, x, rows, lanes]
        wrapped = pltpu.roll(v_ref[k, x, rows, others], 127, 1)
        z = jnp.where(last_lane, wrapped, pltpu.roll(v, 127, 1))
        for i, w in enumerate((v + z, z - v)):
            turned = pltpu.roll(w, 7, 0)
            y = jnp.where(last_row, below[half, x, 2 * k + i], turned)
            below[half, x, 2 * k + i] = turned
            out += [w + y, y - w]
    return out


def along_x(low, high):
    a = {}
    for k in range(3):
        for f in range(4):
            v0, v1 = low[4 * k + f], high[4 * k + f]
            if f:
                a[0, f, k] = v0 + v1
            a[1, f, k] = v1 - v0
    return a


def hooke(a, s):
    def scaled(value):
        return value if s is None else s * value

    lam, two_mu, mu = scaled(lame / 16), scaled(shear / 8), scaled(shear / 16)
    lam3, mu3, last = scaled(lame / 48), scaled(shear / 48), scaled((lame + 4 * shear) / 144)
    x, y, z = 0, 1, 2
    out = {}
    n = ((1, 0, x), (0, 1, y), (0, 2, z))
    trace = lam * (a[n[0]] + a[n[1]] + a[n[2]])
    for m in n:
        out[m] = trace + two_mu * a[m]
    for m, o in (((0, 1, x), (1, 0, y)), ((0, 2, x), (1, 0, z)), ((0, 2, y), (0, 1, z))):
        out[m] = out[o] = mu * (a[m] + a[o])
    for m, o in (((1, 1, x), (0, 3, z)), ((1, 1, y), (1, 2, z)), ((1, 2, x), (0, 3, y))):
        both = lam3 * (a[m] + a[o])
        out[m] = both + mu * a[m]
        out[o] = both + mu * a[o]
    m = ((0, 3, x), (1, 2, y), (1, 1, z))
    three = a[m[0]] + a[m[1]] + a[m[2]]
    for o in m:
        out[o] = mu3 * (three + a[o])
    for k in range(3):
        out[1, 3, k] = last * a[1, 3, k]
    return out


def tiles(body, below):
    def step(i, carry):
        rows = pl.ds(pl.multiple_of(8 * (TILES - 1 - i), 8), 8)
        for half in range(2):
            body((rows, half, below))
        return carry

    lax.fori_loop(0, TILES, step, 0)


def stage_b(v_ref, s_ref, g_ref, below, first, last):
    def body(tile):
        rows, lanes = tile[0], pl.ds(128 * tile[1], 128)
        low = section_sums(v_ref, first, tile)
        carried = None
        for x in range(first, last + 1):
            high = section_sums(v_ref, x + 1, tile)
            force = hooke(along_x(low, high), s_ref[x, rows, lanes])
            kept = []
            for k in range(3):
                for f in range(4):
                    diff = force[1, f, k]
                    near = carried[4 * k + f] - diff if carried is not None else None
                    if f:
                        both = force[0, f, k]
                        near = near + both if carried is not None else None
                        kept.append(both + diff)
                    else:
                        kept.append(diff)
                    if carried is not None:
                        g_ref[4 * k + f, x, rows, lanes] = near
            carried = kept
            low = high

    tiles(body, below)


def stage_c(g_ref, v_ref, m_ref, out_ref, base, first, last):
    def plane(x, carry):
        for k in range(3):
            g = [g_ref[4 * k + f, x] for f in range(4)]
            s = (g[0] - g[1]) + pltpu.roll(g[0] + g[1], 1, 0)
            d = (g[2] - g[3]) + pltpu.roll(g[2] + g[3], 1, 0)
            out = (s - d) + pltpu.roll(s + d, 1, 1)
            out_ref[k, x - base] = m_ref[k, x] * out + (spring - shift) * v_ref[k, x]
        return carry

    lax.fori_loop(first, last + 1, plane, 0)


def energy_of(a):
    force = hooke(a, None)
    total = None
    for key in a:
        term = a[key] * force[key]
        total = term if total is None else total + term
    return total


def krylov_kernel(
    qone_ref, q_ref, qtwo_ref, l_ref, one_ref, two_ref, ylo_ref, yhi_ref,
    v0_ref, v1_ref, v2_ref, pone_ref, ptwo_ref, gain_ref, dots_ref,
    m_ref, s_ref, g_ref, acc_ref, below,
):
    for k in range(3):
        for x in range(D):
            v1_ref[k, x + 2, 0:4, :] = ylo_ref[4 * k + x]
            v1_ref[k, x + 2, 4 : 4 + H, :] = q_ref[k, x]
            v1_ref[k, x + 2, 4 + H :, :] = yhi_ref[4 * k + x]
    for x in range(1, 7):
        s_ref[x] = l_ref[x - 1]

    def receive(even):
        low = (two_ref, qtwo_ref) if even else (one_ref, qone_ref)
        high = (one_ref, qone_ref) if even else (two_ref, qtwo_ref)
        for k in range(3):
            for (ref, main), places in ((low, ((1, 0), (2, 1))), (high, ((0, 6), (1, 7), (2, 8)))):
                for source, x in places:
                    at = 3 * R + 8 * (3 * k + source)
                    v1_ref[k, x, 0:4, :] = ref[at : at + 4, :]
                    v1_ref[k, x, 4 : 4 + H, :] = main[k, source]
                    v1_ref[k, x, 4 + H :, :] = ref[at + 4 : at + 8, :]
        s_ref[0] = low[0][0:R, :]
        s_ref[7] = high[0][2 * R : 3 * R, :]
        for x in (1, 2):
            s_ref[x] += low[0][R * x : R * x + R, :]
        for x in (5, 6):
            s_ref[x] += high[0][R * (x - 5) : R * (x - 5) + R, :]

    by_parity("slab", receive)

    def split(x, carry):
        for k in range(3):
            v = v1_ref[k, x]
            fixed = v > 0.5 * held
            v0_ref[k, x] = jnp.where(fixed, 0.0, v)
            m_ref[k, x] = jnp.where(fixed, 0.0, 1.0)
        return carry

    lax.fori_loop(0, 9, split, 0)

    row = iota((R, Z), 0) - 4
    first_y = jnp.where(is_edge("cross", False), 0, -4)
    last_y = jnp.where(is_edge("cross", True), H - 1, R)
    outside_y = (row < first_y) | (row > last_y)
    for x in range(8):
        logit = s_ref[x]
        gone = (logit < 0.1 * dead) | outside_y
        if x < 2:
            gone = gone | is_edge("slab", False)
        if x > 5:
            gone = gone | is_edge("slab", True)
        density = 1.0 / (1.0 + jnp.exp(-logit))
        cube = density * density * density
        s_ref[x] = jnp.where(gone, 0.0, void_modulus + cube * (1.0 - void_modulus))
        if 1 <= x <= 6:
            factor = (-3.0 * (1.0 - void_modulus)) * cube * (1.0 - density)
            gain_ref[x - 1] = jnp.where(gone, 0.0, factor)

    below[...] = jnp.zeros_like(below)
    stage_b(v0_ref, s_ref, g_ref, below, 0, 7)
    stage_c(g_ref, v0_ref, m_ref, v1_ref, 0, 1, 7)
    stage_b(v1_ref, s_ref, g_ref, below, 1, 6)
    stage_c(g_ref, v1_ref, m_ref, v2_ref, 0, 2, 6)

    def send(even):
        pone_ref[...] = v2_ref[:, 5 if even else 3]
        ptwo_ref[...] = v2_ref[:, 3 if even else 5]

    by_parity("slab", send)
    acc_ref[...] = jnp.zeros_like(acc_ref)

    def sums(tile):
        rows, lanes = tile[0], pl.ds(128 * tile[1], 128)
        row = iota((8, 128), 0) + rows.start
        own = (row >= 4) & (row < 4 + H)
        total = [jnp.zeros((8, 128), f32) for _ in range(6)]
        for x in range(2, 6):
            for k in range(3):
                v0 = v0_ref[k, x, rows, lanes]
                v1 = v1_ref[k, x, rows, lanes]
                v2 = v2_ref[k, x, rows, lanes]
                pairs = ((v0, v0), (v0, v1), (v1, v1), (v1, v2), (v2, v2))
                for i, (left, right) in enumerate(pairs):
                    total[i] = total[i] + left * right
        low = section_sums(v2_ref, 2, tile)
        for x in range(2, 6):
            high = section_sums(v2_ref, x + 1, tile)
            total[5] = total[5] + s_ref[x, rows, lanes] * energy_of(along_x(low, high))
            low = high
        total[5] = total[5] + spring * total[4]
        for i in range(6):
            acc_ref[i] += jnp.where(own, total[i], 0.0)

    tiles(sums, below)
    lane = iota((1, 128), 1)
    dots = jnp.zeros((1, 128), f32)
    for i in range(6):
        total = jnp.sum(jnp.sum(acc_ref[i], axis=0, keepdims=True), axis=1, keepdims=True)
        dots = jnp.where(lane == i, total, dots)
    dots_ref[...] = jnp.broadcast_to(dots, dots_ref.shape)


def coefficients(dots_ref):
    dots = jnp.sum(dots_ref[...], axis=0, keepdims=True)
    total = [jnp.broadcast_to(dots[:, i : i + 1], (8, 128)) for i in range(6)]
    d00, d01, d11, d12, d22, g22 = total
    d02 = d11
    g00 = d01 + shift * d00
    g01 = d02 + shift * d01
    g02 = d12 + shift * d02
    g11 = d12 + shift * d11
    g12 = d22 + shift * d12
    tiny = 4e-6

    def inverse(pivot, scale):
        fine = pivot > tiny * scale
        return jnp.where(fine, 1.0 / jnp.where(fine, pivot, 1.0), 0.0)

    i0 = 1.0 / g00
    l1, l2 = g01 * i0, g02 * i0
    i1 = inverse(g11 - l1 * g01, g11)
    m = g12 - l2 * g01
    l3 = m * i1
    i2 = inverse(g22 - l2 * g02 - l3 * m, g22)
    b0 = d00
    b1 = d01 - l1 * b0
    b2 = d02 - l2 * b0 - l3 * b1
    c2 = b2 * i2
    c1 = b1 * i1 - l3 * c2
    c0 = b0 * i0 - l1 * c1 - l2 * c2
    return [jnp.tile(c, (TILES, Z // 128)) for c in (c0, c1, c2)]


def adjoint_kernel(
    p0_ref, p1_ref, p2_ref, pone_ref, ptwo_ref, gain_ref, dots_ref, f_ref,
    disp_ref, shifted_ref, wpart_ref,
    u_ref, lg_ref, s32_ref, below,
):
    c0, c1, c2 = coefficients(dots_ref)

    def combine(x, third):
        for k in range(3):
            u_ref[k, x] = c0 * p0_ref[k, x + 1] + c1 * p1_ref[k, x + 1] + c2 * third(k)

    def inner(x, carry):
        combine(x, lambda k: p2_ref[k, x + 1])
        return carry

    def receive(even):
        combine(0, lambda k: (ptwo_ref if even else pone_ref)[k])
        combine(6, lambda k: (pone_ref if even else ptwo_ref)[k])

    lax.fori_loop(1, 6, inner, 0)
    by_parity("slab", receive)
    for k in range(3):
        for x in range(D):
            disp_ref[k, x] = u_ref[k, x + 1, 4 : 4 + H, :]

    def energies(tile):
        rows, lanes = tile[0], pl.ds(128 * tile[1], 128)
        low = section_sums(u_ref, 0, tile)
        for x in range(6):
            high = section_sums(u_ref, x + 1, tile)
            grad = gain_ref[x, rows, lanes] * energy_of(along_x(low, high))
            lg_ref[1, x, rows, lanes] = grad.astype(bf16).astype(f32)
            low = high

    below[...] = jnp.zeros_like(below)
    tiles(energies, below)
    lane = iota((R, Z), 1)
    row = iota((R, Z), 0) - 4
    reach = (row >= -1) & (row <= H)
    for x in range(6):
        grad = jnp.where(reach, lg_ref[1, x], 0.0)
        lg_ref[1, x] = grad
        lg_ref[0, x] = jnp.where(lane < Z - 1, pltpu.roll(grad, Z - 1, 1), 0.0)
        lg_ref[2, x] = jnp.where(lane > 0, pltpu.roll(grad, 1, 1), 0.0)
    cross = jnp.zeros((NT, KT), f32)
    for x in range(D):
        for ox in range(3):
            for oz in range(3):
                q = 3 * ox + oz
                s32_ref[q * R : (q + 1) * R, :] = lg_ref[oz, x - (ox - 1) + 1]
        rows = s32_ref[...].astype(bf16)
        shifted_ref[x] = rows
        cross = cross + lax.dot_general(
            rows,
            f_ref[:, x].reshape(KT, Z),
            (((1,), (1,)), ((), ())),
            preferred_element_type=f32,
        )
    away = iota((R, KT), 1) % H - (iota((R, KT), 0) - 4)
    wide = [None] * 27
    for ox in range(3):
        for oz in range(3):
            q = 3 * ox + oz
            block = cross[q * R : (q + 1) * R, :]
            for oy in range(3):
                picked = jnp.where(away == oy - 1, block, 0.0)
                wide[9 * ox + 3 * oy + oz] = jnp.sum(picked, axis=0, keepdims=True)
    for t in range(27):
        s32_ref[t : t + 1, :] = wide[t][:, :Z]
        s32_ref[32 + t : 33 + t, :] = wide[t][:, Z:]
    s32_ref[27:32, :] = jnp.zeros((5, Z), f32)
    s32_ref[59:64, :] = jnp.zeros((5, Z), f32)
    value = s32_ref[0:64, :]
    terms = []
    for _ in range(3):
        terms.append(value.astype(bf16))
        value = value - terms[-1].astype(f32)
    terms = jnp.concatenate(terms, axis=0)
    gather = (iota((Z, 128), 0) // H == iota((Z, 128), 1)).astype(f32).astype(bf16)
    summed = jnp.dot(terms, gather, preferred_element_type=f32)
    summed = summed[0:64] + summed[64:128] + summed[128:192]
    narrow = summed[0:32, :] + pltpu.roll(summed[32:64, :], 8, 1)
    packed = narrow[0:4, :]
    for g in range(1, 8):
        packed = packed + pltpu.roll(narrow[4 * g : 4 * g + 4, :], C * g, 1)
    twice = jnp.concatenate([packed, packed], axis=0)
    wpart_ref[...] = jnp.broadcast_to(twice[None], wpart_ref.shape)


def finish_kernel(parts_ref, out_ref):
    total = jnp.sum(parts_ref[...].reshape(parts_ref.shape[0] // 8, 8, 128), axis=0)
    total = total[0:4, :] + total[4:8, :]
    count = lax.axis_size("slab") * D * lax.axis_size("cross") * H * Z
    taps = [total[:, 0:C]]
    for g in range(1, 8):
        taps.append(pltpu.roll(total, 128 - C * g, 1)[:, 0:C])
    turned = jnp.concatenate(taps, axis=0).T
    out_ref[...] = turned[:, 0:27] * (1.0 / math.sqrt(count))


def feature_kernel(table_ref, shifted_ref, out_ref):
    turned = table_ref[...].astype(f32).T.astype(bf16)
    for x in range(D):
        product = jnp.dot(turned, shifted_ref[x], preferred_element_type=f32)
        out_ref[:, x] = product.astype(bf16).reshape(C, H, Z)


def share(x):
    return lax.all_to_all(x, ("slab", "cross"), 0, 0)


def on_device(load, fixed_dofs, features, conv_weight, active_bricks):
    def swap(x, axis, start):
        pairs = [(i, i + 1) for i in range(start, lax.axis_size(axis) - 1, 2)]
        return lax.ppermute(x, axis, pairs + [(j, i) for i, j in pairs])

    def exchange(first, second, axis):
        return swap(first, axis, 0), swap(second, axis, 1)

    devices = lax.axis_size(("slab", "cross"))
    ids = active_bricks.reshape(1, 256)
    rows = shape_of(12 + D + 2, 4, Z)
    logits = shape_of(D + 2, R, Z)
    part = shape_of(3, 3, H, Z)
    q, qone, qtwo, logit, yone, ytwo, table = call(
        conv_kernel,
        [shape_of(3, D, H, Z), part, part, logits, rows, rows, shape_of(NT, KT, dtype=bf16)],
        [
            pltpu.VMEM((NT, KT), f32),
            pltpu.VMEM((3, D + 2, R, Z), f32),
        ],
        ids, conv_weight.T, features, load, fixed_dofs,
        outside=5,
    )
    yone, ytwo = exchange(yone, ytwo, "cross")
    qone, qtwo = exchange(qone, qtwo, "slab")
    wide = shape_of(3 * R + 72, Z)
    logit, ylo, yhi, xone, xtwo = call(
        pack_kernel, [logits, rows, rows, wide, wide], [], logit, yone, ytwo
    )
    xone, xtwo = exchange(xone, xtwo, "slab")
    field = shape_of(3, 9, R, Z)
    plane = shape_of(3, R, Z)
    p0, p1, p2, pone, ptwo, gain, dots = call(
        krylov_kernel,
        [field, field, field, plane, plane, logits, shape_of(devices, 128)],
        [
            pltpu.VMEM((3, 9, R, Z), f32),
            pltpu.VMEM((8, R, Z), f32),
            pltpu.VMEM((12, 9, R, Z), f32),
            pltpu.VMEM((6, 8, 128), f32),
            pltpu.VMEM((2, 9, 6, 8, 128), f32),
        ],
        qone, q, qtwo, logit, xone, xtwo, ylo, yhi,
    )
    dots = share(dots.reshape(devices, 1, 128)).reshape(devices, 128)
    pone, ptwo = exchange(pone, ptwo, "slab")
    displacement, shifted, wpart = call(
        adjoint_kernel,
        [shape_of(3, D, H, Z), shape_of(D, NT, Z, dtype=bf16), shape_of(devices // 2, 8, 128)],
        [
            pltpu.VMEM((3, 7, R, Z), f32),
            pltpu.VMEM((3, 6, R, Z), f32),
            pltpu.VMEM((NT, Z), f32),
            pltpu.VMEM((2, 7, 6, 8, 128), f32),
        ],
        p0, p1, p2, pone, ptwo, gain, dots, features,
    )
    parts = share(wpart.reshape(devices, 4, 128)).reshape(4 * devices, 128)
    (feature_grad,) = call(
        feature_kernel, [jax.ShapeDtypeStruct((C, D, H, Z), bf16)], [], table, shifted
    )
    (weight_grad,) = call(finish_kernel, [jax.ShapeDtypeStruct((C, 27), f32)], [], parts)
    return displacement, feature_grad, weight_grad.T


def sharded(mesh):
    in_specs = (
        P(None, "slab", "cross", None),
        P(None, "slab", "cross", None),
        P(None, "slab", "cross", None),
        P(),
        P("slab", "cross", None),
    )
    out_specs = (P(None, "slab", "cross", None), P(None, "slab", "cross", None), P())

    return jax.shard_map(
        on_device, mesh=mesh, in_specs=in_specs, out_specs=out_specs, check_vma=False
    )


def solution(mesh):
    return sharded(mesh)
```

```python
import math

import jax
import jax.numpy as jnp
from jax import lax
from jax.experimental import pallas as pl
from jax.experimental.pallas import tpu as pltpu
from jax.sharding import PartitionSpec as P


INTERPRET = False

void_modulus = 0.001
spring = 0.1
shift = 0.4
held = 64.0
dead = -1e30
poisson = 0.3
lame = poisson / ((1.0 + poisson) * (1.0 - 2.0 * poisson))
shear = 0.5 / (1.0 + poisson)

D, H, Z, C = 4, 32, 256, 16
R = 40
TILES = R // 8
KT = C * H
NT = 9 * R

f32 = jnp.float32
bf16 = jnp.bfloat16


def iota(shape, dim):
    return lax.broadcasted_iota(jnp.int32, shape, dim)


def call(kernel, out_shape, scratch, *args, outside=0):
    vmem = pl.BlockSpec(memory_space=pltpu.VMEM)
    if not INTERPRET:
        spaces = [pltpu.HBM] * outside + [pltpu.VMEM] * (len(args) - outside)
        args = [pltpu.with_memory_space_constraint(x, s) for x, s in zip(args, spaces)]
    return pl.pallas_call(
        kernel,
        out_shape=out_shape,
        in_specs=[vmem] * len(args),
        out_specs=[vmem] * len(out_shape),
        scratch_shapes=scratch,
        compiler_params=pltpu.CompilerParams(vmem_limit_bytes=24 * 1024 * 1024),
        interpret=INTERPRET,
    )(*args)


def shape_of(*dims, dtype=f32):
    if INTERPRET:
        return jax.ShapeDtypeStruct(dims, dtype)
    return pltpu.VMEM(dims, dtype)


def toeplitz(w_ref, t_ref):
    spread = (iota((C, KT), 1) // H == iota((C, KT), 0)).astype(bf16)
    wide = lax.dot_general(
        w_ref[...], spread, (((0,), (0,)), ((), ())), preferred_element_type=f32
    )
    away = iota((R, KT), 1) % H - (iota((R, KT), 0) - 4)
    for ox in range(3):
        for oz in range(3):
            block = jnp.zeros((R, KT), f32)
            for oy in range(3):
                t = 9 * ox + 3 * oy + oz
                block = jnp.where(away == oy - 1, wide[t : t + 1, :], block)
            t_ref[(3 * ox + oz) * R : (3 * ox + oz + 1) * R, :] = block


def is_edge(axis, last):
    return lax.axis_index(axis) == (lax.axis_size(axis) - 1 if last else 0)


def by_parity(axis, body):
    even = lax.axis_index(axis) % 2 == 0
    pl.when(even)(lambda: body(True))
    pl.when(jnp.logical_not(even))(lambda: body(False))


def conv_kernel(
    ids_ref, w_ref, f_ref, load_ref, fixed_ref,
    q_ref, qone_ref, qtwo_ref, l_ref, yone_ref, ytwo_ref, tout_ref,
    t_ref, acc_ref,
):
    q_ref[...] = jnp.where(fixed_ref[...] != 0, held, load_ref[...])

    def send_length(even):
        up_ref, down_ref = (qone_ref, qtwo_ref) if even else (qtwo_ref, qone_ref)
        up_ref[...] = q_ref[:, D - 3 : D]
        down_ref[...] = q_ref[:, 0:3]

    by_parity("slab", send_length)
    toeplitz(w_ref, t_ref)
    table = t_ref[...].astype(bf16)
    tout_ref[...] = table
    acc_ref[...] = jnp.zeros_like(acc_ref)
    for xin in range(D):
        product = jnp.dot(table, f_ref[:, xin].reshape(KT, Z), preferred_element_type=f32)
        for ox in range(3):
            for oz in range(3):
                q = 3 * ox + oz
                acc_ref[oz, xin - (ox - 1) + 1] += product[q * R : (q + 1) * R, :]
    ids = jnp.broadcast_to(ids_ref[...], (R, 256))
    row = iota((R, 256), 0) - 4
    own = (row >= 0) & (row < H)
    pick_y = ((ids >> 6) == (row >> 2)) & own
    ids = jnp.broadcast_to(ids_ref[...], (Z, 256))
    pick_z = (ids >= 0) & ((ids & 63) == (iota((Z, 256), 0) >> 2))
    live = lax.dot_general(
        pick_y.astype(f32).astype(bf16),
        pick_z.astype(f32).astype(bf16),
        (((1,), (1,)), ((), ())),
        preferred_element_type=f32,
    )
    lane = iota((R, Z), 1)
    row = iota((R, Z), 0) - 4
    last_y = jnp.where(is_edge("cross", True), H - 1, H)
    killed = own & ((live < 0.5) | (lane == Z - 1) | (row >= last_y))
    for x in range(D + 2):
        behind = jnp.where(lane > 0, pltpu.roll(acc_ref[0, x], 1, 1), 0.0)
        ahead = jnp.where(lane < Z - 1, pltpu.roll(acc_ref[2, x], Z - 1, 1), 0.0)
        logit = acc_ref[1, x] + behind + ahead
        if 1 <= x <= D:
            gone = killed
            if x == D:
                gone = gone | (own & is_edge("slab", True))
            logit = jnp.where(gone, dead, logit)
        l_ref[x] = logit

    def send_section(even):
        up_ref, down_ref = (yone_ref, ytwo_ref) if even else (ytwo_ref, yone_ref)
        for k in range(3):
            for x in range(D):
                up_ref[4 * k + x] = q_ref[k, x, H - 4 : H, :]
                down_ref[4 * k + x] = q_ref[k, x, 0:4, :]
        for x in range(D + 2):
            up_ref[12 + x] = l_ref[x, 33:37, :]
            down_ref[12 + x] = l_ref[x, 3:7, :]

    by_parity("cross", send_section)


def pack_kernel(l_ref, yone_ref, ytwo_ref, l2_ref, ylo_ref, yhi_ref, one_ref, two_ref):
    l2_ref[...] = l_ref[...]

    def receive(even):
        ylo_ref[...] = ytwo_ref[...] if even else yone_ref[...]
        yhi_ref[...] = yone_ref[...] if even else ytwo_ref[...]

    by_parity("cross", receive)
    for x in range(D + 2):
        l2_ref[x, 1:5, :] += ylo_ref[12 + x]
        l2_ref[x, 35:39, :] += yhi_ref[12 + x]

    def send(even):
        up_ref, down_ref = (one_ref, two_ref) if even else (two_ref, one_ref)
        for x in range(3):
            up_ref[R * x : R * x + R, :] = l2_ref[x + 3]
            down_ref[R * x : R * x + R, :] = l2_ref[x]
        for k in range(3):
            for ref, first in ((up_ref, D - 3), (down_ref, 0)):
                for x in range(3):
                    at = 3 * R + 8 * (3 * k + x)
                    ref[at : at + 4, :] = ylo_ref[4 * k + first + x]
                    ref[at + 4 : at + 8, :] = yhi_ref[4 * k + first + x]

    by_parity("slab", send)


def section_sums(v_ref, x, tile):
    rows, half, below = tile
    lanes, others = pl.ds(128 * half, 128), pl.ds(128 - 128 * half, 128)
    last_lane = iota((8, 128), 1) == 127
    last_row = iota((8, 128), 0) == 7
    out = []
    for k in range(3):
        v = v_ref[k, x, rows, lanes]
        wrapped = pltpu.roll(v_ref[k, x, rows, others], 127, 1)
        z = jnp.where(last_lane, wrapped, pltpu.roll(v, 127, 1))
        for i, w in enumerate((v + z, z - v)):
            turned = pltpu.roll(w, 7, 0)
            y = jnp.where(last_row, below[half, x, 2 * k + i], turned)
            below[half, x, 2 * k + i] = turned
            out += [w + y, y - w]
    return out


def along_x(low, high):
    a = {}
    for k in range(3):
        for f in range(4):
            v0, v1 = low[4 * k + f], high[4 * k + f]
            if f:
                a[0, f, k] = v0 + v1
            a[1, f, k] = v1 - v0
    return a


def hooke(a, s):
    def scaled(value):
        return value if s is None else s * value

    lam, two_mu, mu = scaled(lame / 16), scaled(shear / 8), scaled(shear / 16)
    lam3, mu3, last = scaled(lame / 48), scaled(shear / 48), scaled((lame + 4 * shear) / 144)
    x, y, z = 0, 1, 2
    out = {}
    n = ((1, 0, x), (0, 1, y), (0, 2, z))
    trace = lam * (a[n[0]] + a[n[1]] + a[n[2]])
    for m in n:
        out[m] = trace + two_mu * a[m]
    for m, o in (((0, 1, x), (1, 0, y)), ((0, 2, x), (1, 0, z)), ((0, 2, y), (0, 1, z))):
        out[m] = out[o] = mu * (a[m] + a[o])
    for m, o in (((1, 1, x), (0, 3, z)), ((1, 1, y), (1, 2, z)), ((1, 2, x), (0, 3, y))):
        both = lam3 * (a[m] + a[o])
        out[m] = both + mu * a[m]
        out[o] = both + mu * a[o]
    m = ((0, 3, x), (1, 2, y), (1, 1, z))
    three = a[m[0]] + a[m[1]] + a[m[2]]
    for o in m:
        out[o] = mu3 * (three + a[o])
    for k in range(3):
        out[1, 3, k] = last * a[1, 3, k]
    return out


def tiles(body, below):
    def step(i, carry):
        rows = pl.ds(pl.multiple_of(8 * (TILES - 1 - i), 8), 8)
        for half in range(2):
            body((rows, half, below))
        return carry

    lax.fori_loop(0, TILES, step, 0)


def stage_b(v_ref, s_ref, g_ref, below, first, last):
    def body(tile):
        rows, lanes = tile[0], pl.ds(128 * tile[1], 128)
        low = section_sums(v_ref, first, tile)
        carried = None
        for x in range(first, last + 1):
            high = section_sums(v_ref, x + 1, tile)
            force = hooke(along_x(low, high), s_ref[x, rows, lanes])
            kept = []
            for k in range(3):
                for f in range(4):
                    diff = force[1, f, k]
                    near = carried[4 * k + f] - diff if carried is not None else None
                    if f:
                        both = force[0, f, k]
                        near = near + both if carried is not None else None
                        kept.append(both + diff)
                    else:
                        kept.append(diff)
                    if carried is not None:
                        g_ref[4 * k + f, x, rows, lanes] = near
            carried = kept
            low = high

    tiles(body, below)


def stage_c(g_ref, v_ref, m_ref, out_ref, base, first, last):
    def plane(x, carry):
        for k in range(3):
            g = [g_ref[4 * k + f, x] for f in range(4)]
            s = (g[0] - g[1]) + pltpu.roll(g[0] + g[1], 1, 0)
            d = (g[2] - g[3]) + pltpu.roll(g[2] + g[3], 1, 0)
            out = (s - d) + pltpu.roll(s + d, 1, 1)
            out_ref[k, x - base] = m_ref[k, x] * out + (spring - shift) * v_ref[k, x]
        return carry

    lax.fori_loop(first, last + 1, plane, 0)


def energy_of(a):
    force = hooke(a, None)
    total = None
    for key in a:
        term = a[key] * force[key]
        total = term if total is None else total + term
    return total


def krylov_kernel(
    qone_ref, q_ref, qtwo_ref, l_ref, one_ref, two_ref, ylo_ref, yhi_ref,
    v0_ref, v1_ref, v2_ref, pone_ref, ptwo_ref, gain_ref, dots_ref,
    m_ref, s_ref, g_ref, acc_ref, below,
):
    for k in range(3):
        for x in range(D):
            v1_ref[k, x + 2, 0:4, :] = ylo_ref[4 * k + x]
            v1_ref[k, x + 2, 4 : 4 + H, :] = q_ref[k, x]
            v1_ref[k, x + 2, 4 + H :, :] = yhi_ref[4 * k + x]
    for x in range(1, 7):
        s_ref[x] = l_ref[x - 1]

    def receive(even):
        low = (two_ref, qtwo_ref) if even else (one_ref, qone_ref)
        high = (one_ref, qone_ref) if even else (two_ref, qtwo_ref)
        for k in range(3):
            for (ref, main), places in ((low, ((1, 0), (2, 1))), (high, ((0, 6), (1, 7), (2, 8)))):
                for source, x in places:
                    at = 3 * R + 8 * (3 * k + source)
                    v1_ref[k, x, 0:4, :] = ref[at : at + 4, :]
                    v1_ref[k, x, 4 : 4 + H, :] = main[k, source]
                    v1_ref[k, x, 4 + H :, :] = ref[at + 4 : at + 8, :]
        s_ref[0] = low[0][0:R, :]
        s_ref[7] = high[0][2 * R : 3 * R, :]
        for x in (1, 2):
            s_ref[x] += low[0][R * x : R * x + R, :]
        for x in (5, 6):
            s_ref[x] += high[0][R * (x - 5) : R * (x - 5) + R, :]

    by_parity("slab", receive)

    def split(x, carry):
        for k in range(3):
            v = v1_ref[k, x]
            fixed = v > 0.5 * held
            v0_ref[k, x] = jnp.where(fixed, 0.0, v)
            m_ref[k, x] = jnp.where(fixed, 0.0, 1.0)
        return carry

    lax.fori_loop(0, 9, split, 0)

    row = iota((R, Z), 0) - 4
    first_y = jnp.where(is_edge("cross", False), 0, -4)
    last_y = jnp.where(is_edge("cross", True), H - 1, R)
    outside_y = (row < first_y) | (row > last_y)
    for x in range(8):
        logit = s_ref[x]
        gone = (logit < 0.1 * dead) | outside_y
        if x < 2:
            gone = gone | is_edge("slab", False)
        if x > 5:
            gone = gone | is_edge("slab", True)
        density = 1.0 / (1.0 + jnp.exp(-logit))
        cube = density * density * density
        s_ref[x] = jnp.where(gone, 0.0, void_modulus + cube * (1.0 - void_modulus))
        if 1 <= x <= 6:
            factor = (-3.0 * (1.0 - void_modulus)) * cube * (1.0 - density)
            gain_ref[x - 1] = jnp.where(gone, 0.0, factor)

    below[...] = jnp.zeros_like(below)
    stage_b(v0_ref, s_ref, g_ref, below, 0, 7)
    stage_c(g_ref, v0_ref, m_ref, v1_ref, 0, 1, 7)
    stage_b(v1_ref, s_ref, g_ref, below, 1, 6)
    stage_c(g_ref, v1_ref, m_ref, v2_ref, 0, 2, 6)

    def send(even):
        pone_ref[...] = v2_ref[:, 5 if even else 3]
        ptwo_ref[...] = v2_ref[:, 3 if even else 5]

    by_parity("slab", send)
    acc_ref[...] = jnp.zeros_like(acc_ref)

    def sums(tile):
        rows, lanes = tile[0], pl.ds(128 * tile[1], 128)
        row = iota((8, 128), 0) + rows.start
        own = (row >= 4) & (row < 4 + H)
        total = [jnp.zeros((8, 128), f32) for _ in range(6)]
        for x in range(2, 6):
            for k in range(3):
                v0 = v0_ref[k, x, rows, lanes]
                v1 = v1_ref[k, x, rows, lanes]
                v2 = v2_ref[k, x, rows, lanes]
                pairs = ((v0, v0), (v0, v1), (v1, v1), (v1, v2), (v2, v2))
                for i, (left, right) in enumerate(pairs):
                    total[i] = total[i] + left * right
        low = section_sums(v2_ref, 2, tile)
        for x in range(2, 6):
            high = section_sums(v2_ref, x + 1, tile)
            total[5] = total[5] + s_ref[x, rows, lanes] * energy_of(along_x(low, high))
            low = high
        total[5] = total[5] + spring * total[4]
        for i in range(6):
            acc_ref[i] += jnp.where(own, total[i], 0.0)

    tiles(sums, below)
    lane = iota((1, 128), 1)
    dots = jnp.zeros((1, 128), f32)
    for i in range(6):
        total = jnp.sum(jnp.sum(acc_ref[i], axis=0, keepdims=True), axis=1, keepdims=True)
        dots = jnp.where(lane == i, total, dots)
    dots_ref[...] = jnp.broadcast_to(dots, dots_ref.shape)


def coefficients(dots_ref):
    dots = jnp.sum(dots_ref[...], axis=0, keepdims=True)
    total = [jnp.broadcast_to(dots[:, i : i + 1], (8, 128)) for i in range(6)]
    d00, d01, d11, d12, d22, g22 = total
    d02 = d11
    g00 = d01 + shift * d00
    g01 = d02 + shift * d01
    g02 = d12 + shift * d02
    g11 = d12 + shift * d11
    g12 = d22 + shift * d12
    tiny = 4e-6

    def inverse(pivot, scale):
        fine = pivot > tiny * scale
        return jnp.where(fine, 1.0 / jnp.where(fine, pivot, 1.0), 0.0)

    i0 = 1.0 / g00
    l1, l2 = g01 * i0, g02 * i0
    i1 = inverse(g11 - l1 * g01, g11)
    m = g12 - l2 * g01
    l3 = m * i1
    i2 = inverse(g22 - l2 * g02 - l3 * m, g22)
    b0 = d00
    b1 = d01 - l1 * b0
    b2 = d02 - l2 * b0 - l3 * b1
    c2 = b2 * i2
    c1 = b1 * i1 - l3 * c2
    c0 = b0 * i0 - l1 * c1 - l2 * c2
    return [jnp.tile(c, (TILES, Z // 128)) for c in (c0, c1, c2)]


def adjoint_kernel(
    p0_ref, p1_ref, p2_ref, pone_ref, ptwo_ref, gain_ref, dots_ref, f_ref,
    disp_ref, shifted_ref, wpart_ref,
    u_ref, lg_ref, s32_ref, below,
):
    c0, c1, c2 = coefficients(dots_ref)

    def combine(x, third):
        for k in range(3):
            u_ref[k, x] = c0 * p0_ref[k, x + 1] + c1 * p1_ref[k, x + 1] + c2 * third(k)

    def inner(x, carry):
        combine(x, lambda k: p2_ref[k, x + 1])
        return carry

    def receive(even):
        combine(0, lambda k: (ptwo_ref if even else pone_ref)[k])
        combine(6, lambda k: (pone_ref if even else ptwo_ref)[k])

    lax.fori_loop(1, 6, inner, 0)
    by_parity("slab", receive)
    for k in range(3):
        for x in range(D):
            disp_ref[k, x] = u_ref[k, x + 1, 4 : 4 + H, :]

    def energies(tile):
        rows, lanes = tile[0], pl.ds(128 * tile[1], 128)
        low = section_sums(u_ref, 0, tile)
        for x in range(6):
            high = section_sums(u_ref, x + 1, tile)
            grad = gain_ref[x, rows, lanes] * energy_of(along_x(low, high))
            lg_ref[1, x, rows, lanes] = grad.astype(bf16).astype(f32)
            low = high

    below[...] = jnp.zeros_like(below)
    tiles(energies, below)
    lane = iota((R, Z), 1)
    row = iota((R, Z), 0) - 4
    reach = (row >= -1) & (row <= H)
    for x in range(6):
        grad = jnp.where(reach, lg_ref[1, x], 0.0)
        lg_ref[1, x] = grad
        lg_ref[0, x] = jnp.where(lane < Z - 1, pltpu.roll(grad, Z - 1, 1), 0.0)
        lg_ref[2, x] = jnp.where(lane > 0, pltpu.roll(grad, 1, 1), 0.0)
    cross = jnp.zeros((NT, KT), f32)
    for x in range(D):
        for ox in range(3):
            for oz in range(3):
                q = 3 * ox + oz
                s32_ref[q * R : (q + 1) * R, :] = lg_ref[oz, x - (ox - 1) + 1]
        rows = s32_ref[...].astype(bf16)
        shifted_ref[x] = rows
        cross = cross + lax.dot_general(
            rows,
            f_ref[:, x].reshape(KT, Z),
            (((1,), (1,)), ((), ())),
            preferred_element_type=f32,
        )
    away = iota((R, KT), 1) % H - (iota((R, KT), 0) - 4)
    wide = [None] * 27
    for ox in range(3):
        for oz in range(3):
            q = 3 * ox + oz
            block = cross[q * R : (q + 1) * R, :]
            for oy in range(3):
                picked = jnp.where(away == oy - 1, block, 0.0)
                wide[9 * ox + 3 * oy + oz] = jnp.sum(picked, axis=0, keepdims=True)
    for t in range(27):
        s32_ref[t : t + 1, :] = wide[t][:, :Z]
        s32_ref[32 + t : 33 + t, :] = wide[t][:, Z:]
    s32_ref[27:32, :] = jnp.zeros((5, Z), f32)
    s32_ref[59:64, :] = jnp.zeros((5, Z), f32)
    value = s32_ref[0:64, :]
    terms = []
    for _ in range(3):
        terms.append(value.astype(bf16))
        value = value - terms[-1].astype(f32)
    terms = jnp.concatenate(terms, axis=0)
    gather = (iota((Z, 128), 0) // H == iota((Z, 128), 1)).astype(f32).astype(bf16)
    summed = jnp.dot(terms, gather, preferred_element_type=f32)
    summed = summed[0:64] + summed[64:128] + summed[128:192]
    narrow = summed[0:32, :] + pltpu.roll(summed[32:64, :], 8, 1)
    packed = narrow[0:4, :]
    for g in range(1, 8):
        packed = packed + pltpu.roll(narrow[4 * g : 4 * g + 4, :], C * g, 1)
    twice = jnp.concatenate([packed, packed], axis=0)
    wpart_ref[...] = jnp.broadcast_to(twice[None], wpart_ref.shape)


def finish_kernel(parts_ref, out_ref):
    total = jnp.sum(parts_ref[...].reshape(parts_ref.shape[0] // 8, 8, 128), axis=0)
    total = total[0:4, :] + total[4:8, :]
    count = lax.axis_size("slab") * D * lax.axis_size("cross") * H * Z
    taps = [total[:, 0:C]]
    for g in range(1, 8):
        taps.append(pltpu.roll(total, 128 - C * g, 1)[:, 0:C])
    turned = jnp.concatenate(taps, axis=0).T
    out_ref[...] = turned[:, 0:27] * (1.0 / math.sqrt(count))


def feature_kernel(table_ref, shifted_ref, out_ref):
    turned = table_ref[...].astype(f32).T.astype(bf16)
    for x in range(D):
        product = jnp.dot(turned, shifted_ref[x], preferred_element_type=f32)
        out_ref[:, x] = product.astype(bf16).reshape(C, H, Z)


def share(x):
    return lax.all_to_all(x, ("slab", "cross"), 0, 0)


def on_device(load, fixed_dofs, features, conv_weight, active_bricks):
    def swap(x, axis, start):
        pairs = [(i, i + 1) for i in range(start, lax.axis_size(axis) - 1, 2)]
        return lax.ppermute(x, axis, pairs + [(j, i) for i, j in pairs])

    def exchange(first, second, axis):
        return swap(first, axis, 0), swap(second, axis, 1)

    devices = lax.axis_size(("slab", "cross"))
    ids = active_bricks.reshape(1, 256)
    rows = shape_of(12 + D + 2, 4, Z)
    logits = shape_of(D + 2, R, Z)
    part = shape_of(3, 3, H, Z)
    q, qone, qtwo, logit, yone, ytwo, table = call(
        conv_kernel,
        [shape_of(3, D, H, Z), part, part, logits, rows, rows, shape_of(NT, KT, dtype=bf16)],
        [
            pltpu.VMEM((NT, KT), f32),
            pltpu.VMEM((3, D + 2, R, Z), f32),
        ],
        ids, conv_weight.T, features, load, fixed_dofs,
        outside=5,
    )
    yone = swap(yone, "cross", 0)
    ytwo = swap(ytwo, "cross", 1)
    qone = swap(qone, "slab", 0)
    qtwo = swap(qtwo, "slab", 1)
    wide = shape_of(3 * R + 72, Z)
    logit, ylo, yhi, xone, xtwo = call(
        pack_kernel, [logits, rows, rows, wide, wide], [], logit, yone, ytwo
    )
    xone, xtwo = exchange(xone, xtwo, "slab")
    field = shape_of(3, 9, R, Z)
    plane = shape_of(3, R, Z)
    p0, p1, p2, pone, ptwo, gain, dots = call(
        krylov_kernel,
        [field, field, field, plane, plane, logits, shape_of(devices, 128)],
        [
            pltpu.VMEM((3, 9, R, Z), f32),
            pltpu.VMEM((8, R, Z), f32),
            pltpu.VMEM((12, 9, R, Z), f32),
            pltpu.VMEM((6, 8, 128), f32),
            pltpu.VMEM((2, 9, 6, 8, 128), f32),
        ],
        qone, q, qtwo, logit, xone, xtwo, ylo, yhi,
    )
    dots = share(dots.reshape(devices, 1, 128)).reshape(devices, 128)
    pone, ptwo = exchange(pone, ptwo, "slab")
    displacement, shifted, wpart = call(
        adjoint_kernel,
        [shape_of(3, D, H, Z), shape_of(D, NT, Z, dtype=bf16), shape_of(devices // 2, 8, 128)],
        [
            pltpu.VMEM((3, 7, R, Z), f32),
            pltpu.VMEM((3, 6, R, Z), f32),
            pltpu.VMEM((NT, Z), f32),
            pltpu.VMEM((2, 7, 6, 8, 128), f32),
        ],
        p0, p1, p2, pone, ptwo, gain, dots, features,
    )
    parts = share(wpart.reshape(devices, 4, 128)).reshape(4 * devices, 128)
    (feature_grad,) = call(
        feature_kernel, [jax.ShapeDtypeStruct((C, D, H, Z), bf16)], [], table, shifted
    )
    (weight_grad,) = call(finish_kernel, [jax.ShapeDtypeStruct((C, 27), f32)], [], parts)
    return displacement, feature_grad, weight_grad.T


def sharded(mesh):
    in_specs = (
        P(None, "slab", "cross", None),
        P(None, "slab", "cross", None),
        P(None, "slab", "cross", None),
        P(),
        P("slab", "cross", None),
    )
    out_specs = (P(None, "slab", "cross", None), P(None, "slab", "cross", None), P())

    return jax.shard_map(
        on_device, mesh=mesh, in_specs=in_specs, out_specs=out_specs, check_vma=False
    )


def solution(mesh):
    return sharded(mesh)
```

```python
import math

import jax
import jax.numpy as jnp
from jax import lax
from jax.experimental import pallas as pl
from jax.experimental.pallas import tpu as pltpu
from jax.sharding import PartitionSpec as P


INTERPRET = False

void_modulus = 0.001
spring = 0.1
shift = 0.4
held = 64.0
dead = -1e30
poisson = 0.3
lame = poisson / ((1.0 + poisson) * (1.0 - 2.0 * poisson))
shear = 0.5 / (1.0 + poisson)

D, H, Z, C = 4, 32, 256, 16
R = 40
TILES = R // 8
KT = C * H
NT = 9 * R

f32 = jnp.float32
bf16 = jnp.bfloat16


def iota(shape, dim):
    return lax.broadcasted_iota(jnp.int32, shape, dim)


def call(kernel, out_shape, scratch, *args, outside=0):
    vmem = pl.BlockSpec(memory_space=pltpu.VMEM)
    if not INTERPRET:
        spaces = [pltpu.HBM] * outside + [pltpu.VMEM] * (len(args) - outside)
        args = [pltpu.with_memory_space_constraint(x, s) for x, s in zip(args, spaces)]
    return pl.pallas_call(
        kernel,
        out_shape=out_shape,
        in_specs=[vmem] * len(args),
        out_specs=[vmem] * len(out_shape),
        scratch_shapes=scratch,
        compiler_params=pltpu.CompilerParams(vmem_limit_bytes=24 * 1024 * 1024),
        interpret=INTERPRET,
    )(*args)


def shape_of(*dims, dtype=f32):
    if INTERPRET:
        return jax.ShapeDtypeStruct(dims, dtype)
    return pltpu.VMEM(dims, dtype)


def toeplitz(w_ref, t_ref):
    spread = (iota((C, KT), 1) // H == iota((C, KT), 0)).astype(bf16)
    wide = lax.dot_general(
        w_ref[...], spread, (((0,), (0,)), ((), ())), preferred_element_type=f32
    )
    away = iota((R, KT), 1) % H - (iota((R, KT), 0) - 4)
    for ox in range(3):
        for oz in range(3):
            block = jnp.zeros((R, KT), f32)
            for oy in range(3):
                t = 9 * ox + 3 * oy + oz
                block = jnp.where(away == oy - 1, wide[t : t + 1, :], block)
            t_ref[(3 * ox + oz) * R : (3 * ox + oz + 1) * R, :] = block


def is_edge(axis, last):
    return lax.axis_index(axis) == (lax.axis_size(axis) - 1 if last else 0)


def by_parity(axis, body):
    even = lax.axis_index(axis) % 2 == 0
    pl.when(even)(lambda: body(True))
    pl.when(jnp.logical_not(even))(lambda: body(False))


def conv_kernel(
    ids_ref, w_ref, f_ref, load_ref, fixed_ref,
    q_ref, qone_ref, qtwo_ref, l_ref, yone_ref, ytwo_ref, tout_ref,
    t_ref, acc_ref,
):
    q_ref[...] = jnp.where(fixed_ref[...] != 0, held, load_ref[...])

    def send_length(even):
        up_ref, down_ref = (qone_ref, qtwo_ref) if even else (qtwo_ref, qone_ref)
        up_ref[...] = q_ref[:, D - 3 : D]
        down_ref[...] = q_ref[:, 0:3]

    by_parity("slab", send_length)
    toeplitz(w_ref, t_ref)
    table = t_ref[...].astype(bf16)
    tout_ref[...] = table
    acc_ref[...] = jnp.zeros_like(acc_ref)
    for xin in range(D):
        product = jnp.dot(table, f_ref[:, xin].reshape(KT, Z), preferred_element_type=f32)
        for ox in range(3):
            for oz in range(3):
                q = 3 * ox + oz
                acc_ref[oz, xin - (ox - 1) + 1] += product[q * R : (q + 1) * R, :]
    ids = jnp.broadcast_to(ids_ref[...], (R, 256))
    row = iota((R, 256), 0) - 4
    own = (row >= 0) & (row < H)
    pick_y = ((ids >> 6) == (row >> 2)) & own
    ids = jnp.broadcast_to(ids_ref[...], (Z, 256))
    pick_z = (ids >= 0) & ((ids & 63) == (iota((Z, 256), 0) >> 2))
    live = lax.dot_general(
        pick_y.astype(f32).astype(bf16),
        pick_z.astype(f32).astype(bf16),
        (((1,), (1,)), ((), ())),
        preferred_element_type=f32,
    )
    lane = iota((R, Z), 1)
    row = iota((R, Z), 0) - 4
    last_y = jnp.where(is_edge("cross", True), H - 1, H)
    killed = own & ((live < 0.5) | (lane == Z - 1) | (row >= last_y))
    for x in range(D + 2):
        behind = jnp.where(lane > 0, pltpu.roll(acc_ref[0, x], 1, 1), 0.0)
        ahead = jnp.where(lane < Z - 1, pltpu.roll(acc_ref[2, x], Z - 1, 1), 0.0)
        logit = acc_ref[1, x] + behind + ahead
        if 1 <= x <= D:
            gone = killed
            if x == D:
                gone = gone | (own & is_edge("slab", True))
            logit = jnp.where(gone, dead, logit)
        l_ref[x] = logit

    def send_section(even):
        up_ref, down_ref = (yone_ref, ytwo_ref) if even else (ytwo_ref, yone_ref)
        for k in range(3):
            for x in range(D):
                up_ref[4 * k + x] = q_ref[k, x, H - 4 : H, :]
                down_ref[4 * k + x] = q_ref[k, x, 0:4, :]
        for x in range(D + 2):
            up_ref[12 + x] = l_ref[x, 33:37, :]
            down_ref[12 + x] = l_ref[x, 3:7, :]

    by_parity("cross", send_section)


def pack_kernel(l_ref, yone_ref, ytwo_ref, l2_ref, ylo_ref, yhi_ref, one_ref, two_ref):
    l2_ref[...] = l_ref[...]

    def receive(even):
        ylo_ref[...] = ytwo_ref[...] if even else yone_ref[...]
        yhi_ref[...] = yone_ref[...] if even else ytwo_ref[...]

    by_parity("cross", receive)
    for x in range(D + 2):
        l2_ref[x, 1:5, :] += ylo_ref[12 + x]
        l2_ref[x, 35:39, :] += yhi_ref[12 + x]

    def send(even):
        up_ref, down_ref = (one_ref, two_ref) if even else (two_ref, one_ref)
        for x in range(3):
            up_ref[R * x : R * x + R, :] = l2_ref[x + 3]
            down_ref[R * x : R * x + R, :] = l2_ref[x]
        for k in range(3):
            for ref, first in ((up_ref, D - 3), (down_ref, 0)):
                for x in range(3):
                    at = 3 * R + 8 * (3 * k + x)
                    ref[at : at + 4, :] = ylo_ref[4 * k + first + x]
                    ref[at + 4 : at + 8, :] = yhi_ref[4 * k + first + x]

    by_parity("slab", send)


def section_sums(v_ref, x, tile):
    rows, half, below = tile
    lanes, others = pl.ds(128 * half, 128), pl.ds(128 - 128 * half, 128)
    last_lane = iota((8, 128), 1) == 127
    last_row = iota((8, 128), 0) == 7
    out = []
    for k in range(3):
        v = v_ref[k, x, rows, lanes]
        wrapped = pltpu.roll(v_ref[k, x, rows, others], 127, 1)
        z = jnp.where(last_lane, wrapped, pltpu.roll(v, 127, 1))
        for i, w in enumerate((v + z, z - v)):
            turned = pltpu.roll(w, 7, 0)
            y = jnp.where(last_row, below[half, x, 2 * k + i], turned)
            below[half, x, 2 * k + i] = turned
            out += [w + y, y - w]
    return out


def along_x(low, high):
    a = {}
    for k in range(3):
        for f in range(4):
            v0, v1 = low[4 * k + f], high[4 * k + f]
            if f:
                a[0, f, k] = v0 + v1
            a[1, f, k] = v1 - v0
    return a


def hooke(a, s):
    def scaled(value):
        return value if s is None else s * value

    lam, two_mu, mu = scaled(lame / 16), scaled(shear / 8), scaled(shear / 16)
    lam3, mu3, last = scaled(lame / 48), scaled(shear / 48), scaled((lame + 4 * shear) / 144)
    x, y, z = 0, 1, 2
    out = {}
    n = ((1, 0, x), (0, 1, y), (0, 2, z))
    trace = lam * (a[n[0]] + a[n[1]] + a[n[2]])
    for m in n:
        out[m] = trace + two_mu * a[m]
    for m, o in (((0, 1, x), (1, 0, y)), ((0, 2, x), (1, 0, z)), ((0, 2, y), (0, 1, z))):
        out[m] = out[o] = mu * (a[m] + a[o])
    for m, o in (((1, 1, x), (0, 3, z)), ((1, 1, y), (1, 2, z)), ((1, 2, x), (0, 3, y))):
        both = lam3 * (a[m] + a[o])
        out[m] = both + mu * a[m]
        out[o] = both + mu * a[o]
    m = ((0, 3, x), (1, 2, y), (1, 1, z))
    three = a[m[0]] + a[m[1]] + a[m[2]]
    for o in m:
        out[o] = mu3 * (three + a[o])
    for k in range(3):
        out[1, 3, k] = last * a[1, 3, k]
    return out


def tiles(body, below):
    def step(i, carry):
        rows = pl.ds(pl.multiple_of(8 * (TILES - 1 - i), 8), 8)
        for half in range(2):
            body((rows, half, below))
        return carry

    lax.fori_loop(0, TILES, step, 0)


def stage_b(v_ref, s_ref, g_ref, below, first, last):
    def body(tile):
        rows, lanes = tile[0], pl.ds(128 * tile[1], 128)
        low = section_sums(v_ref, first, tile)
        carried = None
        for x in range(first, last + 1):
            high = section_sums(v_ref, x + 1, tile)
            force = hooke(along_x(low, high), s_ref[x, rows, lanes])
            kept = []
            for k in range(3):
                for f in range(4):
                    diff = force[1, f, k]
                    near = carried[4 * k + f] - diff if carried is not None else None
                    if f:
                        both = force[0, f, k]
                        near = near + both if carried is not None else None
                        kept.append(both + diff)
                    else:
                        kept.append(diff)
                    if carried is not None:
                        g_ref[4 * k + f, x, rows, lanes] = near
            carried = kept
            low = high

    tiles(body, below)


def stage_c(g_ref, v_ref, m_ref, out_ref, base, first, last):
    def plane(x, carry):
        for k in range(3):
            g = [g_ref[4 * k + f, x] for f in range(4)]
            s = (g[0] - g[1]) + pltpu.roll(g[0] + g[1], 1, 0)
            d = (g[2] - g[3]) + pltpu.roll(g[2] + g[3], 1, 0)
            out = (s - d) + pltpu.roll(s + d, 1, 1)
            out_ref[k, x - base] = m_ref[k, x] * out + (spring - shift) * v_ref[k, x]
        return carry

    lax.fori_loop(first, last + 1, plane, 0, unroll=True)


def energy_of(a):
    force = hooke(a, None)
    total = None
    for key in a:
        term = a[key] * force[key]
        total = term if total is None else total + term
    return total


def krylov_kernel(
    qone_ref, q_ref, qtwo_ref, l_ref, one_ref, two_ref, ylo_ref, yhi_ref,
    v0_ref, v1_ref, v2_ref, pone_ref, ptwo_ref, gain_ref, dots_ref,
    m_ref, s_ref, g_ref, acc_ref, below,
):
    for k in range(3):
        for x in range(D):
            v1_ref[k, x + 2, 0:4, :] = ylo_ref[4 * k + x]
            v1_ref[k, x + 2, 4 : 4 + H, :] = q_ref[k, x]
            v1_ref[k, x + 2, 4 + H :, :] = yhi_ref[4 * k + x]
    for x in range(1, 7):
        s_ref[x] = l_ref[x - 1]

    def receive(even):
        low = (two_ref, qtwo_ref) if even else (one_ref, qone_ref)
        high = (one_ref, qone_ref) if even else (two_ref, qtwo_ref)
        for k in range(3):
            for (ref, main), places in ((low, ((1, 0), (2, 1))), (high, ((0, 6), (1, 7), (2, 8)))):
                for source, x in places:
                    at = 3 * R + 8 * (3 * k + source)
                    v1_ref[k, x, 0:4, :] = ref[at : at + 4, :]
                    v1_ref[k, x, 4 : 4 + H, :] = main[k, source]
                    v1_ref[k, x, 4 + H :, :] = ref[at + 4 : at + 8, :]
        s_ref[0] = low[0][0:R, :]
        s_ref[7] = high[0][2 * R : 3 * R, :]
        for x in (1, 2):
            s_ref[x] += low[0][R * x : R * x + R, :]
        for x in (5, 6):
            s_ref[x] += high[0][R * (x - 5) : R * (x - 5) + R, :]

    by_parity("slab", receive)

    def split(x, carry):
        for k in range(3):
            v = v1_ref[k, x]
            fixed = v > 0.5 * held
            v0_ref[k, x] = jnp.where(fixed, 0.0, v)
            m_ref[k, x] = jnp.where(fixed, 0.0, 1.0)
        return carry

    lax.fori_loop(0, 9, split, 0, unroll=True)

    row = iota((R, Z), 0) - 4
    first_y = jnp.where(is_edge("cross", False), 0, -4)
    last_y = jnp.where(is_edge("cross", True), H - 1, R)
    outside_y = (row < first_y) | (row > last_y)
    for x in range(8):
        logit = s_ref[x]
        gone = (logit < 0.1 * dead) | outside_y
        if x < 2:
            gone = gone | is_edge("slab", False)
        if x > 5:
            gone = gone | is_edge("slab", True)
        density = 1.0 / (1.0 + jnp.exp(-logit))
        cube = density * density * density
        s_ref[x] = jnp.where(gone, 0.0, void_modulus + cube * (1.0 - void_modulus))
        if 1 <= x <= 6:
            factor = (-3.0 * (1.0 - void_modulus)) * cube * (1.0 - density)
            gain_ref[x - 1] = jnp.where(gone, 0.0, factor)

    below[...] = jnp.zeros_like(below)
    stage_b(v0_ref, s_ref, g_ref, below, 0, 7)
    stage_c(g_ref, v0_ref, m_ref, v1_ref, 0, 1, 7)
    stage_b(v1_ref, s_ref, g_ref, below, 1, 6)
    stage_c(g_ref, v1_ref, m_ref, v2_ref, 0, 2, 6)

    def send(even):
        pone_ref[...] = v2_ref[:, 5 if even else 3]
        ptwo_ref[...] = v2_ref[:, 3 if even else 5]

    by_parity("slab", send)
    acc_ref[...] = jnp.zeros_like(acc_ref)

    def sums(tile):
        rows, lanes = tile[0], pl.ds(128 * tile[1], 128)
        row = iota((8, 128), 0) + rows.start
        own = (row >= 4) & (row < 4 + H)
        total = [jnp.zeros((8, 128), f32) for _ in range(6)]
        for x in range(2, 6):
            for k in range(3):
                v0 = v0_ref[k, x, rows, lanes]
                v1 = v1_ref[k, x, rows, lanes]
                v2 = v2_ref[k, x, rows, lanes]
                pairs = ((v0, v0), (v0, v1), (v1, v1), (v1, v2), (v2, v2))
                for i, (left, right) in enumerate(pairs):
                    total[i] = total[i] + left * right
        low = section_sums(v2_ref, 2, tile)
        for x in range(2, 6):
            high = section_sums(v2_ref, x + 1, tile)
            total[5] = total[5] + s_ref[x, rows, lanes] * energy_of(along_x(low, high))
            low = high
        total[5] = total[5] + spring * total[4]
        for i in range(6):
            acc_ref[i] += jnp.where(own, total[i], 0.0)

    tiles(sums, below)
    lane = iota((1, 128), 1)
    dots = jnp.zeros((1, 128), f32)
    for i in range(6):
        total = jnp.sum(jnp.sum(acc_ref[i], axis=0, keepdims=True), axis=1, keepdims=True)
        dots = jnp.where(lane == i, total, dots)
    dots_ref[...] = jnp.broadcast_to(dots, dots_ref.shape)


def coefficients(dots_ref):
    dots = jnp.sum(dots_ref[...], axis=0, keepdims=True)
    total = [jnp.broadcast_to(dots[:, i : i + 1], (8, 128)) for i in range(6)]
    d00, d01, d11, d12, d22, g22 = total
    d02 = d11
    g00 = d01 + shift * d00
    g01 = d02 + shift * d01
    g02 = d12 + shift * d02
    g11 = d12 + shift * d11
    g12 = d22 + shift * d12
    tiny = 4e-6

    def inverse(pivot, scale):
        fine = pivot > tiny * scale
        return jnp.where(fine, 1.0 / jnp.where(fine, pivot, 1.0), 0.0)

    i0 = 1.0 / g00
    l1, l2 = g01 * i0, g02 * i0
    i1 = inverse(g11 - l1 * g01, g11)
    m = g12 - l2 * g01
    l3 = m * i1
    i2 = inverse(g22 - l2 * g02 - l3 * m, g22)
    b0 = d00
    b1 = d01 - l1 * b0
    b2 = d02 - l2 * b0 - l3 * b1
    c2 = b2 * i2
    c1 = b1 * i1 - l3 * c2
    c0 = b0 * i0 - l1 * c1 - l2 * c2
    return [jnp.tile(c, (TILES, Z // 128)) for c in (c0, c1, c2)]


def adjoint_kernel(
    p0_ref, p1_ref, p2_ref, pone_ref, ptwo_ref, gain_ref, dots_ref, f_ref,
    disp_ref, shifted_ref, wpart_ref,
    u_ref, lg_ref, s32_ref, below,
):
    c0, c1, c2 = coefficients(dots_ref)

    def combine(x, third):
        for k in range(3):
            u_ref[k, x] = c0 * p0_ref[k, x + 1] + c1 * p1_ref[k, x + 1] + c2 * third(k)

    def inner(x, carry):
        combine(x, lambda k: p2_ref[k, x + 1])
        return carry

    def receive(even):
        combine(0, lambda k: (ptwo_ref if even else pone_ref)[k])
        combine(6, lambda k: (pone_ref if even else ptwo_ref)[k])

    lax.fori_loop(1, 6, inner, 0, unroll=True)
    by_parity("slab", receive)
    for k in range(3):
        for x in range(D):
            disp_ref[k, x] = u_ref[k, x + 1, 4 : 4 + H, :]

    def energies(tile):
        rows, lanes = tile[0], pl.ds(128 * tile[1], 128)
        low = section_sums(u_ref, 0, tile)
        for x in range(6):
            high = section_sums(u_ref, x + 1, tile)
            grad = gain_ref[x, rows, lanes] * energy_of(along_x(low, high))
            lg_ref[1, x, rows, lanes] = grad.astype(bf16).astype(f32)
            low = high

    below[...] = jnp.zeros_like(below)
    tiles(energies, below)
    lane = iota((R, Z), 1)
    row = iota((R, Z), 0) - 4
    reach = (row >= -1) & (row <= H)
    for x in range(6):
        grad = jnp.where(reach, lg_ref[1, x], 0.0)
        lg_ref[1, x] = grad
        lg_ref[0, x] = jnp.where(lane < Z - 1, pltpu.roll(grad, Z - 1, 1), 0.0)
        lg_ref[2, x] = jnp.where(lane > 0, pltpu.roll(grad, 1, 1), 0.0)
    cross = jnp.zeros((NT, KT), f32)
    for x in range(D):
        for ox in range(3):
            for oz in range(3):
                q = 3 * ox + oz
                s32_ref[q * R : (q + 1) * R, :] = lg_ref[oz, x - (ox - 1) + 1]
        rows = s32_ref[...].astype(bf16)
        shifted_ref[x] = rows
        cross = cross + lax.dot_general(
            rows,
            f_ref[:, x].reshape(KT, Z),
            (((1,), (1,)), ((), ())),
            preferred_element_type=f32,
        )
    away = iota((R, KT), 1) % H - (iota((R, KT), 0) - 4)
    wide = [None] * 27
    for ox in range(3):
        for oz in range(3):
            q = 3 * ox + oz
            block = cross[q * R : (q + 1) * R, :]
            for oy in range(3):
                picked = jnp.where(away == oy - 1, block, 0.0)
                wide[9 * ox + 3 * oy + oz] = jnp.sum(picked, axis=0, keepdims=True)
    for t in range(27):
        s32_ref[t : t + 1, :] = wide[t][:, :Z]
        s32_ref[32 + t : 33 + t, :] = wide[t][:, Z:]
    s32_ref[27:32, :] = jnp.zeros((5, Z), f32)
    s32_ref[59:64, :] = jnp.zeros((5, Z), f32)
    value = s32_ref[0:64, :]
    terms = []
    for _ in range(3):
        terms.append(value.astype(bf16))
        value = value - terms[-1].astype(f32)
    terms = jnp.concatenate(terms, axis=0)
    gather = (iota((Z, 128), 0) // H == iota((Z, 128), 1)).astype(f32).astype(bf16)
    summed = jnp.dot(terms, gather, preferred_element_type=f32)
    summed = summed[0:64] + summed[64:128] + summed[128:192]
    narrow = summed[0:32, :] + pltpu.roll(summed[32:64, :], 8, 1)
    packed = narrow[0:4, :]
    for g in range(1, 8):
        packed = packed + pltpu.roll(narrow[4 * g : 4 * g + 4, :], C * g, 1)
    twice = jnp.concatenate([packed, packed], axis=0)
    wpart_ref[...] = jnp.broadcast_to(twice[None], wpart_ref.shape)


def finish_kernel(parts_ref, out_ref):
    total = jnp.sum(parts_ref[...].reshape(parts_ref.shape[0] // 8, 8, 128), axis=0)
    total = total[0:4, :] + total[4:8, :]
    count = lax.axis_size("slab") * D * lax.axis_size("cross") * H * Z
    taps = [total[:, 0:C]]
    for g in range(1, 8):
        taps.append(pltpu.roll(total, 128 - C * g, 1)[:, 0:C])
    turned = jnp.concatenate(taps, axis=0).T
    out_ref[...] = turned[:, 0:27] * (1.0 / math.sqrt(count))


def feature_kernel(table_ref, shifted_ref, out_ref):
    turned = table_ref[...].astype(f32).T.astype(bf16)
    for x in range(D):
        product = jnp.dot(turned, shifted_ref[x], preferred_element_type=f32)
        out_ref[:, x] = product.astype(bf16).reshape(C, H, Z)


def share(x):
    return lax.all_to_all(x, ("slab", "cross"), 0, 0)


def on_device(load, fixed_dofs, features, conv_weight, active_bricks):
    def swap(x, axis, start):
        pairs = [(i, i + 1) for i in range(start, lax.axis_size(axis) - 1, 2)]
        return lax.ppermute(x, axis, pairs + [(j, i) for i, j in pairs])

    def exchange(first, second, axis):
        return swap(first, axis, 0), swap(second, axis, 1)

    devices = lax.axis_size(("slab", "cross"))
    ids = active_bricks.reshape(1, 256)
    rows = shape_of(12 + D + 2, 4, Z)
    logits = shape_of(D + 2, R, Z)
    part = shape_of(3, 3, H, Z)
    q, qone, qtwo, logit, yone, ytwo, table = call(
        conv_kernel,
        [shape_of(3, D, H, Z), part, part, logits, rows, rows, shape_of(NT, KT, dtype=bf16)],
        [
            pltpu.VMEM((NT, KT), f32),
            pltpu.VMEM((3, D + 2, R, Z), f32),
        ],
        ids, conv_weight.T, features, load, fixed_dofs,
        outside=5,
    )
    yone, ytwo = exchange(yone, ytwo, "cross")
    qone, qtwo = exchange(qone, qtwo, "slab")
    wide = shape_of(3 * R + 72, Z)
    logit, ylo, yhi, xone, xtwo = call(
        pack_kernel, [logits, rows, rows, wide, wide], [], logit, yone, ytwo
    )
    xone, xtwo = exchange(xone, xtwo, "slab")
    field = shape_of(3, 9, R, Z)
    plane = shape_of(3, R, Z)
    p0, p1, p2, pone, ptwo, gain, dots = call(
        krylov_kernel,
        [field, field, field, plane, plane, logits, shape_of(devices, 128)],
        [
            pltpu.VMEM((3, 9, R, Z), f32),
            pltpu.VMEM((8, R, Z), f32),
            pltpu.VMEM((12, 9, R, Z), f32),
            pltpu.VMEM((6, 8, 128), f32),
            pltpu.VMEM((2, 9, 6, 8, 128), f32),
        ],
        qone, q, qtwo, logit, xone, xtwo, ylo, yhi,
    )
    dots = share(dots.reshape(devices, 1, 128)).reshape(devices, 128)
    pone, ptwo = exchange(pone, ptwo, "slab")
    displacement, shifted, wpart = call(
        adjoint_kernel,
        [shape_of(3, D, H, Z), shape_of(D, NT, Z, dtype=bf16), shape_of(devices // 2, 8, 128)],
        [
            pltpu.VMEM((3, 7, R, Z), f32),
            pltpu.VMEM((3, 6, R, Z), f32),
            pltpu.VMEM((NT, Z), f32),
            pltpu.VMEM((2, 7, 6, 8, 128), f32),
        ],
        p0, p1, p2, pone, ptwo, gain, dots, features,
    )
    parts = share(wpart.reshape(devices, 4, 128)).reshape(4 * devices, 128)
    (feature_grad,) = call(
        feature_kernel, [jax.ShapeDtypeStruct((C, D, H, Z), bf16)], [], table, shifted
    )
    (weight_grad,) = call(finish_kernel, [jax.ShapeDtypeStruct((C, 27), f32)], [], parts)
    return displacement, feature_grad, weight_grad.T


def sharded(mesh):
    in_specs = (
        P(None, "slab", "cross", None),
        P(None, "slab", "cross", None),
        P(None, "slab", "cross", None),
        P(),
        P("slab", "cross", None),
    )
    out_specs = (P(None, "slab", "cross", None), P(None, "slab", "cross", None), P())

    return jax.shard_map(
        on_device, mesh=mesh, in_specs=in_specs, out_specs=out_specs, check_vma=False
    )


def solution(mesh):
    return sharded(mesh)
```
